32 devices in a mesh: blk: 8 (over z, x), tile: 4 (over y, core).
Axes of the slice: x: 2, y: 2, z: 4, core: 2. Of those that a mesh axis runs over, the one named last changes fastest.
Arguments:
- blocks: float32 [96, 384, 1024], P('blk', None, 'tile')
- orders: int32 [96], replicated, may hold values from 96 to 384, as said below
- pattern: int32 [96, 8], replicated, may hold values 0 or 1
- dest: int32 [96], replicated, may hold values from 0 to 7, as said below
- inv_factor: float32 [96, 384, 384], P('blk'), as said below
Outputs:
- gram_matrix: float32 [1024, 1024], P('blk', 'tile')
The draws below stay inside these ranges and needn't reach their ends.
Inputs may be any that keep to these rules, and one draw needn't show every extreme that they name: `dest`: each owner owns exactly 12 blocks; of the 12 blocks numbered s * 12 to (s + 1) * 12 - 1, each owner owns 0 or exactly 2, and the owners are s + k modulo the number of owners for the same set of 6 offsets k at every s. `orders`: some block has order 384. `inv_factor`: each matrix is lower triangular with its diagonal from 1 to 2.
All inputs are finite; a program needn't handle non-finite values.
Results may differ from the reference program's by a relative error of at most 0.0003.
Values sent between devices are 32-bit elements; how exact they have to be, the bound alone decides.
No kernel may reach another device: no remote copies, remote signals or barrier semaphores. Data moves between devices by JAX's collectives and lax.ppermute only.
A program may use at most 128 MiB of HBM per device.

```python
import jax
import jax.numpy as jnp
from jax import lax

P_SIZE = 1024
MAXORD = 384
CTW = 128
SLOTS = 12
CAP = 2
NBLOCKS = 96
NCT = 8
N_BLK = 8


def draw_blocks(key, part):
    first = jax.random.fold_in(jax.random.fold_in(key, 11), 0)
    return jax.random.normal(first, (NBLOCKS, MAXORD, P_SIZE), jnp.float32)


def draw_orders(key, part):
    first, second = jax.random.split(jax.random.fold_in(key, 23))
    values = jax.random.randint(first, (NBLOCKS,), MAXORD // 4, MAXORD + 1).astype(jnp.int32)
    spot = jax.random.randint(second, (), 0, NBLOCKS)
    return values.at[spot].set(MAXORD).astype(jnp.int32)


def draw_dest(key, part):
    first, second = jax.random.split(jax.random.fold_in(key, 37))
    shuffled = jax.random.permutation(first, N_BLK).astype(jnp.int32)
    places = jnp.arange(N_BLK, dtype=jnp.int32)
    scores = jnp.where(shuffled == 1, 0, jnp.where(shuffled == N_BLK // 2, 1, places + 2)).astype(jnp.int32)
    chosen = jnp.argsort(scores).astype(jnp.int32)
    residues = shuffled[chosen][:SLOTS // CAP]
    offsets = jnp.repeat(residues, CAP)
    arrange = jax.vmap(lambda sub: jax.random.permutation(sub, SLOTS))(jax.random.split(second, N_BLK))
    shifted = offsets[arrange]
    sources = jnp.arange(N_BLK, dtype=jnp.int32)[:, None]
    return ((sources + shifted) % N_BLK).reshape(NBLOCKS).astype(jnp.int32)


def draw_inv_factor(key, part):
    first, second = jax.random.split(jax.random.fold_in(key, 41))
    below = jax.random.normal(first, (NBLOCKS, MAXORD, MAXORD), jnp.float32) * (0.8 / MAXORD ** 0.5)
    diagonal = jax.random.uniform(second, (NBLOCKS, MAXORD, 1), jnp.float32, 1.0, 2.0)
    row_ids = lax.broadcasted_iota(jnp.int32, (MAXORD, MAXORD), 0)
    col_ids = lax.broadcasted_iota(jnp.int32, (MAXORD, MAXORD), 1)
    return jnp.where(row_ids > col_ids, below, 0.0) + jnp.where(row_ids == col_ids, diagonal, 0.0)


def place_ends(drawn, own_key, least, top_value):
    dims = drawn.shape
    index_at = [jax.random.randint(jax.random.fold_in(own_key, axis), (), 0, dims[axis]) for axis in range(len(dims))]
    drawn = drawn.at[tuple(index_at)].set(least)
    longest = dims.index(max(dims))
    index_at[longest] = (index_at[longest] + 1) % dims[longest]
    return drawn.at[tuple(index_at)].set(top_value)


def setup_inputs(seed: int = 0) -> dict:
    seeds = jax.random.split(jax.random.key(seed), 6)
    return {
        "blocks": draw_blocks(jax.random.fold_in(seeds[5], 71), 0),
        "orders": draw_orders(jax.random.fold_in(seeds[5], 71), 0),
        "pattern": place_ends((jax.random.randint(seeds[2], (NBLOCKS, NCT), 0, 5) < 3).astype(jnp.int32), jax.random.fold_in(seeds[2], 1), 0, 1),
        "dest": draw_dest(jax.random.fold_in(seeds[5], 71), 0),
        "inv_factor": draw_inv_factor(jax.random.fold_in(seeds[5], 71), 0),
    }


def reference(blocks, orders, pattern, dest, inv_factor):
    owned = jnp.argsort(dest, stable=True).astype(jnp.int32)
    row_ids = jnp.arange(MAXORD, dtype=jnp.int32)
    factor = 1.0 / (NBLOCKS * MAXORD ** 0.5)

    def accumulate(carry, index):
        number = owned[index]
        row_mask = (row_ids < orders[number]).astype(jnp.float32)
        col_mask = jnp.repeat(pattern[number].astype(jnp.float32), CTW)
        masked = blocks[number] * row_mask[:, None] * col_mask[None, :]
        whitened = jnp.dot(inv_factor[index], masked, precision=lax.Precision.HIGHEST, preferred_element_type=jnp.float32)
        whitened = whitened * row_mask[:, None]
        update = lax.dot_general(whitened, whitened, (((0,), (0,)), ((), ())), precision=lax.Precision.HIGHEST, preferred_element_type=jnp.float32)
        return carry + update, None

    start = jnp.zeros((P_SIZE, P_SIZE), jnp.float32)
    summed, _ = lax.scan(accumulate, start, jnp.arange(NBLOCKS, dtype=jnp.int32))
    return summed * factor
```

```python
import functools

import jax
import jax.numpy as jnp
from jax import lax
from jax.experimental import pallas as pl
from jax.experimental.pallas import tpu as pltpu
from jax.sharding import PartitionSpec as P

CTW = 128
F32 = jnp.float32
BF16 = jnp.bfloat16
XY_FIRST = 88


def general_body(blocks, orders, pattern, dest, inv_factor):
    source_index = lax.axis_index("blk")
    owner_count = lax.axis_size("blk")
    tile_index = lax.axis_index("tile")
    slot_count, max_order, column_width = blocks.shape
    block_count = dest.shape[0]
    tiles_here = column_width // CTW
    highest = lax.Precision.HIGHEST
    capacity = (slot_count + owner_count - 1) // owner_count
    dest_grid = dest.reshape(owner_count, slot_count)
    earlier = lax.broadcasted_iota(jnp.int32, (slot_count, slot_count), 1) < lax.broadcasted_iota(
        jnp.int32, (slot_count, slot_count), 0
    )
    matching = dest_grid[:, :, None] == dest_grid[:, None, :]
    ranks = jnp.sum((matching & earlier[None]).astype(jnp.int32), axis=2).reshape(block_count)
    my_dest = lax.dynamic_slice_in_dim(dest, source_index * slot_count, slot_count)
    my_rank = lax.dynamic_slice_in_dim(ranks, source_index * slot_count, slot_count)
    my_orders = lax.dynamic_slice_in_dim(orders, source_index * slot_count, slot_count)
    my_tiles = lax.dynamic_slice(
        pattern, (source_index * slot_count, tile_index * tiles_here), (slot_count, tiles_here)
    )
    row_ids = lax.broadcasted_iota(jnp.int32, (slot_count, max_order), 1)
    row_mask = (row_ids < my_orders[:, None]).astype(F32)
    col_mask = jnp.repeat(my_tiles.astype(F32), CTW, axis=1)
    masked = blocks * row_mask[:, :, None] * col_mask[:, None, :]
    owned = lax.dynamic_slice_in_dim(
        jnp.argsort(dest, stable=True), source_index * slot_count, slot_count
    )
    slot_ids = my_dest * capacity + my_rank
    placing = (
        lax.broadcasted_iota(jnp.int32, (owner_count * capacity, slot_count), 0)
        == slot_ids[None, :]
    ).astype(F32)
    outgoing = jnp.einsum("ak,krc->arc", placing, masked, precision=highest, preferred_element_type=F32)
    arrived = lax.all_to_all(outgoing, "blk", split_axis=0, concat_axis=0, tiled=True)
    positions = owned // slot_count * capacity + ranks[owned]
    own_blocks = jnp.take(arrived, positions, axis=0)
    own_mask = (row_ids < orders[owned][:, None]).astype(F32)
    whitened = jnp.einsum(
        "jrq,jqc->jrc", inv_factor, own_blocks, precision=highest, preferred_element_type=F32
    )
    whitened_rows = (whitened * own_mask[:, :, None]).reshape(slot_count * max_order, column_width)
    factor = 1.0 / (block_count * max_order**0.5)
    partial_sums = lax.dot_general(
        lax.all_gather(whitened_rows, "tile", axis=1, tiled=True),
        whitened_rows,
        (((0,), (0,)), ((), ())),
        precision=highest,
        preferred_element_type=F32,
    )
    gram_tile = lax.psum_scatter(partial_sums, "blk", scatter_dimension=0, tiled=True)
    return gram_tile * factor


def pack_kernel(
    dest_ref, blocks_ref, inv_ref, y_send, core_send, factor_send, table_ref, factor_at, block_at, count, sem, factor_sem
):
    s = lax.axis_index("blk")
    t = lax.axis_index("tile")
    y, c = t // 2, t % 2
    n_blk = factor_at.shape[0]
    slots = blocks_ref.shape[0]

    def scan_source(source, found):
        def scan_block(i, carry):
            found, seen = carry
            mine = dest_ref[source * slots + i] == s

            @pl.when(mine & (seen == y))
            def _():
                factor_at[source] = found

            step = jnp.where(mine, 1, 0)
            return found + step, seen + step

        factor_at[source] = 0
        return lax.fori_loop(0, slots, scan_block, (found, 0), unroll=True)[0]

    lax.fori_loop(0, n_blk, scan_source, 0)

    def factor_copies(source):
        row = factor_at[source]
        for k, (ti, tj) in enumerate(((0, 0), (1, 0), (1, 1))):
            ri, rj = jnp.where(c == 0, ti, 2), jnp.where(c == 0, tj, k)
            yield pltpu.make_async_copy(
                inv_ref.at[row, pl.ds(pl.multiple_of(ri * 128, 128), 128), pl.ds(pl.multiple_of(rj * 128, 128), 128)],
                factor_send.at[source, pl.ds(k * 128, 128), :],
                factor_sem,
            )

    for source in range(n_blk):
        for copy in factor_copies(source):
            copy.start()

    def clear(o, carry):
        count[o] = 0
        return carry

    lax.fori_loop(0, n_blk, clear, 0, unroll=True)

    def place(i, carry):
        o = dest_ref[s * slots + i]
        r = count[o]
        block_at[r, o] = i
        count[o] = r + 1
        return carry

    lax.fori_loop(0, slots, place, 0, unroll=True)

    def compact(o, p):
        @pl.when(count[o] > 0)
        def _():
            table_ref[0, p] = block_at[y, o]
            table_ref[1, p] = block_at[1 - y, o]
            table_ref[2, p] = o

        return p + jnp.where(count[o] > 0, 1, 0)

    lax.fori_loop(0, n_blk, compact, 0, unroll=True)

    half = slots // 4

    def block_copies():
        for p in range(2 * half):
            yield pltpu.make_async_copy(blocks_ref.at[table_ref[1, p]], y_send.at[p], sem)
        for p in range(half):
            yield pltpu.make_async_copy(
                blocks_ref.at[table_ref[0, (1 - c) * half + p]], core_send.at[p], sem
            )

    for copy in block_copies():
        copy.start()
    for copy in block_copies():
        copy.wait()
    for source in range(n_blk):
        for copy in factor_copies(source):
            copy.wait()


def split(x):
    high = x.astype(BF16)
    return high, (x - high.astype(F32)).astype(BF16)


def dot3(a, b, dims):
    def dot(p, q):
        return lax.dot_general(p, q, (dims, ((), ())), preferred_element_type=F32)

    return dot(a[0], b[0]) + (dot(a[0], b[1]) + dot(a[1], b[0]))


def gram_kernel(
    table_ref,
    orders_ref,
    pattern_ref,
    blocks_ref,
    core_recv,
    y_recv,
    yc_recv,
    factor_ref,
    factor_other,
    send_out,
    keep_out,
    xs,
    fs,
    w_high,
    w_low,
    wt_high,
    wt_low,
    gram,
    sems,
    out_sem,
):
    s = lax.axis_index("blk")
    t = lax.axis_index("tile")
    c = t % 2
    slots, max_order, width = blocks_ref.shape
    half = slots // 4
    base = c * half

    def loads(p):
        at = base + p
        owner = table_ref[2, at]
        for m, src in enumerate(
            (blocks_ref.at[table_ref[0, at]], core_recv.at[p], y_recv.at[at], yc_recv.at[p])
        ):
            q = t ^ m
            yield pltpu.make_async_copy(
                src, xs.at[p, :, pl.ds(pl.multiple_of(q * width, width), width)], sems.at[p]
            )
        for which, src in ((c, factor_ref), (1 - c, factor_other)):
            yield pltpu.make_async_copy(src.at[owner], fs.at[p, which], sems.at[p])

    for p in range(half):
        for copy in loads(p):
            copy.start()

    row_ids = lax.broadcasted_iota(jnp.int32, (max_order, CTW), 0)
    for p in range(half):
        for copy in loads(p):
            copy.wait()
        number = s * slots + table_ref[0, base + p]
        order = orders_ref[number]
        row_on = row_ids < order
        top, low = fs[p, 0], fs[p, 1]
        f00, f10, f11 = top[:128], top[128:256], top[256:]
        f2 = jnp.concatenate([low[:128], low[128:256], low[256:]], axis=1)
        f1 = jnp.concatenate([jnp.concatenate([f00, jnp.zeros_like(f00)], axis=1), jnp.concatenate([f10, f11], axis=1)], axis=0)
        f1s, f2s = split(f1), split(f2)
        for q in range(4):
            parts = []
            for e in range(width // CTW):
                ct = q * (width // CTW) + e
                on = row_on & (pattern_ref[number * 8 + ct] != 0)
                parts.append(jnp.where(on, xs[p, :, ct * CTW : (ct + 1) * CTW], 0.0))
            x = split(jnp.concatenate(parts, axis=1))
            w = jnp.concatenate(
                [
                    dot3(f1s, (x[0][:256], x[1][:256]), ((1,), (0,))),
                    dot3(f2s, x, ((1,), (0,))),
                ],
                axis=0,
            )
            w = jnp.where(jnp.concatenate([row_on, row_on], axis=1), w, 0.0)
            rows, cols = pl.ds(p * max_order, max_order), pl.ds(q * width, width)
            w_high[rows, cols], w_low[rows, cols] = split(w)
            wt_high[cols, rows], wt_low[cols, rows] = split(w.T)

    for q1 in range(4):
        rows = pl.ds(q1 * width, width)
        lhs = wt_high[rows, :], wt_low[rows, :]
        for q2 in range(q1 + 1):
            cols = pl.ds(q2 * width, width)
            g = dot3(lhs, (w_high[:, cols], w_low[:, cols]), ((1,), (0,)))
            gram[q1, q2] = g
            if q1 != q2:
                gram[q2, q1] = g.T

    z, x = s // 2, s % 2

    def stores():
        for m in range(4):
            out = send_out if m % 2 else keep_out
            for n in range(4):
                for a in range(2):
                    yield pltpu.make_async_copy(
                        gram.at[z ^ n, t ^ m, pl.ds(pl.multiple_of((x ^ a) * 128, 128), 128), :],
                        out.at[n, a, m // 2],
                        out_sem,
                    )

    for copy in stores():
        copy.start()
    for copy in stores():
        copy.wait()


def paired_body(blocks, orders, pattern, dest, inv_factor):
    slots, max_order, width = blocks.shape
    n_blk = lax.axis_size("blk")
    n_tile = lax.axis_size("tile")
    half = slots // 4
    block_count = dest.shape[0]
    axes = ("blk", "tile")

    def exchange(value, blk_bits, tile_bits):
        perm = [
            (b * n_tile + t, (b ^ blk_bits) * n_tile + (t ^ tile_bits)) for b in range(n_blk) for t in range(n_tile)
        ]
        return lax.ppermute(value, axes, perm)

    hbm = pl.BlockSpec(memory_space=pl.ANY)
    smem = pl.BlockSpec(memory_space=pltpu.SMEM)
    shape = jax.ShapeDtypeStruct
    y_send, core_send, factor_send, table = pl.pallas_call(
        pack_kernel,
        out_shape=(
            shape((2 * half, max_order, width), F32),
            shape((half, max_order, width), F32),
            shape((n_blk, max_order, CTW), F32),
            shape((3, 8), jnp.int32),
        ),
        in_specs=[smem, hbm, hbm],
        out_specs=(hbm, hbm, hbm, smem),
        scratch_shapes=[
            pltpu.SMEM((n_blk,), jnp.int32),
            pltpu.SMEM((2, n_blk), jnp.int32),
            pltpu.SMEM((n_blk,), jnp.int32),
            pltpu.SemaphoreType.DMA,
            pltpu.SemaphoreType.DMA,
        ],
        name="pack",
    )(dest, blocks, inv_factor)

    factors = lax.all_to_all(factor_send, "blk", split_axis=0, concat_axis=0, tiled=True)
    y_recv = exchange(y_send, 0, 2)
    core_recv = exchange(core_send, 0, 1)
    factors_other = exchange(factors, 0, 1)
    core = lax.axis_index("tile") % 2
    yc_recv = exchange(lax.dynamic_slice_in_dim(y_recv, (1 - core) * half, half), 0, 1)

    pieces = (4, 2, 2, 128, width)
    send, keep = pl.pallas_call(
        gram_kernel,
        out_shape=(shape(pieces, F32), shape(pieces, F32)),
        in_specs=[smem, smem, smem] + [hbm] * 6,
        out_specs=(hbm, hbm),
        scratch_shapes=[
            pltpu.VMEM((half, max_order, 4 * width), F32),
            pltpu.VMEM((half, 2, max_order, CTW), F32),
            pltpu.VMEM((half * max_order, 4 * width), BF16),
            pltpu.VMEM((half * max_order, 4 * width), BF16),
            pltpu.VMEM((4 * width, half * max_order), BF16),
            pltpu.VMEM((4 * width, half * max_order), BF16),
            pltpu.VMEM((4, 4, width, width), F32),
            pltpu.SemaphoreType.DMA((half,)),
            pltpu.SemaphoreType.DMA,
        ],
        compiler_params=pltpu.CompilerParams(vmem_limit_bytes=48 << 20),
        name="gram",
    )(table, orders, pattern.reshape(-1), blocks, core_recv, y_recv, yc_recv, factors, factors_other)

    total = keep + exchange(send, 0, 1)
    first, second = total[..., :XY_FIRST, :], total[..., XY_FIRST:, :]
    plane = [(a, b) for a in range(2) for b in range(2) if a or b]
    plane_in = [exchange(first[:, a, b], a, 2 * b) for a, b in plane]
    line_in = [exchange(second[n], 2 * n, 0) for n in range(1, 4)]
    first = first[:, 0, 0] + sum(plane_in)
    second = second[0] + sum(line_in)
    line_in = [exchange(first[n], 2 * n, 0) for n in range(1, 4)]
    plane_in = [exchange(second[a, b], a, 2 * b) for a, b in plane]
    gram_tile = jnp.concatenate([first[0] + sum(line_in), second[0, 0] + sum(plane_in)], axis=0)
    return gram_tile * (1.0 / (block_count * max_order**0.5))


def solution(mesh):
    in_specs = (P("blk", None, "tile"), P(), P(), P(), P("blk", None, None))
    out_specs = P("blk", "tile")
    paired = mesh.shape["blk"] == 8 and mesh.shape["tile"] == 4
    body = paired_body if paired else general_body
    return jax.shard_map(body, mesh=mesh, in_specs=in_specs, out_specs=out_specs, check_vma=False)
```

```python
import jax
import jax.numpy as jnp
from jax import lax
from jax.experimental import pallas as pl
from jax.experimental.pallas import tpu as pltpu
from jax.sharding import PartitionSpec as P

CTW = 128
F32 = jnp.float32
BF16 = jnp.bfloat16
XY_FIRST = 88


def general_body(blocks, orders, pattern, dest, inv_factor):
    source_index = lax.axis_index("blk")
    owner_count = lax.axis_size("blk")
    tile_index = lax.axis_index("tile")
    slot_count, max_order, column_width = blocks.shape
    block_count = dest.shape[0]
    tiles_here = column_width // CTW
    highest = lax.Precision.HIGHEST
    capacity = (slot_count + owner_count - 1) // owner_count
    dest_grid = dest.reshape(owner_count, slot_count)
    earlier = lax.broadcasted_iota(jnp.int32, (slot_count, slot_count), 1) < lax.broadcasted_iota(
        jnp.int32, (slot_count, slot_count), 0
    )
    matching = dest_grid[:, :, None] == dest_grid[:, None, :]
    ranks = jnp.sum((matching & earlier[None]).astype(jnp.int32), axis=2).reshape(block_count)
    my_dest = lax.dynamic_slice_in_dim(dest, source_index * slot_count, slot_count)
    my_rank = lax.dynamic_slice_in_dim(ranks, source_index * slot_count, slot_count)
    my_orders = lax.dynamic_slice_in_dim(orders, source_index * slot_count, slot_count)
    my_tiles = lax.dynamic_slice(
        pattern, (source_index * slot_count, tile_index * tiles_here), (slot_count, tiles_here)
    )
    row_ids = lax.broadcasted_iota(jnp.int32, (slot_count, max_order), 1)
    row_mask = (row_ids < my_orders[:, None]).astype(F32)
    col_mask = jnp.repeat(my_tiles.astype(F32), CTW, axis=1)
    masked = blocks * row_mask[:, :, None] * col_mask[:, None, :]
    owned = lax.dynamic_slice_in_dim(
        jnp.argsort(dest, stable=True), source_index * slot_count, slot_count
    )
    slot_ids = my_dest * capacity + my_rank
    placing = (
        lax.broadcasted_iota(jnp.int32, (owner_count * capacity, slot_count), 0)
        == slot_ids[None, :]
    ).astype(F32)
    outgoing = jnp.einsum("ak,krc->arc", placing, masked, precision=highest, preferred_element_type=F32)
    arrived = lax.all_to_all(outgoing, "blk", split_axis=0, concat_axis=0, tiled=True)
    positions = owned // slot_count * capacity + ranks[owned]
    own_blocks = jnp.take(arrived, positions, axis=0)
    own_mask = (row_ids < orders[owned][:, None]).astype(F32)
    whitened = jnp.einsum(
        "jrq,jqc->jrc", inv_factor, own_blocks, precision=highest, preferred_element_type=F32
    )
    whitened_rows = (whitened * own_mask[:, :, None]).reshape(slot_count * max_order, column_width)
    factor = 1.0 / (block_count * max_order**0.5)
    partial_sums = lax.dot_general(
        lax.all_gather(whitened_rows, "tile", axis=1, tiled=True),
        whitened_rows,
        (((0,), (0,)), ((), ())),
        precision=highest,
        preferred_element_type=F32,
    )
    gram_tile = lax.psum_scatter(partial_sums, "blk", scatter_dimension=0, tiled=True)
    return gram_tile * factor


MINE, OTHERS, OWNER, ROW_AT = 0, 1, 2, 3


def round8(order):
    return (order + 7) // 8 * 8


def pack_rows(dest_ref, orders_ref, pattern_ref, blocks_ref, rows_out, table_ref, block_at, count, staged, packed, sems, out_sem):
    s = lax.axis_index("blk")
    t = lax.axis_index("tile")
    y = t // 2
    slots, max_order, width = blocks_ref.shape
    n_blk = count.shape[0]
    tiles = width // CTW

    def clear(o, carry):
        count[o] = 0
        return carry

    lax.fori_loop(0, n_blk, clear, 0, unroll=True)

    def place(i, carry):
        o = dest_ref[s * slots + i]
        r = count[o]
        block_at[r, o] = i
        count[o] = r + 1
        return carry

    lax.fori_loop(0, slots, place, 0, unroll=True)

    def compact(o, p):
        @pl.when(count[o] > 0)
        def _():
            table_ref[MINE, p] = block_at[y, o]
            table_ref[OTHERS, p] = block_at[1 - y, o]
            table_ref[OWNER, p] = o

        return p + jnp.where(count[o] > 0, 1, 0)

    lax.fori_loop(0, n_blk, compact, 0, unroll=True)

    def loads():
        for p in range(slots // 2):
            yield pltpu.make_async_copy(blocks_ref.at[table_ref[OTHERS, p]], staged.at[p], sems.at[p])

    for copy in loads():
        copy.start()

    for k in range(2):
        at = jnp.int32(0)
        for p in range(slots // 2):
            number = s * slots + table_ref[MINE, p]
            for e in range(tiles):
                table_ref[ROW_AT + k, p * tiles + e] = jnp.minimum(at, rows_out.shape[0] - max_order)
                on = pattern_ref[number * 8 + (t ^ (2 + k)) * tiles + e] != 0
                at = at + jnp.where(on, round8(orders_ref[number]), 0)

    at = jnp.int32(0)
    for p, copy in enumerate(loads()):
        copy.wait()
        number = s * slots + table_ref[OTHERS, p]
        for e in range(tiles):
            on = pattern_ref[number * 8 + t * tiles + e] != 0

            @pl.when(on)
            def _(at=at, p=p, e=e):
                packed[pl.ds(pl.multiple_of(at, 8), max_order), :] = staged[p, :, e * CTW : (e + 1) * CTW]

            at = at + jnp.where(on, round8(orders_ref[number]), 0)
    out = pltpu.make_async_copy(packed.at[pl.ds(0, rows_out.shape[0])], rows_out, out_sem)
    out.start()
    out.wait()


def pack_own(table_ref, dest_ref, blocks_ref, inv_ref, own_out, factor_out, factor_at, own, factor, own_sems, factor_sems, out_sem):
    s = lax.axis_index("blk")
    t = lax.axis_index("tile")
    y, c = t // 2, t % 2
    slots = blocks_ref.shape[0]
    n_blk = factor_at.shape[0]

    def scan_source(source, found):
        def scan_block(i, carry):
            found, seen = carry
            mine = dest_ref[source * slots + i] == s

            @pl.when(mine & (seen == y))
            def _():
                factor_at[source] = found

            step = jnp.where(mine, 1, 0)
            return found + step, seen + step

        factor_at[source] = 0
        return lax.fori_loop(0, slots, scan_block, (found, 0), unroll=True)[0]

    lax.fori_loop(0, n_blk, scan_source, 0)

    def factor_loads(source):
        row = factor_at[source]
        for k, (ti, tj) in enumerate(((0, 0), (1, 0), (1, 1))):
            ri, rj = jnp.where(c == 0, ti, 2), jnp.where(c == 0, tj, k)
            yield pltpu.make_async_copy(
                inv_ref.at[row, pl.ds(pl.multiple_of(ri * 128, 128), 128), pl.ds(pl.multiple_of(rj * 128, 128), 128)],
                factor.at[source, pl.ds(k * 128, 128), :],
                factor_sems.at[source],
            )

    def own_load(p):
        return pltpu.make_async_copy(blocks_ref.at[table_ref[MINE, p]], own.at[p], own_sems.at[p])

    def outs():
        for source in range(n_blk):
            yield pltpu.make_async_copy(factor.at[source], factor_out.at[source], out_sem)
        for p in range(slots // 2):
            yield pltpu.make_async_copy(own.at[p], own_out.at[p], out_sem)

    for source in range(n_blk):
        for copy in factor_loads(source):
            copy.start()
    for p in range(slots // 2):
        own_load(p).start()
    for i, out in enumerate(outs()):
        if i < n_blk:
            for copy in factor_loads(i):
                copy.wait()
        else:
            own_load(i - n_blk).wait()
        out.start()
    for out in outs():
        out.wait()


def split(x):
    high = x.astype(BF16)
    return high, (x - high.astype(F32)).astype(BF16)


def dot3(a, b):
    def dot(p, q):
        return jnp.dot(p, q, preferred_element_type=F32)

    return dot(a[0], b[0]) + (dot(a[0], b[1]) + dot(a[1], b[0]))


def whiten(tiles, number, upper, lower, orders_ref, pattern_ref, tile_ids):
    row_on = lax.broadcasted_iota(jnp.int32, tiles[0].shape, 0) < orders_ref[number]
    parts = [
        jnp.where(row_on & (pattern_ref[number * 8 + ct] != 0), tile, 0.0) for tile, ct in zip(tiles, tile_ids)
    ]
    x = split(jnp.concatenate(parts, axis=1))
    w = jnp.concatenate([dot3(upper, (x[0][:256], x[1][:256])), dot3(lower, x)], axis=0)
    return [jnp.where(row_on, w[:, i * CTW : (i + 1) * CTW], 0.0) for i in range(len(tiles))]


def gram_own(
    table_ref, orders_ref, pattern_ref, own_ref, core_ref, factor_ref, factor_other,
    upper_high, upper_low, lower_high, lower_low, w0_high, w0_low, w1t_high, w1t_low, g_out,
    xs, fs, w0t_high, w0t_low, sems,
):
    s = lax.axis_index("blk")
    t = lax.axis_index("tile")
    c = t % 2
    half, max_order, width = own_ref.shape

    def loads(p):
        yield pltpu.make_async_copy(own_ref.at[p], xs.at[p, 0], sems.at[p])
        yield pltpu.make_async_copy(core_ref.at[p], xs.at[p, 1], sems.at[p])
        for which, src in ((c, factor_ref), (1 - c, factor_other)):
            yield pltpu.make_async_copy(src.at[table_ref[OWNER, p]], fs.at[p, which], sems.at[p])

    for p in range(half):
        for copy in loads(p):
            copy.start()
    for p in range(half):
        for copy in loads(p):
            copy.wait()
        top, low = fs[p, 0], fs[p, 1]
        f00, f10, f11 = top[:128], top[128:256], top[256:]
        upper = split(
            jnp.concatenate(
                [jnp.concatenate([f00, jnp.zeros_like(f00)], axis=1), jnp.concatenate([f10, f11], axis=1)], axis=0
            )
        )
        lower = split(jnp.concatenate([low[:128], low[128:256], low[256:]], axis=1))
        upper_high[p], upper_low[p] = upper
        lower_high[p], lower_low[p] = lower
        tiles = [xs[p, m, :, e * CTW : (e + 1) * CTW] for m in range(2) for e in range(2)]
        tile_ids = [(t ^ m) * 2 + e for m in range(2) for e in range(2)]
        number = s * 2 * half + table_ref[MINE, p]
        w = whiten(tiles, number, upper, lower, orders_ref, pattern_ref, tile_ids)
        rows = pl.ds(p * max_order, max_order)
        w0, w1 = jnp.concatenate(w[:2], axis=1), jnp.concatenate(w[2:], axis=1)
        w0_high[rows, :], w0_low[rows, :] = split(w0)
        w0t_high[:, rows], w0t_low[:, rows] = split(w0.T)
        w1t_high[:, rows], w1t_low[:, rows] = split(w1.T)
    w0 = w0_high[...], w0_low[...]
    g_out[0] = dot3((w0t_high[...], w0t_low[...]), w0)
    g_out[1] = dot3((w1t_high[...], w1t_low[...]), w0)


def gram_rest(
    table_ref, orders_ref, pattern_ref, y_ref, yc_ref,
    upper_high, upper_low, lower_high, lower_low, w0_high, w0_low, w1t_high, w1t_low, g_own,
    *refs,
):
    firsts, seconds = refs[:4], refs[4:8]
    xs, w2_high, w2_low, w2t_high, w2t_low, w3t_high, w3t_low, gram, sems, out_sem = refs[8:]
    s = lax.axis_index("blk")
    t = lax.axis_index("tile")
    half, tiles, max_order, _ = xs.shape
    width = w0_high.shape[1]

    def loads(p):
        for k, src in enumerate((y_ref, yc_ref)):
            for e in range(2):
                at = pl.multiple_of(table_ref[ROW_AT + k, p * 2 + e], 8)
                yield pltpu.make_async_copy(src.at[pl.ds(at, max_order), :], xs.at[p, k * 2 + e], sems.at[p])

    for p in range(half):
        for copy in loads(p):
            copy.start()
    for p in range(half):
        for copy in loads(p):
            copy.wait()
        tile_ids = [(t ^ (2 + k)) * 2 + e for k in range(2) for e in range(2)]
        number = s * 2 * half + table_ref[MINE, p]
        upper, lower = (upper_high[p], upper_low[p]), (lower_high[p], lower_low[p])
        w = whiten([xs[p, i] for i in range(tiles)], number, upper, lower, orders_ref, pattern_ref, tile_ids)
        rows = pl.ds(p * max_order, max_order)
        w2, w3 = jnp.concatenate(w[:2], axis=1), jnp.concatenate(w[2:], axis=1)
        w2_high[rows, :], w2_low[rows, :] = split(w2)
        w2t_high[:, rows], w2t_low[:, rows] = split(w2.T)
        w3t_high[:, rows], w3t_low[:, rows] = split(w3.T)

    w0, w2 = (w0_high[...], w0_low[...]), (w2_high[...], w2_low[...])
    w1t, w2t, w3t = (w1t_high[...], w1t_low[...]), (w2t_high[...], w2t_low[...]), (w3t_high[...], w3t_low[...])
    gram[0, 0] = g_own[0]
    gram[0, 1] = g_own[1]
    g20 = dot3(w2t, w0)
    gram[0, 2] = g20
    gram[1, 0] = g20.T
    gram[0, 3] = dot3(w3t, w0)
    gram[1, 1] = dot3(w1t, w2)
    gram[1, 2] = dot3(w2t, w2)
    gram[1, 3] = dot3(w3t, w2)

    z, x = s // 2, s % 2

    def stores():
        for n in range(4):
            for a in range(2):
                for b in range(2):
                    m, at = (z ^ n) ^ t, (x ^ a) * 128
                    first, second = firsts[2 * a + b], seconds[n]
                    yield pltpu.make_async_copy(
                        gram.at[b, m, pl.ds(pl.multiple_of(at, 8), XY_FIRST), :], first.at[n], out_sem
                    )
                    yield pltpu.make_async_copy(
                        gram.at[b, m, pl.ds(pl.multiple_of(at + XY_FIRST, 8), 128 - XY_FIRST), :],
                        second.at[a, b],
                        out_sem,
                    )

    for copy in stores():
        copy.start()
    for copy in stores():
        copy.wait()


def paired_body(blocks, orders, pattern, dest, inv_factor):
    slots, max_order, width = blocks.shape
    n_blk = lax.axis_size("blk")
    n_tile = lax.axis_size("tile")
    half = slots // 2
    tiles = width // CTW
    block_count = dest.shape[0]
    axes = ("blk", "tile")
    pattern = pattern.reshape(-1)

    def exchange(value, blk_bits, tile_bits):
        perm = [
            (b * n_tile + t, (b ^ blk_bits) * n_tile + (t ^ tile_bits)) for b in range(n_blk) for t in range(n_tile)
        ]
        return lax.ppermute(value, axes, perm)

    hbm = pl.BlockSpec(memory_space=pltpu.HBM)
    smem = pl.BlockSpec(memory_space=pltpu.SMEM)
    vmem = pl.BlockSpec(memory_space=pltpu.VMEM)
    shape = jax.ShapeDtypeStruct
    params = pltpu.CompilerParams(vmem_limit_bytes=48 << 20)
    dma = pltpu.SemaphoreType.DMA
    row_count = half * tiles * max_order

    y_rows, table = pl.pallas_call(
        pack_rows,
        out_shape=(pltpu.HBM((row_count, CTW), F32), shape((5, half * tiles), jnp.int32)),
        in_specs=[smem, smem, smem, hbm],
        out_specs=(hbm, smem),
        scratch_shapes=[
            pltpu.SMEM((2, n_blk), jnp.int32),
            pltpu.SMEM((n_blk,), jnp.int32),
            pltpu.VMEM((half, max_order, width), F32),
            pltpu.VMEM((row_count, CTW), F32),
            dma((half,)),
            dma,
        ],
        compiler_params=params,
        name="pack_rows",
    )(dest, orders, pattern, blocks)
    y_recv = exchange(y_rows, 0, 2)

    own, factor_send = pl.pallas_call(
        pack_own,
        out_shape=(pltpu.HBM((half, max_order, width), F32), pltpu.HBM((n_blk, max_order, CTW), F32)),
        in_specs=[smem, smem, hbm, hbm],
        out_specs=(hbm, hbm),
        scratch_shapes=[
            pltpu.SMEM((n_blk,), jnp.int32),
            pltpu.VMEM((half, max_order, width), F32),
            pltpu.VMEM((n_blk, max_order, CTW), F32),
            dma((half,)),
            dma((n_blk,)),
            dma,
        ],
        compiler_params=params,
        name="pack_own",
    )(table, dest, blocks, inv_factor)
    factors = lax.all_to_all(factor_send, "blk", split_axis=0, concat_axis=0, tiled=True)
    core_recv = exchange(own, 0, 1)
    factors_other = exchange(factors, 0, 1)

    depth = half * max_order
    own_results = pl.pallas_call(
        gram_own,
        out_shape=(
            shape((half, 256, 256), BF16),
            shape((half, 256, 256), BF16),
            shape((half, 128, 384), BF16),
            shape((half, 128, 384), BF16),
            shape((depth, width), BF16),
            shape((depth, width), BF16),
            shape((width, depth), BF16),
            shape((width, depth), BF16),
            shape((2, width, width), F32),
        ),
        in_specs=[smem] * 3 + [hbm] * 4,
        out_specs=(vmem,) * 9,
        scratch_shapes=[
            pltpu.VMEM((half, 2, max_order, width), F32),
            pltpu.VMEM((half, 2, max_order, CTW), F32),
            pltpu.VMEM((width, depth), BF16),
            pltpu.VMEM((width, depth), BF16),
            dma((half,)),
        ],
        compiler_params=params,
        name="gram_own",
    )(table, orders, pattern, own, core_recv, factors, factors_other)

    y_recv, own_results = lax.optimization_barrier((y_recv, own_results))
    yc_recv = exchange(y_recv, 0, 1)
    first_shape, second_shape = (4, XY_FIRST, width), (2, 2, 128 - XY_FIRST, width)
    pieces = pl.pallas_call(
        gram_rest,
        out_shape=(shape(first_shape, F32),) * 4 + (shape(second_shape, F32),) * 4,
        in_specs=[smem] * 3 + [hbm] * 2 + [vmem] * 9,
        out_specs=(hbm,) * 8,
        scratch_shapes=[
            pltpu.VMEM((half, 2 * tiles, max_order, CTW), F32),
            pltpu.VMEM((depth, width), BF16),
            pltpu.VMEM((depth, width), BF16),
            pltpu.VMEM((width, depth), BF16),
            pltpu.VMEM((width, depth), BF16),
            pltpu.VMEM((width, depth), BF16),
            pltpu.VMEM((width, depth), BF16),
            pltpu.VMEM((2, 4, width, width), F32),
            dma((half,)),
            dma,
        ],
        compiler_params=params,
        name="gram_rest",
    )(table, orders, pattern, y_recv, yc_recv, *own_results)
    firsts, seconds = pieces[:4], pieces[4:]

    plane = [(a, b) for a in range(2) for b in range(2) if a or b]
    plane_in = [exchange(firsts[2 * a + b], a, 2 * b) for a, b in plane]
    line_in = [exchange(seconds[n], 2 * n, 0) for n in range(1, 4)]
    first = firsts[0] + sum(plane_in)
    second = seconds[0] + sum(line_in)
    line_in = [exchange(first[n], 2 * n, 0) for n in range(1, 4)]
    plane_in = [exchange(second[a, b], a, 2 * b) for a, b in plane]
    gram_tile = jnp.concatenate([first[0] + sum(line_in), second[0, 0] + sum(plane_in)], axis=0)
    return gram_tile * (1.0 / (block_count * max_order**0.5))


def solution(mesh):
    in_specs = (P("blk", None, "tile"), P(), P(), P(), P("blk", None, None))
    out_specs = P("blk", "tile")
    paired = mesh.shape["blk"] == 8 and mesh.shape["tile"] == 4
    body = paired_body if paired else general_body
    return jax.shard_map(body, mesh=mesh, in_specs=in_specs, out_specs=out_specs, check_vma=False)
```

```python
import functools

import jax
import jax.numpy as jnp
from jax import lax
from jax.experimental import pallas as pl
from jax.experimental.pallas import tpu as pltpu
from jax.sharding import PartitionSpec as P

CTW = 128
F32 = jnp.float32
BF16 = jnp.bfloat16
XY_FIRST = 88
VMEM_LIMIT = 32 << 20


def general_body(blocks, orders, pattern, dest, inv_factor):
    source_index = lax.axis_index("blk")
    owner_count = lax.axis_size("blk")
    tile_index = lax.axis_index("tile")
    slot_count, max_order, column_width = blocks.shape
    block_count = dest.shape[0]
    tiles_here = column_width // CTW
    highest = lax.Precision.HIGHEST
    capacity = (slot_count + owner_count - 1) // owner_count
    dest_grid = dest.reshape(owner_count, slot_count)
    earlier = lax.broadcasted_iota(jnp.int32, (slot_count, slot_count), 1) < lax.broadcasted_iota(
        jnp.int32, (slot_count, slot_count), 0
    )
    matching = dest_grid[:, :, None] == dest_grid[:, None, :]
    ranks = jnp.sum((matching & earlier[None]).astype(jnp.int32), axis=2).reshape(block_count)
    my_dest = lax.dynamic_slice_in_dim(dest, source_index * slot_count, slot_count)
    my_rank = lax.dynamic_slice_in_dim(ranks, source_index * slot_count, slot_count)
    my_orders = lax.dynamic_slice_in_dim(orders, source_index * slot_count, slot_count)
    my_tiles = lax.dynamic_slice(
        pattern, (source_index * slot_count, tile_index * tiles_here), (slot_count, tiles_here)
    )
    row_ids = lax.broadcasted_iota(jnp.int32, (slot_count, max_order), 1)
    row_mask = (row_ids < my_orders[:, None]).astype(F32)
    col_mask = jnp.repeat(my_tiles.astype(F32), CTW, axis=1)
    masked = blocks * row_mask[:, :, None] * col_mask[:, None, :]
    owned = lax.dynamic_slice_in_dim(
        jnp.argsort(dest, stable=True), source_index * slot_count, slot_count
    )
    slot_ids = my_dest * capacity + my_rank
    placing = (
        lax.broadcasted_iota(jnp.int32, (owner_count * capacity, slot_count), 0)
        == slot_ids[None, :]
    ).astype(F32)
    outgoing = jnp.einsum("ak,krc->arc", placing, masked, precision=highest, preferred_element_type=F32)
    arrived = lax.all_to_all(outgoing, "blk", split_axis=0, concat_axis=0, tiled=True)
    positions = owned // slot_count * capacity + ranks[owned]
    own_blocks = jnp.take(arrived, positions, axis=0)
    own_mask = (row_ids < orders[owned][:, None]).astype(F32)
    whitened = jnp.einsum(
        "jrq,jqc->jrc", inv_factor, own_blocks, precision=highest, preferred_element_type=F32
    )
    whitened_rows = (whitened * own_mask[:, :, None]).reshape(slot_count * max_order, column_width)
    factor = 1.0 / (block_count * max_order**0.5)
    partial_sums = lax.dot_general(
        lax.all_gather(whitened_rows, "tile", axis=1, tiled=True),
        whitened_rows,
        (((0,), (0,)), ((), ())),
        precision=highest,
        preferred_element_type=F32,
    )
    gram_tile = lax.psum_scatter(partial_sums, "blk", scatter_dimension=0, tiled=True)
    return gram_tile * factor


MINE, OWNER, ORDER, BITS, OTHERS, ORDER_OTHERS, BITS_OTHERS, ROW_AT = 0, 1, 2, 3, 4, 5, 6, 7
SHARES = (0.625, 1.0)


def round8(order):
    return (order + 7) // 8 * 8


def row_counts(all_rows):
    return [int(share * all_rows) // 8 * 8 for share in SHARES]


def plan(
    dest_ref, weight_ref, orders_ref, pattern_ref, blocks_ref, inv_ref, own_out, factor_out, table_ref, level_ref,
    block_at, count, found_at, factor_at, sem,
):
    s = lax.axis_index("blk")
    t = lax.axis_index("tile")
    y, c = t // 2, t % 2
    slots, max_order, width = blocks_ref.shape
    n_blk = count.shape[0]
    tiles = width // CTW

    def scan_source(source, carry):
        found, most = carry
        for o in range(n_blk):
            count[o] = 0
            block_at[0, o] = 0
            block_at[1, o] = 0
        for i in range(slots):
            o = dest_ref[source * slots + i]
            r = count[o]
            block_at[r, o] = i
            count[o] = r + 1
            mine = o == s
            found_at[jnp.where(mine, r, 2)] = found
            found = found + jnp.where(mine, 1, 0)

        def place_pair(o, carry):
            p, sent = carry[0], carry[1:]
            on = count[o] > 0
            first, second = block_at[0, o], block_at[1, o]
            w_first = [weight_ref[q, source * slots + first] for q in range(4)]
            w_second = [weight_ref[q, source * slots + second] for q in range(4)]
            straight = [sent[q] + (w_second[q] if q < 2 else w_first[q]) for q in range(4)]
            crossed = [sent[q] + (w_first[q] if q < 2 else w_second[q]) for q in range(4)]

            def top(v):
                return jnp.maximum(jnp.maximum(v[0], v[1]), jnp.maximum(v[2], v[3]))

            flip = jnp.where(top(crossed) < top(straight), 1, 0)

            @pl.when(on & (o == s))
            def _():
                factor_at[source] = found_at[y ^ flip]

            @pl.when(on & (source == s))
            def _():
                here, there = jnp.where((y ^ flip) == 0, first, second), jnp.where((y ^ flip) == 0, second, first)
                table_ref[MINE, p] = here
                table_ref[OTHERS, p] = there
                table_ref[OWNER, p] = o

            sent = [jnp.where(on, jnp.where(flip == 1, f, d), q) for f, d, q in zip(crossed, straight, sent)]
            return (p + jnp.where(on, 1, 0), *sent)

        factor_at[source] = 0
        zero = jnp.int32(0)
        sent = lax.fori_loop(0, n_blk, place_pair, (zero,) * 5)[1:]
        for q in sent:
            most = jnp.maximum(most, q)
        return found, most

    most = lax.fori_loop(0, n_blk, scan_source, (jnp.int32(0), jnp.int32(0)))[1]

    def factor_loads():
        for source in range(n_blk):
            row = factor_at[source]
            for k, (ti, tj) in enumerate(((0, 0), (1, 0), (1, 1))):
                ri, rj = jnp.where(c == 0, ti, 2), jnp.where(c == 0, tj, k)
                yield pltpu.make_async_copy(
                    inv_ref.at[row, pl.ds(pl.multiple_of(ri * 128, 128), 128), pl.ds(pl.multiple_of(rj * 128, 128), 128)],
                    factor_out.at[source, pl.ds(k * 128, 128), :],
                    sem,
                )

    def own_loads():
        for p in range(slots // 2):
            yield pltpu.make_async_copy(blocks_ref.at[table_ref[MINE, p]], own_out.at[p], sem)

    for copy in factor_loads():
        copy.start()
    for copy in own_loads():
        copy.start()

    level = jnp.int32(0)
    for rows in row_counts(slots // 2 * tiles * max_order)[:-1]:
        level = level + jnp.where(most + (max_order - 96) > rows, 1, 0)
    level_ref[0] = level

    for which, order_row, bits_row in ((MINE, ORDER, BITS), (OTHERS, ORDER_OTHERS, BITS_OTHERS)):
        for p in range(slots // 2):
            number = s * slots + table_ref[which, p]
            table_ref[order_row, p] = orders_ref[number]
            bits = jnp.int32(0)
            for ct in range(4 * tiles):
                bits = bits + jnp.where(pattern_ref[ct, number] != 0, 1 << ct, 0)
            table_ref[bits_row, p] = bits
    for k in range(2):
        at = jnp.int32(0)
        for p in range(slots // 2):
            rows, bits = round8(table_ref[ORDER, p]), table_ref[BITS, p]
            for e in range(tiles):
                table_ref[ROW_AT + k, p * tiles + e] = at
                at = at + jnp.where(tile_on(bits, (t ^ (2 + k)) * tiles + e), rows, 0)

    for copy in own_loads():
        copy.wait()
    for copy in factor_loads():
        copy.wait()


def tile_on(bits, tile):
    return ((bits >> tile) & 1) == 1


def pack_rows(table_ref, blocks_ref, packed, staged, sems):
    t = lax.axis_index("tile")
    slots, max_order, width = blocks_ref.shape
    tiles = width // CTW

    def loads():
        for p in range(slots // 2):
            yield pltpu.make_async_copy(blocks_ref.at[table_ref[OTHERS, p]], staged.at[p], sems.at[p])

    for copy in loads():
        copy.start()
    at = jnp.int32(0)
    for p, copy in enumerate(loads()):
        copy.wait()
        for e in range(tiles):
            on = tile_on(table_ref[BITS_OTHERS, p], t * tiles + e)

            @pl.when(on)
            def _(at=at, p=p, e=e):
                packed[pl.ds(pl.multiple_of(at, 8), max_order), :] = staged[p, :, e * CTW : (e + 1) * CTW]

            at = at + jnp.where(on, round8(table_ref[ORDER_OTHERS, p]), 0)


def split(x):
    high = x.astype(BF16)
    return high, (x - high.astype(F32)).astype(BF16)


def dot3(a, b):
    def dot(p, q):
        return jnp.dot(p, q, preferred_element_type=F32)

    return dot(a[0], b[0]) + (dot(a[0], b[1]) + dot(a[1], b[0]))


def whiten(tiles, table_ref, p, upper, lower, tile_ids):
    row_on = lax.broadcasted_iota(jnp.int32, tiles[0].shape, 0) < table_ref[ORDER, p]
    parts = [
        jnp.where(row_on & tile_on(table_ref[BITS, p], ct), tile, 0.0) for tile, ct in zip(tiles, tile_ids)
    ]
    x = split(jnp.concatenate(parts, axis=1))
    w = jnp.concatenate([dot3(upper, (x[0][:256], x[1][:256])), dot3(lower, x)], axis=0)
    return [jnp.where(row_on, w[:, i * CTW : (i + 1) * CTW], 0.0) for i in range(len(tiles))]


def gram_own(
    table_ref, own_ref, core_ref, factor_ref, factor_other,
    upper_high, upper_low, lower_high, lower_low, w0_high, w0_low, w1t_high, w1t_low, g_out,
    w0t_high, w0t_low,
):
    t = lax.axis_index("tile")
    c = t % 2
    half, max_order, width = own_ref.shape
    for p in range(half):
        here, there = factor_ref[table_ref[OWNER, p]], factor_other[table_ref[OWNER, p]]
        top, low = jnp.where(c == 0, here, there), jnp.where(c == 0, there, here)
        f00, f10, f11 = top[:128], top[128:256], top[256:]
        upper = split(
            jnp.concatenate(
                [jnp.concatenate([f00, jnp.zeros_like(f00)], axis=1), jnp.concatenate([f10, f11], axis=1)], axis=0
            )
        )
        lower = split(jnp.concatenate([low[:128], low[128:256], low[256:]], axis=1))
        upper_high[p], upper_low[p] = upper
        lower_high[p], lower_low[p] = lower
        tiles = [ref[p, :, e * CTW : (e + 1) * CTW] for ref in (own_ref, core_ref) for e in range(2)]
        tile_ids = [(t ^ m) * 2 + e for m in range(2) for e in range(2)]
        w = whiten(tiles, table_ref, p, upper, lower, tile_ids)
        rows = pl.ds(p * max_order, max_order)
        w0, w1 = jnp.concatenate(w[:2], axis=1), jnp.concatenate(w[2:], axis=1)
        w0_high[rows, :], w0_low[rows, :] = split(w0)
        w0t_high[:, rows], w0t_low[:, rows] = split(w0.T)
        w1t_high[:, rows], w1t_low[:, rows] = split(w1.T)
    w0 = w0_high[...], w0_low[...]
    g_out[0] = dot3((w0t_high[...], w0t_low[...]), w0)
    g_out[1] = dot3((w1t_high[...], w1t_low[...]), w0)


def gram_rest(
    table_ref, y_ref, yc_ref,
    upper_high, upper_low, lower_high, lower_low, w0_high, w0_low, w1t_high, w1t_low, g_own,
    *refs,
):
    firsts, seconds = refs[:4], refs[4:8]
    w2_high, w2_low, w23t_high, w23t_low, gram, out_sem = refs[8:]
    s = lax.axis_index("blk")
    t = lax.axis_index("tile")
    half = upper_high.shape[0]
    depth, width = w0_high.shape
    max_order = depth // half
    last = y_ref.shape[0] - max_order
    for p in range(half):
        tiles = []
        for k, ref in enumerate((y_ref, yc_ref)):
            for e in range(2):
                at = pl.multiple_of(jnp.minimum(table_ref[ROW_AT + k, p * 2 + e], last), 8)
                tiles.append(ref[pl.ds(at, max_order), :])
        tile_ids = [(t ^ (2 + k)) * 2 + e for k in range(2) for e in range(2)]
        upper, lower = (upper_high[p], upper_low[p]), (lower_high[p], lower_low[p])
        w = whiten(tiles, table_ref, p, upper, lower, tile_ids)
        rows = pl.ds(p * max_order, max_order)
        w2_high[rows, :], w2_low[rows, :] = split(jnp.concatenate(w[:2], axis=1))
        w23t_high[:, rows], w23t_low[:, rows] = split(jnp.concatenate(w, axis=1).T)

    w0, w2 = (w0_high[...], w0_low[...]), (w2_high[...], w2_low[...])
    w1t, w23t = (w1t_high[...], w1t_low[...]), (w23t_high[...], w23t_low[...])
    gram[0, 0] = g_own[0]
    gram[0, 1] = g_own[1]
    g = dot3(w23t, w0)
    gram[0, 2] = g[:width]
    gram[0, 3] = g[width:]
    gram[1, 0] = g[:width].T
    gram[1, 1] = dot3(w1t, w2)
    g = dot3(w23t, w2)
    gram[1, 2] = g[:width]
    gram[1, 3] = g[width:]

    z, x = s // 2, s % 2

    def stores():
        for n in range(4):
            for a in range(2):
                for b in range(2):
                    m, at = (z ^ n) ^ t, (x ^ a) * 128
                    first, second = firsts[2 * a + b], seconds[n]
                    yield pltpu.make_async_copy(
                        gram.at[b, m, pl.ds(pl.multiple_of(at, 8), XY_FIRST), :], first.at[n], out_sem
                    )
                    yield pltpu.make_async_copy(
                        gram.at[b, m, pl.ds(pl.multiple_of(at + XY_FIRST, 8), 128 - XY_FIRST), :],
                        second.at[a, b],
                        out_sem,
                    )

    for copy in stores():
        copy.start()
    for copy in stores():
        copy.wait()


def paired_body(blocks, orders, pattern, dest, inv_factor):
    slots, max_order, width = blocks.shape
    n_blk = lax.axis_size("blk")
    half = slots // 2
    tiles = width // CTW
    blocks = pltpu.with_memory_space_constraint(blocks, pltpu.HBM)
    inv_factor = pltpu.with_memory_space_constraint(inv_factor, pltpu.HBM)
    pattern = pattern.T
    weights = round8(orders)[None, :] * jnp.sum((pattern != 0).astype(jnp.int32).reshape(4, tiles, -1), axis=1)
    hbm = pl.BlockSpec(memory_space=pltpu.HBM)
    smem = pl.BlockSpec(memory_space=pltpu.SMEM)
    vmem = pl.BlockSpec(memory_space=pltpu.VMEM)
    shape = jax.ShapeDtypeStruct
    own, factor_send, table, level = pl.pallas_call(
        plan,
        out_shape=(
            shape((half, max_order, width), F32),
            shape((n_blk, max_order, CTW), F32),
            shape((9, half * tiles), jnp.int32),
            shape((1,), jnp.int32),
        ),
        in_specs=[smem] * 4 + [hbm] * 2,
        out_specs=(vmem, vmem, smem, smem),
        scratch_shapes=[
            pltpu.SMEM((2, n_blk), jnp.int32),
            pltpu.SMEM((n_blk,), jnp.int32),
            pltpu.SMEM((3,), jnp.int32),
            pltpu.SMEM((n_blk,), jnp.int32),
            pltpu.SemaphoreType.DMA,
        ],
        compiler_params=pltpu.CompilerParams(vmem_limit_bytes=VMEM_LIMIT),
        name="plan",
    )(dest, weights, orders, pattern, blocks, inv_factor)
    rest = [functools.partial(paired_rest, rows) for rows in row_counts(half * tiles * max_order)]
    gram_tile = lax.switch(level[0], rest, table, blocks, own, factor_send)
    return gram_tile * (1.0 / (dest.shape[0] * max_order**0.5))


def paired_rest(row_count, table, blocks, own, factor_send):
    slots, max_order, width = blocks.shape
    n_blk = lax.axis_size("blk")
    n_tile = lax.axis_size("tile")
    half = slots // 2
    tiles = width // CTW
    axes = ("blk", "tile")

    def exchange(value, blk_bits, tile_bits):
        perm = [
            (b * n_tile + t, (b ^ blk_bits) * n_tile + (t ^ tile_bits)) for b in range(n_blk) for t in range(n_tile)
        ]
        return lax.ppermute(value, axes, perm)

    hbm = pl.BlockSpec(memory_space=pltpu.HBM)
    smem = pl.BlockSpec(memory_space=pltpu.SMEM)
    vmem = pl.BlockSpec(memory_space=pltpu.VMEM)
    any_space = pl.BlockSpec(memory_space=pl.ANY)
    shape = jax.ShapeDtypeStruct
    params = pltpu.CompilerParams(vmem_limit_bytes=VMEM_LIMIT)
    dma = pltpu.SemaphoreType.DMA

    y_rows = pl.pallas_call(
        pack_rows,
        out_shape=shape((row_count, CTW), F32),
        in_specs=[smem, hbm],
        out_specs=vmem,
        scratch_shapes=[pltpu.VMEM((half, max_order, width), F32), dma((half,))],
        compiler_params=params,
        name="pack_rows",
    )(table, blocks)
    y_recv = exchange(y_rows, 0, 2)
    factors = lax.all_to_all(factor_send, "blk", split_axis=0, concat_axis=0, tiled=True)
    core_recv = exchange(own, 0, 1)
    factors_other = exchange(factors, 0, 1)

    depth = half * max_order
    own_results = pl.pallas_call(
        gram_own,
        out_shape=(
            shape((half, 256, 256), BF16),
            shape((half, 256, 256), BF16),
            shape((half, 128, 384), BF16),
            shape((half, 128, 384), BF16),
            shape((depth, width), BF16),
            shape((depth, width), BF16),
            shape((width, depth), BF16),
            shape((width, depth), BF16),
            shape((2, width, width), F32),
        ),
        in_specs=[smem] + [vmem] * 4,
        out_specs=(vmem,) * 9,
        scratch_shapes=[pltpu.VMEM((width, depth), BF16), pltpu.VMEM((width, depth), BF16)],
        compiler_params=params,
        name="gram_own",
    )(table, own, core_recv, factors, factors_other)

    yc_recv = exchange(y_recv, 0, 1)
    first_shape, second_shape = (4, XY_FIRST, width), (2, 2, 128 - XY_FIRST, width)
    pieces = pl.pallas_call(
        gram_rest,
        out_shape=(shape(first_shape, F32),) * 4 + (shape(second_shape, F32),) * 4,
        in_specs=[smem] + [vmem] * 11,
        out_specs=(any_space,) * 8,
        scratch_shapes=[
            pltpu.VMEM((depth, width), BF16),
            pltpu.VMEM((depth, width), BF16),
            pltpu.VMEM((2 * width, depth), BF16),
            pltpu.VMEM((2 * width, depth), BF16),
            pltpu.VMEM((2, 4, width, width), F32),
            dma,
        ],
        compiler_params=params,
        name="gram_rest",
    )(table, y_recv, yc_recv, *own_results)
    firsts, seconds = pieces[:4], pieces[4:]

    plane = [(a, b) for a in range(2) for b in range(2) if a or b]
    plane_in = [exchange(firsts[2 * a + b], a, 2 * b) for a, b in plane]
    line_in = [exchange(seconds[n], 2 * n, 0) for n in range(1, 4)]
    first = firsts[0] + sum(plane_in)
    second = seconds[0] + sum(line_in)
    line_in = [exchange(first[n], 2 * n, 0) for n in range(1, 4)]
    plane_in = [exchange(second[a, b], a, 2 * b) for a, b in plane]
    return jnp.concatenate([first[0] + sum(line_in), second[0, 0] + sum(plane_in)], axis=0)


def solution(mesh):
    in_specs = (P("blk", None, "tile"), P(), P(), P(), P("blk", None, None))
    out_specs = P("blk", "tile")
    paired = mesh.shape["blk"] == 8 and mesh.shape["tile"] == 4
    body = paired_body if paired else general_body
    return jax.shard_map(body, mesh=mesh, in_specs=in_specs, out_specs=out_specs, check_vma=False)
```

```python
import functools

import jax
import jax.numpy as jnp
from jax import lax
from jax.experimental import pallas as pl
from jax.experimental.pallas import tpu as pltpu
from jax.sharding import PartitionSpec as P

CTW = 128
F32 = jnp.float32
BF16 = jnp.bfloat16
XY_FIRST = 88
VMEM_LIMIT = 32 << 20


def general_body(blocks, orders, pattern, dest, inv_factor):
    source_index = lax.axis_index("blk")
    owner_count = lax.axis_size("blk")
    tile_index = lax.axis_index("tile")
    slot_count, max_order, column_width = blocks.shape
    block_count = dest.shape[0]
    tiles_here = column_width // CTW
    highest = lax.Precision.HIGHEST
    capacity = (slot_count + owner_count - 1) // owner_count
    dest_grid = dest.reshape(owner_count, slot_count)
    earlier = lax.broadcasted_iota(jnp.int32, (slot_count, slot_count), 1) < lax.broadcasted_iota(
        jnp.int32, (slot_count, slot_count), 0
    )
    matching = dest_grid[:, :, None] == dest_grid[:, None, :]
    ranks = jnp.sum((matching & earlier[None]).astype(jnp.int32), axis=2).reshape(block_count)
    my_dest = lax.dynamic_slice_in_dim(dest, source_index * slot_count, slot_count)
    my_rank = lax.dynamic_slice_in_dim(ranks, source_index * slot_count, slot_count)
    my_orders = lax.dynamic_slice_in_dim(orders, source_index * slot_count, slot_count)
    my_tiles = lax.dynamic_slice(
        pattern, (source_index * slot_count, tile_index * tiles_here), (slot_count, tiles_here)
    )
    row_ids = lax.broadcasted_iota(jnp.int32, (slot_count, max_order), 1)
    row_mask = (row_ids < my_orders[:, None]).astype(F32)
    col_mask = jnp.repeat(my_tiles.astype(F32), CTW, axis=1)
    masked = blocks * row_mask[:, :, None] * col_mask[:, None, :]
    owned = lax.dynamic_slice_in_dim(
        jnp.argsort(dest, stable=True), source_index * slot_count, slot_count
    )
    slot_ids = my_dest * capacity + my_rank
    placing = (
        lax.broadcasted_iota(jnp.int32, (owner_count * capacity, slot_count), 0)
        == slot_ids[None, :]
    ).astype(F32)
    outgoing = jnp.einsum("ak,krc->arc", placing, masked, precision=highest, preferred_element_type=F32)
    arrived = lax.all_to_all(outgoing, "blk", split_axis=0, concat_axis=0, tiled=True)
    positions = owned // slot_count * capacity + ranks[owned]
    own_blocks = jnp.take(arrived, positions, axis=0)
    own_mask = (row_ids < orders[owned][:, None]).astype(F32)
    whitened = jnp.einsum(
        "jrq,jqc->jrc", inv_factor, own_blocks, precision=highest, preferred_element_type=F32
    )
    whitened_rows = (whitened * own_mask[:, :, None]).reshape(slot_count * max_order, column_width)
    factor = 1.0 / (block_count * max_order**0.5)
    partial_sums = lax.dot_general(
        lax.all_gather(whitened_rows, "tile", axis=1, tiled=True),
        whitened_rows,
        (((0,), (0,)), ((), ())),
        precision=highest,
        preferred_element_type=F32,
    )
    gram_tile = lax.psum_scatter(partial_sums, "blk", scatter_dimension=0, tiled=True)
    return gram_tile * factor


MINE, OWNER, ORDER, BITS, OTHERS, ORDER_OTHERS, BITS_OTHERS, ROW_AT = 0, 1, 2, 3, 4, 5, 6, 7
SHARES = (0.625, 1.0)


def round8(order):
    return (order + 7) // 8 * 8


def row_counts(all_rows):
    return [int(share * all_rows) // 8 * 8 for share in SHARES]


TOP_ROWS = 32
FACTOR_ROWS = 128 + 128 + 8 + TOP_ROWS


def iotas(rows):
    return tuple(lax.broadcasted_iota(jnp.int32, (rows, 128), axis) for axis in range(2))


def fold_factor(c, tiles, top, out):
    @pl.when(c == 0)
    def _():
        row, col = iotas(128)
        t11 = tiles[2]
        out[:128] = tiles[1]
        out[128:256] = jnp.where(row >= col, tiles[0], t11.T)
        out[256:264] = jnp.broadcast_to(jnp.sum(jnp.where(row == col, t11, 0.0), axis=0, keepdims=True), (8, 128))
        out[264:] = top[...]

    @pl.when(c == 1)
    def _():
        row, col = iotas(64)
        t22 = tiles[2]
        low = t22[64:]
        out[: 128 - TOP_ROWS] = tiles[0, TOP_ROWS:]
        out[128 - TOP_ROWS : 256 - TOP_ROWS] = tiles[1]
        out[256 - TOP_ROWS : 320 - TOP_ROWS] = jnp.where(
            col >= 64,
            pltpu.roll(low, 64, 1),
            jnp.where(row >= col, t22[:64], pltpu.roll(t22.T[64:], 64, 1)),
        )
        out[320 - TOP_ROWS :] = jnp.broadcast_to(
            jnp.sum(jnp.where(row + 64 == col, low, 0.0), axis=0, keepdims=True), (8, 128)
        )


def unfold_factor(first, second):
    row, col = iotas(128)
    both = first[128:256]
    f00 = jnp.where(row >= col, both, 0.0)
    f11 = jnp.where(row > col, both.T, jnp.where(row == col, first[256:257], 0.0))
    upper = jnp.concatenate(
        [jnp.concatenate([f00, jnp.zeros_like(f00)], axis=1), jnp.concatenate([first[:128], f11], axis=1)], axis=0
    )
    f20 = jnp.concatenate([first[264:], second[: 128 - TOP_ROWS]], axis=0)
    f21 = second[128 - TOP_ROWS : 256 - TOP_ROWS]
    fold, diagonal = second[256 - TOP_ROWS : 320 - TOP_ROWS], second[320 - TOP_ROWS : 321 - TOP_ROWS]
    turned = jnp.concatenate([fold, fold], axis=0).T[:64]
    row, col = iotas(64)
    f22 = jnp.concatenate(
        [
            jnp.where((row >= col) & (col < 64), fold, 0.0),
            jnp.where(
                col < 64,
                pltpu.roll(fold, 64, 1),
                jnp.where(row + 64 > col, pltpu.roll(turned, 64, 1), jnp.where(row + 64 == col, diagonal, 0.0)),
            ),
        ],
        axis=0,
    )
    return upper, jnp.concatenate([f20, f21, f22], axis=1)


def plan(
    dest_hbm, orders_hbm, pattern_hbm, blocks_ref, inv_ref, own_out, factor_out, table_ref, level_ref,
    dest_ref, orders_ref, pattern_ref, orders_at, pattern_at, weight_at, weight_ref, block_at, count, found_at, factor_at, tiles_at, top_at, small_sem, factor_sem, sem,
):
    s = lax.axis_index("blk")
    t = lax.axis_index("tile")
    y, c = t // 2, t % 2
    slots, max_order, width = blocks_ref.shape
    n_blk = count.shape[0]
    tiles = width // CTW

    def small_loads():
        for src, dst in (
            (orders_hbm, orders_at), (pattern_hbm, pattern_at), (dest_hbm, dest_ref), (orders_hbm, orders_ref), (pattern_hbm, pattern_ref),
        ):
            yield pltpu.make_async_copy(src, dst, small_sem)

    def factor_loads():
        for row in range(slots):
            for k, (ti, tj) in enumerate(((0, 0), (1, 0), (1, 1))):
                ri, rj = jnp.where(c == 0, ti, 2), jnp.where(c == 0, tj, k)
                yield pltpu.make_async_copy(
                    inv_ref.at[row, pl.ds(pl.multiple_of(ri * 128, 128), 128), pl.ds(pl.multiple_of(rj * 128, 128), 128)],
                    tiles_at.at[row, k],
                    factor_sem,
                )
            yield pltpu.make_async_copy(
                inv_ref.at[row, pl.ds(256, TOP_ROWS), pl.ds(0, 128)], top_at.at[row], factor_sem
            )

    for copy in small_loads():
        copy.start()
    for copy in factor_loads():
        copy.start()
    for copy in small_loads():
        copy.wait()
    ones = pattern_at[...]
    counts = [sum(ones[q * tiles + e : q * tiles + e + 1] for e in range(tiles)) for q in range(4)]
    rows = round8(orders_at[...])[None, :]
    weight_at[...] = jnp.concatenate([rows * (counts[q] + counts[q + 1] * 65536) for q in (0, 2)], axis=0)
    weights = pltpu.make_async_copy(weight_at, weight_ref, small_sem)
    weights.start()
    weights.wait()

    def scan_source(source, carry):
        found, most = carry
        base = source * slots
        for o in range(n_blk):
            count[o] = 0
            block_at[0, o] = 0
            block_at[1, o] = 0
        for i in range(slots):
            o = dest_ref[base + i]
            r = count[o]
            block_at[r, o] = i
            count[o] = r + 1
            mine = o == s
            found_at[jnp.where(mine, r, 2)] = found
            found = found + jnp.where(mine, 1, 0)

        def top(v):
            return jnp.maximum(jnp.maximum(v[0] & 65535, v[0] >> 16), jnp.maximum(v[1] & 65535, v[1] >> 16))

        here = source == s
        p, low, high = jnp.int32(0), jnp.int32(0), jnp.int32(0)
        for o in range(n_blk):
            on = count[o] > 0
            first, second = block_at[0, o], block_at[1, o]
            straight = low + weight_ref[0, base + second], high + weight_ref[1, base + first]
            crossed = low + weight_ref[0, base + first], high + weight_ref[1, base + second]
            flip = top(crossed) < top(straight)
            side = y ^ jnp.where(flip, 1, 0)
            factor_at[jnp.where(on & (s == o), source, n_blk)] = found_at[side]
            column = jnp.where(on & here, p, slots // 2)
            table_ref[MINE, column] = jnp.where(side == 0, first, second)
            table_ref[OTHERS, column] = jnp.where(side == 0, second, first)
            table_ref[OWNER, column] = jnp.int32(o)
            low = jnp.where(on, jnp.where(flip, crossed[0], straight[0]), low)
            high = jnp.where(on, jnp.where(flip, crossed[1], straight[1]), high)
            p = p + jnp.where(on, 1, 0)
        return found, jnp.maximum(most, top((low, high)))

    for source in range(n_blk):
        factor_at[source] = 0
    found_at[0] = 0
    found_at[1] = 0
    most = lax.fori_loop(0, n_blk, scan_source, (jnp.int32(0), jnp.int32(0)))[1]

    def own_loads():
        for p in range(slots // 2):
            yield pltpu.make_async_copy(blocks_ref.at[table_ref[MINE, p]], own_out.at[p], sem)

    for copy in own_loads():
        copy.start()

    level = jnp.int32(0)
    for rows in row_counts(slots // 2 * tiles * max_order)[:-1]:
        level = level + jnp.where(most + (max_order - 96) > rows, 1, 0)
    level_ref[0] = level

    for which, order_row, bits_row in ((MINE, ORDER, BITS), (OTHERS, ORDER_OTHERS, BITS_OTHERS)):
        for p in range(slots // 2):
            number = s * slots + table_ref[which, p]
            table_ref[order_row, p] = orders_ref[number]
            bits = jnp.int32(0)
            for ct in range(4 * tiles):
                bits = bits + jnp.where(pattern_ref[ct, number] != 0, 1 << ct, 0)
            table_ref[bits_row, p] = bits
    for k in range(2):
        at = jnp.int32(0)
        for p in range(slots // 2):
            rows, bits = round8(table_ref[ORDER, p]), table_ref[BITS, p]
            for e in range(tiles):
                table_ref[ROW_AT + k, p * tiles + e] = at
                at = at + jnp.where(tile_on(bits, (t ^ (2 + k)) * tiles + e), rows, 0)

    for copy in factor_loads():
        copy.wait()

    def fold(source, carry):
        row = factor_at[source]
        fold_factor(c, tiles_at.at[row], top_at.at[row], factor_out.at[source])
        return carry

    lax.fori_loop(0, n_blk, fold, 0)
    for copy in own_loads():
        copy.wait()


def tile_on(bits, tile):
    return ((bits >> tile) & 1) == 1


def pack_rows(table_ref, blocks_ref, packed, staged, sems):
    t = lax.axis_index("tile")
    slots, max_order, width = blocks_ref.shape
    tiles = width // CTW

    def loads():
        for p in range(slots // 2):
            yield pltpu.make_async_copy(blocks_ref.at[table_ref[OTHERS, p]], staged.at[p], sems.at[p])

    for copy in loads():
        copy.start()
    at = jnp.int32(0)
    for p, copy in enumerate(loads()):
        copy.wait()
        for e in range(tiles):
            on = tile_on(table_ref[BITS_OTHERS, p], t * tiles + e)

            @pl.when(on)
            def _(at=at, p=p, e=e):
                packed[pl.ds(pl.multiple_of(at, 8), max_order), :] = staged[p, :, e * CTW : (e + 1) * CTW]

            at = at + jnp.where(on, round8(table_ref[ORDER_OTHERS, p]), 0)


def split(x):
    high = x.astype(BF16)
    return high, (x - high.astype(F32)).astype(BF16)


def dot3(a, b):
    def dot(p, q):
        return jnp.dot(p, q, preferred_element_type=F32)

    return dot(a[0], b[0]) + (dot(a[0], b[1]) + dot(a[1], b[0]))


def whiten(tiles, table_ref, p, upper, lower, tile_ids):
    row_on = lax.broadcasted_iota(jnp.int32, tiles[0].shape, 0) < table_ref[ORDER, p]
    parts = [
        jnp.where(row_on & tile_on(table_ref[BITS, p], ct), tile, 0.0) for tile, ct in zip(tiles, tile_ids)
    ]
    x = split(jnp.concatenate(parts, axis=1))
    w = jnp.concatenate([dot3(upper, (x[0][:256], x[1][:256])), dot3(lower, x)], axis=0)
    return [jnp.where(row_on, w[:, i * CTW : (i + 1) * CTW], 0.0) for i in range(len(tiles))]


def gram_own(
    table_ref, own_ref, core_ref, factor_ref, factor_other,
    upper_high, upper_low, lower_high, lower_low, w0_high, w0_low, w1t_high, w1t_low, g_out,
    w0t_high, w0t_low,
):
    t = lax.axis_index("tile")
    c = t % 2
    half, max_order, width = own_ref.shape
    for p in range(half):
        here, there = factor_ref[table_ref[OWNER, p]], factor_other[table_ref[OWNER, p]]
        upper, lower = unfold_factor(jnp.where(c == 0, here, there), jnp.where(c == 0, there, here))
        upper, lower = split(upper), split(lower)
        upper_high[p], upper_low[p] = upper
        lower_high[p], lower_low[p] = lower
        tiles = [ref[p, :, e * CTW : (e + 1) * CTW] for ref in (own_ref, core_ref) for e in range(2)]
        tile_ids = [(t ^ m) * 2 + e for m in range(2) for e in range(2)]
        w = whiten(tiles, table_ref, p, upper, lower, tile_ids)
        rows = pl.ds(p * max_order, max_order)
        w0, w1 = jnp.concatenate(w[:2], axis=1), jnp.concatenate(w[2:], axis=1)
        w0_high[rows, :], w0_low[rows, :] = split(w0)
        w0t_high[:, rows], w0t_low[:, rows] = split(w0.T)
        w1t_high[:, rows], w1t_low[:, rows] = split(w1.T)
    w0 = w0_high[...], w0_low[...]
    g_out[0] = dot3((w0t_high[...], w0t_low[...]), w0)
    g_out[1] = dot3((w1t_high[...], w1t_low[...]), w0)


def gram_rest(
    table_ref, y_ref, yc_ref,
    upper_high, upper_low, lower_high, lower_low, w0_high, w0_low, w1t_high, w1t_low, g_own,
    *refs,
):
    firsts, seconds = refs[:4], refs[4:8]
    w2_high, w2_low, w23t_high, w23t_low, gram, out_sem = refs[8:]
    s = lax.axis_index("blk")
    t = lax.axis_index("tile")
    half = upper_high.shape[0]
    depth, width = w0_high.shape
    max_order = depth // half
    last = y_ref.shape[0] - max_order
    for p in range(half):
        tiles = []
        for k, ref in enumerate((y_ref, yc_ref)):
            for e in range(2):
                at = pl.multiple_of(jnp.minimum(table_ref[ROW_AT + k, p * 2 + e], last), 8)
                tiles.append(ref[pl.ds(at, max_order), :])
        tile_ids = [(t ^ (2 + k)) * 2 + e for k in range(2) for e in range(2)]
        upper, lower = (upper_high[p], upper_low[p]), (lower_high[p], lower_low[p])
        w = whiten(tiles, table_ref, p, upper, lower, tile_ids)
        rows = pl.ds(p * max_order, max_order)
        w2_high[rows, :], w2_low[rows, :] = split(jnp.concatenate(w[:2], axis=1))
        w23t_high[:, rows], w23t_low[:, rows] = split(jnp.concatenate(w, axis=1).T)

    w0, w2 = (w0_high[...], w0_low[...]), (w2_high[...], w2_low[...])
    w1t, w23t = (w1t_high[...], w1t_low[...]), (w23t_high[...], w23t_low[...])
    gram[0, 0] = g_own[0]
    gram[0, 1] = g_own[1]
    g = dot3(w23t, w0)
    gram[0, 2] = g[:width]
    gram[0, 3] = g[width:]
    gram[1, 0] = g[:width].T
    gram[1, 1] = dot3(w1t, w2)
    g = dot3(w23t, w2)
    gram[1, 2] = g[:width]
    gram[1, 3] = g[width:]

    z, x = s // 2, s % 2

    def stores():
        for n in range(4):
            for a in range(2):
                for b in range(2):
                    m, at = (z ^ n) ^ t, (x ^ a) * 128
                    first, second = firsts[2 * a + b], seconds[n]
                    yield pltpu.make_async_copy(
                        gram.at[b, m, pl.ds(pl.multiple_of(at, 8), XY_FIRST), :], first.at[n], out_sem
                    )
                    yield pltpu.make_async_copy(
                        gram.at[b, m, pl.ds(pl.multiple_of(at + XY_FIRST, 8), 128 - XY_FIRST), :],
                        second.at[a, b],
                        out_sem,
                    )

    for copy in stores():
        copy.start()
    for copy in stores():
        copy.wait()


def paired_body(blocks, orders, pattern, dest, inv_factor):
    slots, max_order, width = blocks.shape
    n_blk = lax.axis_size("blk")
    half = slots // 2
    tiles = width // CTW
    blocks = pltpu.with_memory_space_constraint(blocks, pltpu.HBM)
    inv_factor = pltpu.with_memory_space_constraint(inv_factor, pltpu.HBM)
    dest, orders, pattern = (pltpu.with_memory_space_constraint(v, pltpu.HBM) for v in (dest, orders, pattern.T))
    hbm = pl.BlockSpec(memory_space=pltpu.HBM)
    smem = pl.BlockSpec(memory_space=pltpu.SMEM)
    vmem = pl.BlockSpec(memory_space=pltpu.VMEM)
    shape = jax.ShapeDtypeStruct
    own, factor_send, table, level = pl.pallas_call(
        plan,
        out_shape=(
            shape((half, max_order, width), F32),
            shape((n_blk, FACTOR_ROWS, CTW), F32),
            shape((9, half * tiles), jnp.int32),
            shape((1,), jnp.int32),
        ),
        in_specs=[hbm] * 5,
        out_specs=(vmem, vmem, smem, smem),
        scratch_shapes=[
            pltpu.SMEM(dest.shape, jnp.int32),
            pltpu.SMEM(orders.shape, jnp.int32),
            pltpu.SMEM(pattern.shape, jnp.int32),
            pltpu.VMEM(orders.shape, jnp.int32),
            pltpu.VMEM(pattern.shape, jnp.int32),
            pltpu.VMEM((2, dest.shape[0]), jnp.int32),
            pltpu.SMEM((2, dest.shape[0]), jnp.int32),
            pltpu.SMEM((2, n_blk), jnp.int32),
            pltpu.SMEM((n_blk,), jnp.int32),
            pltpu.SMEM((3,), jnp.int32),
            pltpu.SMEM((n_blk + 1,), jnp.int32),
            pltpu.VMEM((slots, 3, 128, 128), F32),
            pltpu.VMEM((slots, TOP_ROWS, 128), F32),
            pltpu.SemaphoreType.DMA,
            pltpu.SemaphoreType.DMA,
            pltpu.SemaphoreType.DMA,
        ],
        compiler_params=pltpu.CompilerParams(vmem_limit_bytes=VMEM_LIMIT),
        name="plan",
    )(dest, orders, pattern, blocks, inv_factor)
    rest = [functools.partial(paired_rest, rows) for rows in row_counts(half * tiles * max_order)]
    gram_tile = lax.switch(level[0], rest, table, blocks, own, factor_send)
    return gram_tile * (1.0 / (dest.shape[0] * max_order**0.5))


def paired_rest(row_count, table, blocks, own, factor_send):
    slots, max_order, width = blocks.shape
    n_blk = lax.axis_size("blk")
    n_tile = lax.axis_size("tile")
    half = slots // 2
    tiles = width // CTW
    axes = ("blk", "tile")

    def exchange(value, blk_bits, tile_bits):
        perm = [
            (b * n_tile + t, (b ^ blk_bits) * n_tile + (t ^ tile_bits)) for b in range(n_blk) for t in range(n_tile)
        ]
        return lax.ppermute(value, axes, perm)

    hbm = pl.BlockSpec(memory_space=pltpu.HBM)
    smem = pl.BlockSpec(memory_space=pltpu.SMEM)
    vmem = pl.BlockSpec(memory_space=pltpu.VMEM)
    any_space = pl.BlockSpec(memory_space=pl.ANY)
    shape = jax.ShapeDtypeStruct
    params = pltpu.CompilerParams(vmem_limit_bytes=VMEM_LIMIT)
    dma = pltpu.SemaphoreType.DMA

    y_rows = pl.pallas_call(
        pack_rows,
        out_shape=shape((row_count, CTW), F32),
        in_specs=[smem, hbm],
        out_specs=vmem,
        scratch_shapes=[pltpu.VMEM((half, max_order, width), F32), dma((half,))],
        compiler_params=params,
        name="pack_rows",
    )(table, blocks)
    y_recv = exchange(y_rows, 0, 2)
    factors = lax.all_to_all(factor_send, "blk", split_axis=0, concat_axis=0, tiled=True)
    core_recv = exchange(own, 0, 1)
    factors_other = exchange(factors, 0, 1)

    depth = half * max_order
    own_results = pl.pallas_call(
        gram_own,
        out_shape=(
            shape((half, 256, 256), BF16),
            shape((half, 256, 256), BF16),
            shape((half, 128, 384), BF16),
            shape((half, 128, 384), BF16),
            shape((depth, width), BF16),
            shape((depth, width), BF16),
            shape((width, depth), BF16),
            shape((width, depth), BF16),
            shape((2, width, width), F32),
        ),
        in_specs=[smem] + [vmem] * 4,
        out_specs=(vmem,) * 9,
        scratch_shapes=[pltpu.VMEM((width, depth), BF16), pltpu.VMEM((width, depth), BF16)],
        compiler_params=params,
        name="gram_own",
    )(table, own, core_recv, factors, factors_other)

    y_recv, own_results = lax.optimization_barrier((y_recv, own_results))
    yc_recv = exchange(y_recv, 0, 1)
    first_shape, second_shape = (4, XY_FIRST, width), (2, 2, 128 - XY_FIRST, width)
    pieces = pl.pallas_call(
        gram_rest,
        out_shape=(shape(first_shape, F32),) * 4 + (shape(second_shape, F32),) * 4,
        in_specs=[smem] + [vmem] * 11,
        out_specs=(any_space,) * 8,
        scratch_shapes=[
            pltpu.VMEM((depth, width), BF16),
            pltpu.VMEM((depth, width), BF16),
            pltpu.VMEM((2 * width, depth), BF16),
            pltpu.VMEM((2 * width, depth), BF16),
            pltpu.VMEM((2, 4, width, width), F32),
            dma,
        ],
        compiler_params=params,
        name="gram_rest",
    )(table, y_recv, yc_recv, *own_results)
    firsts, seconds = pieces[:4], pieces[4:]

    plane = [(a, b) for a in range(2) for b in range(2) if a or b]
    plane_in = [exchange(firsts[2 * a + b], a, 2 * b) for a, b in plane]
    line_in = [exchange(seconds[n], 2 * n, 0) for n in range(1, 4)]
    first = firsts[0] + sum(plane_in)
    second = seconds[0] + sum(line_in)
    line_in = [exchange(first[n], 2 * n, 0) for n in range(1, 4)]
    plane_in = [exchange(second[a, b], a, 2 * b) for a, b in plane]
    return jnp.concatenate([first[0] + sum(line_in), second[0, 0] + sum(plane_in)], axis=0)


def solution(mesh):
    in_specs = (P("blk", None, "tile"), P(), P(), P(), P("blk", None, None))
    out_specs = P("blk", "tile")
    paired = mesh.shape["blk"] == 8 and mesh.shape["tile"] == 4
    body = paired_body if paired else general_body
    return jax.shard_map(body, mesh=mesh, in_specs=in_specs, out_specs=out_specs, check_vma=False)
```

```python
import functools

import jax
import jax.numpy as jnp
from jax import lax
from jax.experimental import pallas as pl
from jax.experimental.pallas import tpu as pltpu
from jax.sharding import PartitionSpec as P

CTW = 128
F32 = jnp.float32
BF16 = jnp.bfloat16
XY_FIRST = 80
VMEM_LIMIT = 32 << 20


def general_body(blocks, orders, pattern, dest, inv_factor):
    source_index = lax.axis_index("blk")
    owner_count = lax.axis_size("blk")
    tile_index = lax.axis_index("tile")
    slot_count, max_order, column_width = blocks.shape
    block_count = dest.shape[0]
    tiles_here = column_width // CTW
    highest = lax.Precision.HIGHEST
    capacity = (slot_count + owner_count - 1) // owner_count
    dest_grid = dest.reshape(owner_count, slot_count)
    earlier = lax.broadcasted_iota(jnp.int32, (slot_count, slot_count), 1) < lax.broadcasted_iota(
        jnp.int32, (slot_count, slot_count), 0
    )
    matching = dest_grid[:, :, None] == dest_grid[:, None, :]
    ranks = jnp.sum((matching & earlier[None]).astype(jnp.int32), axis=2).reshape(block_count)
    my_dest = lax.dynamic_slice_in_dim(dest, source_index * slot_count, slot_count)
    my_rank = lax.dynamic_slice_in_dim(ranks, source_index * slot_count, slot_count)
    my_orders = lax.dynamic_slice_in_dim(orders, source_index * slot_count, slot_count)
    my_tiles = lax.dynamic_slice(
        pattern, (source_index * slot_count, tile_index * tiles_here), (slot_count, tiles_here)
    )
    row_ids = lax.broadcasted_iota(jnp.int32, (slot_count, max_order), 1)
    row_mask = (row_ids < my_orders[:, None]).astype(F32)
    col_mask = jnp.repeat(my_tiles.astype(F32), CTW, axis=1)
    masked = blocks * row_mask[:, :, None] * col_mask[:, None, :]
    owned = lax.dynamic_slice_in_dim(
        jnp.argsort(dest, stable=True), source_index * slot_count, slot_count
    )
    slot_ids = my_dest * capacity + my_rank
    placing = (
        lax.broadcasted_iota(jnp.int32, (owner_count * capacity, slot_count), 0)
        == slot_ids[None, :]
    ).astype(F32)
    outgoing = jnp.einsum("ak,krc->arc", placing, masked, precision=highest, preferred_element_type=F32)
    arrived = lax.all_to_all(outgoing, "blk", split_axis=0, concat_axis=0, tiled=True)
    positions = owned // slot_count * capacity + ranks[owned]
    own_blocks = jnp.take(arrived, positions, axis=0)
    own_mask = (row_ids < orders[owned][:, None]).astype(F32)
    whitened = jnp.einsum(
        "jrq,jqc->jrc", inv_factor, own_blocks, precision=highest, preferred_element_type=F32
    )
    whitened_rows = (whitened * own_mask[:, :, None]).reshape(slot_count * max_order, column_width)
    factor = 1.0 / (block_count * max_order**0.5)
    partial_sums = lax.dot_general(
        lax.all_gather(whitened_rows, "tile", axis=1, tiled=True),
        whitened_rows,
        (((0,), (0,)), ((), ())),
        precision=highest,
        preferred_element_type=F32,
    )
    gram_tile = lax.psum_scatter(partial_sums, "blk", scatter_dimension=0, tiled=True)
    return gram_tile * factor


MINE, OWNER, ORDER, BITS, OTHERS, ORDER_OTHERS, BITS_OTHERS, ROW_AT = 0, 1, 2, 3, 4, 5, 6, 7
SHARES = (0.625, 1.0)


def round8(order):
    return (order + 7) // 8 * 8


def row_counts(all_rows):
    return [int(share * all_rows) // 8 * 8 for share in SHARES]


TOP_ROWS = 32
FACTOR_ROWS = 128 + 128 + 8 + TOP_ROWS


def iotas(rows):
    return tuple(lax.broadcasted_iota(jnp.int32, (rows, 128), axis) for axis in range(2))


def fold_factor(c, tiles, top, out):
    @pl.when(c == 0)
    def _():
        row, col = iotas(128)
        t11 = tiles[2]
        out[:128] = tiles[1]
        out[128:256] = jnp.where(row >= col, tiles[0], t11.T)
        out[256:264] = jnp.broadcast_to(jnp.sum(jnp.where(row == col, t11, 0.0), axis=0, keepdims=True), (8, 128))
        out[264:] = top[...]

    @pl.when(c == 1)
    def _():
        row, col = iotas(64)
        t22 = tiles[2]
        low = t22[64:]
        out[: 128 - TOP_ROWS] = tiles[0, TOP_ROWS:]
        out[128 - TOP_ROWS : 256 - TOP_ROWS] = tiles[1]
        out[256 - TOP_ROWS : 320 - TOP_ROWS] = jnp.where(
            col >= 64,
            pltpu.roll(low, 64, 1),
            jnp.where(row >= col, t22[:64], pltpu.roll(t22.T[64:], 64, 1)),
        )
        out[320 - TOP_ROWS :] = jnp.broadcast_to(
            jnp.sum(jnp.where(row + 64 == col, low, 0.0), axis=0, keepdims=True), (8, 128)
        )


def unfold_factor(first, second):
    row, col = iotas(128)
    both = first[128:256]
    f00 = jnp.where(row >= col, both, 0.0)
    f11 = jnp.where(row > col, both.T, jnp.where(row == col, first[256:257], 0.0))
    upper = jnp.concatenate(
        [jnp.concatenate([f00, jnp.zeros_like(f00)], axis=1), jnp.concatenate([first[:128], f11], axis=1)], axis=0
    )
    f20 = jnp.concatenate([first[264:], second[: 128 - TOP_ROWS]], axis=0)
    f21 = second[128 - TOP_ROWS : 256 - TOP_ROWS]
    fold, diagonal = second[256 - TOP_ROWS : 320 - TOP_ROWS], second[320 - TOP_ROWS : 321 - TOP_ROWS]
    turned = jnp.concatenate([fold, fold], axis=0).T[:64]
    row, col = iotas(64)
    f22 = jnp.concatenate(
        [
            jnp.where((row >= col) & (col < 64), fold, 0.0),
            jnp.where(
                col < 64,
                pltpu.roll(fold, 64, 1),
                jnp.where(row + 64 > col, pltpu.roll(turned, 64, 1), jnp.where(row + 64 == col, diagonal, 0.0)),
            ),
        ],
        axis=0,
    )
    return upper, jnp.concatenate([f20, f21, f22], axis=1)


def plan(
    dest_hbm, orders_hbm, pattern_hbm, blocks_ref, inv_ref, own_out, factor_out, table_ref, level_ref,
    dest_ref, orders_ref, pattern_ref, orders_at, pattern_at, weight_at, weight_ref, block_at, count, found_at, factor_at, tiles_at, top_at, small_sem, factor_sem, sem,
):
    s = lax.axis_index("blk")
    t = lax.axis_index("tile")
    y, c = t // 2, t % 2
    slots, max_order, width = blocks_ref.shape
    n_blk = count.shape[0]
    tiles = width // CTW

    def small_loads():
        for src, dst in (
            (orders_hbm, orders_at), (pattern_hbm, pattern_at), (dest_hbm, dest_ref), (orders_hbm, orders_ref), (pattern_hbm, pattern_ref),
        ):
            yield pltpu.make_async_copy(src, dst, small_sem)

    def factor_loads():
        for row in range(slots):
            for k, (ti, tj) in enumerate(((0, 0), (1, 0), (1, 1))):
                ri, rj = jnp.where(c == 0, ti, 2), jnp.where(c == 0, tj, k)
                yield pltpu.make_async_copy(
                    inv_ref.at[row, pl.ds(pl.multiple_of(ri * 128, 128), 128), pl.ds(pl.multiple_of(rj * 128, 128), 128)],
                    tiles_at.at[row, k],
                    factor_sem,
                )
            yield pltpu.make_async_copy(
                inv_ref.at[row, pl.ds(256, TOP_ROWS), pl.ds(0, 128)], top_at.at[row], factor_sem
            )

    for copy in small_loads():
        copy.start()
    for copy in factor_loads():
        copy.start()
    for copy in small_loads():
        copy.wait()
    ones = pattern_at[...]
    counts = [sum(ones[q * tiles + e : q * tiles + e + 1] for e in range(tiles)) for q in range(4)]
    rows = round8(orders_at[...])[None, :]
    weight_at[...] = jnp.concatenate([rows * (counts[q] + counts[q + 1] * 65536) for q in (0, 2)], axis=0)
    weights = pltpu.make_async_copy(weight_at, weight_ref, small_sem)
    weights.start()
    weights.wait()

    def scan_source(source, carry):
        found, most = carry
        base = source * slots
        for o in range(n_blk):
            count[o] = 0
            block_at[0, o] = 0
            block_at[1, o] = 0
        for i in range(slots):
            o = dest_ref[base + i]
            r = count[o]
            block_at[r, o] = i
            count[o] = r + 1
            mine = o == s
            found_at[jnp.where(mine, r, 2)] = found
            found = found + jnp.where(mine, 1, 0)

        def top(v):
            return jnp.maximum(jnp.maximum(v[0] & 65535, v[0] >> 16), jnp.maximum(v[1] & 65535, v[1] >> 16))

        here = source == s
        p, low, high = jnp.int32(0), jnp.int32(0), jnp.int32(0)
        for o in range(n_blk):
            on = count[o] > 0
            first, second = block_at[0, o], block_at[1, o]
            straight = low + weight_ref[0, base + second], high + weight_ref[1, base + first]
            crossed = low + weight_ref[0, base + first], high + weight_ref[1, base + second]
            flip = top(crossed) < top(straight)
            side = y ^ jnp.where(flip, 1, 0)
            factor_at[jnp.where(on & (s == o), source, n_blk)] = found_at[side]
            column = jnp.where(on & here, p, slots // 2)
            table_ref[MINE, column] = jnp.where(side == 0, first, second)
            table_ref[OTHERS, column] = jnp.where(side == 0, second, first)
            table_ref[OWNER, column] = jnp.int32(o)
            low = jnp.where(on, jnp.where(flip, crossed[0], straight[0]), low)
            high = jnp.where(on, jnp.where(flip, crossed[1], straight[1]), high)
            p = p + jnp.where(on, 1, 0)
        return found, jnp.maximum(most, top((low, high)))

    for source in range(n_blk):
        factor_at[source] = 0
    found_at[0] = 0
    found_at[1] = 0
    most = lax.fori_loop(0, n_blk, scan_source, (jnp.int32(0), jnp.int32(0)))[1]

    def own_loads():
        for p in range(slots // 2):
            yield pltpu.make_async_copy(blocks_ref.at[table_ref[MINE, p]], own_out.at[p], sem)

    for copy in own_loads():
        copy.start()

    level = jnp.int32(0)
    for rows in row_counts(slots // 2 * tiles * max_order)[:-1]:
        level = level + jnp.where(most + (max_order - 96) > rows, 1, 0)
    level_ref[0] = level

    for which, order_row, bits_row in ((MINE, ORDER, BITS), (OTHERS, ORDER_OTHERS, BITS_OTHERS)):
        for p in range(slots // 2):
            number = s * slots + table_ref[which, p]
            table_ref[order_row, p] = orders_ref[number]
            bits = jnp.int32(0)
            for ct in range(4 * tiles):
                bits = bits + jnp.where(pattern_ref[ct, number] != 0, 1 << ct, 0)
            table_ref[bits_row, p] = bits
    for k in range(2):
        at = jnp.int32(0)
        for p in range(slots // 2):
            rows, bits = round8(table_ref[ORDER, p]), table_ref[BITS, p]
            for e in range(tiles):
                table_ref[ROW_AT + k, p * tiles + e] = at
                at = at + jnp.where(tile_on(bits, (t ^ (2 + k)) * tiles + e), rows, 0)

    for copy in factor_loads():
        copy.wait()

    def fold(source, carry):
        row = factor_at[source]
        fold_factor(c, tiles_at.at[row], top_at.at[row], factor_out.at[source])
        return carry

    lax.fori_loop(0, n_blk, fold, 0)
    for copy in own_loads():
        copy.wait()


def tile_on(bits, tile):
    return ((bits >> tile) & 1) == 1


def pack_rows(table_ref, blocks_ref, packed, staged, sems):
    t = lax.axis_index("tile")
    slots, max_order, width = blocks_ref.shape
    tiles = width // CTW

    def loads():
        for p in range(slots // 2):
            yield pltpu.make_async_copy(blocks_ref.at[table_ref[OTHERS, p]], staged.at[p], sems.at[p])

    for copy in loads():
        copy.start()
    at = jnp.int32(0)
    for p, copy in enumerate(loads()):
        copy.wait()
        for e in range(tiles):
            on = tile_on(table_ref[BITS_OTHERS, p], t * tiles + e)

            @pl.when(on)
            def _(at=at, p=p, e=e):
                packed[pl.ds(pl.multiple_of(at, 8), max_order), :] = staged[p, :, e * CTW : (e + 1) * CTW]

            at = at + jnp.where(on, round8(table_ref[ORDER_OTHERS, p]), 0)


def split(x):
    high = x.astype(BF16)
    return high, (x - high.astype(F32)).astype(BF16)


def dot3(a, b):
    def dot(p, q):
        return jnp.dot(p, q, preferred_element_type=F32)

    return dot(a[0], b[0]) + (dot(a[0], b[1]) + dot(a[1], b[0]))


def whiten(tiles, table_ref, p, upper, lower, tile_ids):
    order = table_ref[ORDER, p]
    row_on = lax.broadcasted_iota(jnp.int32, tiles[0].shape, 0) < order
    parts = [
        jnp.where(row_on & tile_on(table_ref[BITS, p], ct), tile, 0.0) for tile, ct in zip(tiles, tile_ids)
    ]
    x = split(jnp.concatenate(parts, axis=1))
    w = jnp.concatenate([dot3(upper, (x[0][:256], x[1][:256])), dot3(lower, x)], axis=0)
    return jnp.where(lax.broadcasted_iota(jnp.int32, w.shape, 0) < order, w, 0.0)


def gram_own(
    table_ref, own_ref, core_ref, factor_ref, factor_other,
    upper_high, upper_low, lower_high, lower_low, w0_high, w0_low, w1t_high, w1t_low, g_out, w0t_high, w0t_low,
):
    t = lax.axis_index("tile")
    c = t % 2
    half, max_order, width = own_ref.shape
    for p in range(half):
        here, there = factor_ref[table_ref[OWNER, p]], factor_other[table_ref[OWNER, p]]
        upper, lower = unfold_factor(jnp.where(c == 0, here, there), jnp.where(c == 0, there, here))
        upper, lower = split(upper), split(lower)
        upper_high[p], upper_low[p] = upper
        lower_high[p], lower_low[p] = lower
        tiles = [ref[p, :, e * CTW : (e + 1) * CTW] for ref in (own_ref, core_ref) for e in range(2)]
        tile_ids = [(t ^ m) * 2 + e for m in range(2) for e in range(2)]
        w = whiten(tiles, table_ref, p, upper, lower, tile_ids)
        rows = pl.ds(p * max_order, max_order)
        w0_high[rows, :], w0_low[rows, :] = split(w[:, :width])
        w0t_high[:, rows], w0t_low[:, rows] = split(w[:, :width].T)
        w1t_high[:, rows], w1t_low[:, rows] = split(w[:, width:].T)
    w0 = w0_high[...], w0_low[...]
    g_out[:width] = dot3((w0t_high[...], w0t_low[...]), w0)
    g_out[width:] = dot3((w1t_high[...], w1t_low[...]), w0)


def across(table_ref, rows_ref, group, p, upper_high, upper_low, lower_high, lower_low, max_order):
    t = lax.axis_index("tile")
    last = rows_ref.shape[0] - max_order
    tiles = []
    for e in range(2):
        at = pl.multiple_of(jnp.minimum(table_ref[ROW_AT + group - 2, p * 2 + e], last), 8)
        tiles.append(rows_ref[pl.ds(at, max_order), :])
    upper, lower = (upper_high[p], upper_low[p]), (lower_high[p], lower_low[p])
    return whiten(tiles, table_ref, p, upper, lower, [(t ^ group) * 2 + e for e in range(2)])


def gram_y(
    table_ref, y_ref, upper_high, upper_low, lower_high, lower_low, w0_high, w0_low, w1t_high, w1t_low,
    w2_high, w2_low, g_out, w2t_high, w2t_low,
):
    depth, width = w0_high.shape
    half = upper_high.shape[0]
    max_order = depth // half
    for p in range(half):
        w = across(table_ref, y_ref, 2, p, upper_high, upper_low, lower_high, lower_low, max_order)
        rows = pl.ds(p * max_order, max_order)
        w2_high[rows, :], w2_low[rows, :] = split(w)
        w2t_high[:, rows], w2t_low[:, rows] = split(w.T)
    w2, w2t = (w2_high[...], w2_low[...]), (w2t_high[...], w2t_low[...])
    g_out[:width] = dot3(w2t, (w0_high[...], w0_low[...]))
    g_out[width : 2 * width] = dot3((w1t_high[...], w1t_low[...]), w2)
    g_out[2 * width :] = dot3(w2t, w2)


def gram_rest(
    table_ref, yc_ref, upper_high, upper_low, lower_high, lower_low, w0_high, w0_low, w2_high, w2_low, g_own, g_y, *refs
):
    firsts, seconds = refs[:4], refs[4:8]
    w3t_high, w3t_low, gram = refs[8:]
    s = lax.axis_index("blk")
    t = lax.axis_index("tile")
    depth, width = w0_high.shape
    half = upper_high.shape[0]
    max_order = depth // half
    for p in range(half):
        w = across(table_ref, yc_ref, 3, p, upper_high, upper_low, lower_high, lower_low, max_order)
        rows = pl.ds(p * max_order, max_order)
        w3t_high[:, rows], w3t_low[:, rows] = split(w.T)
    w3t = w3t_high[...], w3t_low[...]
    for m in range(2):
        gram[0, m] = g_own[m * width : (m + 1) * width]
    gram[0, 2] = g_y[:width]
    gram[0, 3] = dot3(w3t, (w0_high[...], w0_low[...]))
    gram[1, 0] = g_y[:width].T
    for m in range(1, 3):
        gram[1, m] = g_y[m * width : (m + 1) * width]
    gram[1, 3] = dot3(w3t, (w2_high[...], w2_low[...]))

    z, x = s // 2, s % 2

    for n in range(4):
        for a in range(2):
            for b in range(2):
                m, at = (z ^ n) ^ t, (x ^ a) * 128
                firsts[2 * a + b][n] = gram[b, m, pl.ds(pl.multiple_of(at, 8), XY_FIRST), :]
                seconds[n][a, b] = gram[b, m, pl.ds(pl.multiple_of(at + XY_FIRST, 8), 128 - XY_FIRST), :]


def paired_body(blocks, orders, pattern, dest, inv_factor):
    slots, max_order, width = blocks.shape
    n_blk = lax.axis_size("blk")
    half = slots // 2
    tiles = width // CTW
    blocks = pltpu.with_memory_space_constraint(blocks, pltpu.HBM)
    inv_factor = pltpu.with_memory_space_constraint(inv_factor, pltpu.HBM)
    dest, orders, pattern = (pltpu.with_memory_space_constraint(v, pltpu.HBM) for v in (dest, orders, pattern.T))
    hbm = pl.BlockSpec(memory_space=pltpu.HBM)
    smem = pl.BlockSpec(memory_space=pltpu.SMEM)
    vmem = pl.BlockSpec(memory_space=pltpu.VMEM)
    shape = jax.ShapeDtypeStruct
    own, factor_send, table, level = pl.pallas_call(
        plan,
        out_shape=(
            shape((half, max_order, width), F32),
            shape((n_blk, FACTOR_ROWS, CTW), F32),
            shape((9, half * tiles), jnp.int32),
            shape((1,), jnp.int32),
        ),
        in_specs=[hbm] * 5,
        out_specs=(vmem, vmem, smem, smem),
        scratch_shapes=[
            pltpu.SMEM(dest.shape, jnp.int32),
            pltpu.SMEM(orders.shape, jnp.int32),
            pltpu.SMEM(pattern.shape, jnp.int32),
            pltpu.VMEM(orders.shape, jnp.int32),
            pltpu.VMEM(pattern.shape, jnp.int32),
            pltpu.VMEM((2, dest.shape[0]), jnp.int32),
            pltpu.SMEM((2, dest.shape[0]), jnp.int32),
            pltpu.SMEM((2, n_blk), jnp.int32),
            pltpu.SMEM((n_blk,), jnp.int32),
            pltpu.SMEM((3,), jnp.int32),
            pltpu.SMEM((n_blk + 1,), jnp.int32),
            pltpu.VMEM((slots, 3, 128, 128), F32),
            pltpu.VMEM((slots, TOP_ROWS, 128), F32),
            pltpu.SemaphoreType.DMA,
            pltpu.SemaphoreType.DMA,
            pltpu.SemaphoreType.DMA,
        ],
        compiler_params=pltpu.CompilerParams(vmem_limit_bytes=VMEM_LIMIT),
        name="plan",
    )(dest, orders, pattern, blocks, inv_factor)
    rest = [functools.partial(paired_rest, rows) for rows in row_counts(half * tiles * max_order)]
    return lax.switch(level[0], rest, table, blocks, own, factor_send)


def paired_rest(row_count, table, blocks, own, factor_send):
    slots, max_order, width = blocks.shape
    n_blk = lax.axis_size("blk")
    n_tile = lax.axis_size("tile")
    half = slots // 2
    tiles = width // CTW
    axes = ("blk", "tile")

    def exchange(value, blk_bits, tile_bits):
        perm = [
            (b * n_tile + t, (b ^ blk_bits) * n_tile + (t ^ tile_bits)) for b in range(n_blk) for t in range(n_tile)
        ]
        return lax.ppermute(value, axes, perm)

    hbm = pl.BlockSpec(memory_space=pltpu.HBM)
    smem = pl.BlockSpec(memory_space=pltpu.SMEM)
    vmem = pl.BlockSpec(memory_space=pltpu.VMEM)
    shape = jax.ShapeDtypeStruct
    params = pltpu.CompilerParams(vmem_limit_bytes=VMEM_LIMIT)
    dma = pltpu.SemaphoreType.DMA

    y_rows = pl.pallas_call(
        pack_rows,
        out_shape=shape((row_count, CTW), F32),
        in_specs=[smem, hbm],
        out_specs=vmem,
        scratch_shapes=[pltpu.VMEM((half, max_order, width), F32), dma((half,))],
        compiler_params=params,
        name="pack_rows",
    )(table, blocks)
    y_recv = exchange(y_rows, 0, 2)
    factors = lax.all_to_all(factor_send, "blk", split_axis=0, concat_axis=0, tiled=True)
    core_recv = exchange(own, 0, 1)
    factors_other = exchange(factors, 0, 1)

    depth = half * max_order
    *factor, w0_high, w0_low, w1t_high, w1t_low, g_own = pl.pallas_call(
        gram_own,
        out_shape=(
            shape((half, 256, 256), BF16),
            shape((half, 256, 256), BF16),
            shape((half, 128, 384), BF16),
            shape((half, 128, 384), BF16),
            shape((depth, width), BF16),
            shape((depth, width), BF16),
            shape((width, depth), BF16),
            shape((width, depth), BF16),
            shape((2 * width, width), F32),
        ),
        in_specs=[smem] + [vmem] * 4,
        out_specs=(vmem,) * 9,
        scratch_shapes=[pltpu.VMEM((width, depth), BF16), pltpu.VMEM((width, depth), BF16)],
        compiler_params=params,
        name="gram_own",
    )(table, own, core_recv, factors, factors_other)

    y_recv, g_own = lax.optimization_barrier((y_recv, g_own))
    yc_recv = exchange(y_recv, 0, 1)
    w2_high, w2_low, g_y = pl.pallas_call(
        gram_y,
        out_shape=(shape((depth, width), BF16), shape((depth, width), BF16), shape((3 * width, width), F32)),
        in_specs=[smem] + [vmem] * 9,
        out_specs=(vmem,) * 3,
        scratch_shapes=[pltpu.VMEM((width, depth), BF16), pltpu.VMEM((width, depth), BF16)],
        compiler_params=params,
        name="gram_y",
    )(table, y_recv, *factor, w0_high, w0_low, w1t_high, w1t_low)
    first_shape, second_shape = (4, XY_FIRST, width), (2, 2, 128 - XY_FIRST, width)
    pieces = pl.pallas_call(
        gram_rest,
        out_shape=(shape(first_shape, F32),) * 4 + (shape(second_shape, F32),) * 4,
        in_specs=[smem] + [vmem] * 11,
        out_specs=(vmem,) * 8,
        scratch_shapes=[
            pltpu.VMEM((width, depth), BF16),
            pltpu.VMEM((width, depth), BF16),
            pltpu.VMEM((2, 4, width, width), F32),
        ],
        compiler_params=params,
        name="gram_rest",
    )(table, yc_recv, *factor, w0_high, w0_low, w2_high, w2_low, g_own, g_y)
    firsts, seconds = pieces[:4], pieces[4:]

    plane = [(a, b) for a in range(2) for b in range(2) if a or b]
    plane_in = [exchange(firsts[2 * a + b], a, 2 * b) for a, b in plane]
    line_in = [exchange(seconds[n], 2 * n, 0) for n in range(1, 4)]
    first = firsts[0] + sum(plane_in)
    second = seconds[0] + sum(line_in)
    line_in = [exchange(first[n], 2 * n, 0) for n in range(1, 4)]
    plane_in = [exchange(second[a, b], a, 2 * b) for a, b in plane]
    gram_tile = jnp.concatenate([first[0] + sum(line_in), second[0, 0] + sum(plane_in)], axis=0)
    return gram_tile * (1.0 / (n_blk * slots * max_order**0.5))


def solution(mesh):
    in_specs = (P("blk", None, "tile"), P(), P(), P(), P("blk", None, None))
    out_specs = P("blk", "tile")
    paired = mesh.shape["blk"] == 8 and mesh.shape["tile"] == 4
    body = paired_body if paired else general_body
    return jax.shard_map(body, mesh=mesh, in_specs=in_specs, out_specs=out_specs, check_vma=False)
```

```python
import functools

import jax
import jax.numpy as jnp
from jax import lax
from jax.experimental import pallas as pl
from jax.experimental.pallas import tpu as pltpu
from jax.sharding import PartitionSpec as P

CTW = 128
F32 = jnp.float32
BF16 = jnp.bfloat16
XY_FIRST = 80
VMEM_LIMIT = 24 << 20


def general_body(blocks, orders, pattern, dest, inv_factor):
    source_index = lax.axis_index("blk")
    owner_count = lax.axis_size("blk")
    tile_index = lax.axis_index("tile")
    slot_count, max_order, column_width = blocks.shape
    block_count = dest.shape[0]
    tiles_here = column_width // CTW
    highest = lax.Precision.HIGHEST
    capacity = (slot_count + owner_count - 1) // owner_count
    dest_grid = dest.reshape(owner_count, slot_count)
    earlier = lax.broadcasted_iota(jnp.int32, (slot_count, slot_count), 1) < lax.broadcasted_iota(
        jnp.int32, (slot_count, slot_count), 0
    )
    matching = dest_grid[:, :, None] == dest_grid[:, None, :]
    ranks = jnp.sum((matching & earlier[None]).astype(jnp.int32), axis=2).reshape(block_count)
    my_dest = lax.dynamic_slice_in_dim(dest, source_index * slot_count, slot_count)
    my_rank = lax.dynamic_slice_in_dim(ranks, source_index * slot_count, slot_count)
    my_orders = lax.dynamic_slice_in_dim(orders, source_index * slot_count, slot_count)
    my_tiles = lax.dynamic_slice(
        pattern, (source_index * slot_count, tile_index * tiles_here), (slot_count, tiles_here)
    )
    row_ids = lax.broadcasted_iota(jnp.int32, (slot_count, max_order), 1)
    row_mask = (row_ids < my_orders[:, None]).astype(F32)
    col_mask = jnp.repeat(my_tiles.astype(F32), CTW, axis=1)
    masked = blocks * row_mask[:, :, None] * col_mask[:, None, :]
    owned = lax.dynamic_slice_in_dim(
        jnp.argsort(dest, stable=True), source_index * slot_count, slot_count
    )
    slot_ids = my_dest * capacity + my_rank
    placing = (
        lax.broadcasted_iota(jnp.int32, (owner_count * capacity, slot_count), 0)
        == slot_ids[None, :]
    ).astype(F32)
    outgoing = jnp.einsum("ak,krc->arc", placing, masked, precision=highest, preferred_element_type=F32)
    arrived = lax.all_to_all(outgoing, "blk", split_axis=0, concat_axis=0, tiled=True)
    positions = owned // slot_count * capacity + ranks[owned]
    own_blocks = jnp.take(arrived, positions, axis=0)
    own_mask = (row_ids < orders[owned][:, None]).astype(F32)
    whitened = jnp.einsum(
        "jrq,jqc->jrc", inv_factor, own_blocks, precision=highest, preferred_element_type=F32
    )
    whitened_rows = (whitened * own_mask[:, :, None]).reshape(slot_count * max_order, column_width)
    factor = 1.0 / (block_count * max_order**0.5)
    partial_sums = lax.dot_general(
        lax.all_gather(whitened_rows, "tile", axis=1, tiled=True),
        whitened_rows,
        (((0,), (0,)), ((), ())),
        precision=highest,
        preferred_element_type=F32,
    )
    gram_tile = lax.psum_scatter(partial_sums, "blk", scatter_dimension=0, tiled=True)
    return gram_tile * factor


MINE, OWNER, ORDER, BITS, OTHERS, ORDER_OTHERS, BITS_OTHERS, ROW_AT = 0, 1, 2, 3, 4, 5, 6, 7
SHARES = (0.65625, 1.0)


def round8(order):
    return (order + 7) // 8 * 8


def row_counts(all_rows):
    return [int(share * all_rows) // 8 * 8 for share in SHARES]


TOP_ROWS = 32
FACTOR_ROWS = 128 + 128 + 8 + TOP_ROWS


def iotas(rows):
    return tuple(lax.broadcasted_iota(jnp.int32, (rows, 128), axis) for axis in range(2))


def fold_factor(c, tiles, top, out):
    @pl.when(c == 0)
    def _():
        row, col = iotas(128)
        t11 = tiles[2]
        out[:128] = tiles[1]
        out[128:256] = jnp.where(row >= col, tiles[0], t11.T)
        out[256:264] = jnp.broadcast_to(jnp.sum(jnp.where(row == col, t11, 0.0), axis=0, keepdims=True), (8, 128))
        out[264:] = top[...]

    @pl.when(c == 1)
    def _():
        row, col = iotas(64)
        t22 = tiles[2]
        low = t22[64:]
        out[: 128 - TOP_ROWS] = tiles[0, TOP_ROWS:]
        out[128 - TOP_ROWS : 256 - TOP_ROWS] = tiles[1]
        out[256 - TOP_ROWS : 320 - TOP_ROWS] = jnp.where(
            col >= 64,
            pltpu.roll(low, 64, 1),
            jnp.where(row >= col, t22[:64], pltpu.roll(t22.T[64:], 64, 1)),
        )
        out[320 - TOP_ROWS :] = jnp.broadcast_to(
            jnp.sum(jnp.where(row + 64 == col, low, 0.0), axis=0, keepdims=True), (8, 128)
        )


def unfold_factor(first, second):
    row, col = iotas(128)
    both = first[128:256]
    f00 = jnp.where(row >= col, both, 0.0)
    f11 = jnp.where(row > col, both.T, jnp.where(row == col, first[256:257], 0.0))
    upper = jnp.concatenate(
        [jnp.concatenate([f00, jnp.zeros_like(f00)], axis=1), jnp.concatenate([first[:128], f11], axis=1)], axis=0
    )
    f20 = jnp.concatenate([first[264:], second[: 128 - TOP_ROWS]], axis=0)
    f21 = second[128 - TOP_ROWS : 256 - TOP_ROWS]
    fold, diagonal = second[256 - TOP_ROWS : 320 - TOP_ROWS], second[320 - TOP_ROWS : 321 - TOP_ROWS]
    turned = jnp.concatenate([fold, fold], axis=0).T[:64]
    row, col = iotas(64)
    f22 = jnp.concatenate(
        [
            jnp.where((row >= col) & (col < 64), fold, 0.0),
            jnp.where(
                col < 64,
                pltpu.roll(fold, 64, 1),
                jnp.where(row + 64 > col, pltpu.roll(turned, 64, 1), jnp.where(row + 64 == col, diagonal, 0.0)),
            ),
        ],
        axis=0,
    )
    return upper, jnp.concatenate([f20, f21, f22], axis=1)


def plan(
    dest_hbm, orders_hbm, pattern_hbm, inv_ref, factor_out, table_ref, level_ref,
    dest_ref, orders_ref, pattern_ref, orders_at, pattern_at, weight_at, weight_ref, block_at, count, found_at, factor_at, tiles_at, top_at, small_sem, factor_sem,
):
    s = lax.axis_index("blk")
    t = lax.axis_index("tile")
    y, c = t // 2, t % 2
    slots, max_order, _ = inv_ref.shape
    n_blk = count.shape[0]
    tiles = pattern_ref.shape[0] // 4

    def small_loads():
        for src, dst in (
            (orders_hbm, orders_at), (pattern_hbm, pattern_at), (dest_hbm, dest_ref), (orders_hbm, orders_ref), (pattern_hbm, pattern_ref),
        ):
            yield pltpu.make_async_copy(src, dst, small_sem)

    def factor_loads():
        for row in range(slots):
            for k, (ti, tj) in enumerate(((0, 0), (1, 0), (1, 1))):
                ri, rj = jnp.where(c == 0, ti, 2), jnp.where(c == 0, tj, k)
                yield pltpu.make_async_copy(
                    inv_ref.at[row, pl.ds(pl.multiple_of(ri * 128, 128), 128), pl.ds(pl.multiple_of(rj * 128, 128), 128)],
                    tiles_at.at[row, k],
                    factor_sem,
                )
            yield pltpu.make_async_copy(
                inv_ref.at[row, pl.ds(256, TOP_ROWS), pl.ds(0, 128)], top_at.at[row], factor_sem
            )

    for copy in small_loads():
        copy.start()
    for copy in factor_loads():
        copy.start()
    for copy in small_loads():
        copy.wait()
    ones = pattern_at[...]
    counts = [sum(ones[q * tiles + e : q * tiles + e + 1] for e in range(tiles)) for q in range(4)]
    rows = round8(orders_at[...])[None, :]
    weight_at[...] = jnp.concatenate([rows * (counts[q] + counts[q + 1] * 65536) for q in (0, 2)], axis=0)
    weights = pltpu.make_async_copy(weight_at, weight_ref, small_sem)
    weights.start()

    def scan_blocks(source, found):
        for o in range(n_blk):
            count[source, o] = 0
            block_at[source, 0, o] = 0
            block_at[source, 1, o] = 0
        found_at[source, 0] = 0
        found_at[source, 1] = 0
        for i in range(slots):
            o = dest_ref[source * slots + i]
            r = count[source, o]
            block_at[source, r, o] = i
            count[source, o] = r + 1
            mine = o == s
            found_at[source, jnp.where(mine, r, 2)] = found
            found = found + jnp.where(mine, 1, 0)
        return found

    lax.fori_loop(0, n_blk, scan_blocks, jnp.int32(0))
    weights.wait()

    def scan_source(source, most):
        base = source * slots

        def top(v):
            return jnp.maximum(jnp.maximum(v[0] & 65535, v[0] >> 16), jnp.maximum(v[1] & 65535, v[1] >> 16))

        here = source == s
        p, low, high = jnp.int32(0), jnp.int32(0), jnp.int32(0)
        for o in range(n_blk):
            on = count[source, o] > 0
            first, second = block_at[source, 0, o], block_at[source, 1, o]
            straight = low + weight_ref[0, base + second], high + weight_ref[1, base + first]
            crossed = low + weight_ref[0, base + first], high + weight_ref[1, base + second]
            flip = top(crossed) < top(straight)
            side = y ^ jnp.where(flip, 1, 0)
            factor_at[jnp.where(on & (s == o), source, n_blk)] = found_at[source, side]
            column = jnp.where(on & here, p, slots // 2)
            table_ref[MINE, column] = jnp.where(side == 0, first, second)
            table_ref[OTHERS, column] = jnp.where(side == 0, second, first)
            table_ref[OWNER, column] = jnp.int32(o)
            low = jnp.where(on, jnp.where(flip, crossed[0], straight[0]), low)
            high = jnp.where(on, jnp.where(flip, crossed[1], straight[1]), high)
            p = p + jnp.where(on, 1, 0)
        return jnp.maximum(most, top((low, high)))

    for source in range(n_blk):
        factor_at[source] = 0
    most = lax.fori_loop(0, n_blk, scan_source, jnp.int32(0))

    level = jnp.int32(0)
    for rows in row_counts(slots // 2 * tiles * max_order)[:-1]:
        level = level + jnp.where(most + (max_order - 96) > rows, 1, 0)
    level_ref[0] = level

    for which, order_row, bits_row in ((MINE, ORDER, BITS), (OTHERS, ORDER_OTHERS, BITS_OTHERS)):
        for p in range(slots // 2):
            number = s * slots + table_ref[which, p]
            table_ref[order_row, p] = orders_ref[number]
            bits = jnp.int32(0)
            for ct in range(4 * tiles):
                bits = bits + jnp.where(pattern_ref[ct, number] != 0, 1 << ct, 0)
            table_ref[bits_row, p] = bits
    for k in range(2):
        at = jnp.int32(0)
        for p in range(slots // 2):
            rows, bits = round8(table_ref[ORDER, p]), table_ref[BITS, p]
            for e in range(tiles):
                table_ref[ROW_AT + k, p * tiles + e] = at
                at = at + jnp.where(tile_on(bits, (t ^ (2 + k)) * tiles + e), rows, 0)

    for copy in factor_loads():
        copy.wait()

    def fold(source, carry):
        row = factor_at[source]
        fold_factor(c, tiles_at.at[row], top_at.at[row], factor_out.at[source])
        return carry

    lax.fori_loop(0, n_blk, fold, 0)


def tile_on(bits, tile):
    return ((bits >> tile) & 1) == 1


def pack_rows(table_ref, blocks_ref, packed, staged, sems):
    t = lax.axis_index("tile")
    slots, max_order, width = blocks_ref.shape
    tiles = width // CTW

    def loads():
        for p in range(slots // 2):
            yield pltpu.make_async_copy(blocks_ref.at[table_ref[OTHERS, p]], staged.at[p], sems.at[p])

    for copy in loads():
        copy.start()
    at = jnp.int32(0)
    for p, copy in enumerate(loads()):
        copy.wait()
        for e in range(tiles):
            on = tile_on(table_ref[BITS_OTHERS, p], t * tiles + e)

            @pl.when(on)
            def _(at=at, p=p, e=e):
                packed[pl.ds(pl.multiple_of(at, 8), max_order), :] = staged[p, :, e * CTW : (e + 1) * CTW]

            at = at + jnp.where(on, round8(table_ref[ORDER_OTHERS, p]), 0)


def load_columns(table_ref, blocks_ref, core_ref, x_out, sem):
    def loads():
        for p in range(x_out.shape[0]):
            for m, ref in enumerate((blocks_ref, core_ref)):
                yield pltpu.make_async_copy(ref.at[table_ref[MINE, p]], x_out.at[p, m], sem)

    for copy in loads():
        copy.start()
    for copy in loads():
        copy.wait()


def split(x):
    high = x.astype(BF16)
    return high, (x - high.astype(F32)).astype(BF16)


def dot3(a, b):
    def dot(p, q):
        return jnp.dot(p, q, preferred_element_type=F32)

    return dot(a[0], b[0]) + (dot(a[0], b[1]) + dot(a[1], b[0]))


def whiten(tiles, table_ref, p, upper, lower, tile_ids):
    order = table_ref[ORDER, p]
    row_on = lax.broadcasted_iota(jnp.int32, tiles[0].shape, 0) < order
    parts = [
        jnp.where(row_on & tile_on(table_ref[BITS, p], ct), tile, 0.0) for tile, ct in zip(tiles, tile_ids)
    ]
    x = split(jnp.concatenate(parts, axis=1))
    w = jnp.concatenate([dot3(upper, (x[0][:256], x[1][:256])), dot3(lower, x)], axis=0)
    return jnp.where(lax.broadcasted_iota(jnp.int32, w.shape, 0) < order, w, 0.0)


def gram_own(
    table_ref, x_ref, factor_ref, factor_other,
    upper_high, upper_low, lower_high, lower_low, w0_high, w0_low, w1t_high, w1t_low, g_out, w0t_high, w0t_low,
):
    t = lax.axis_index("tile")
    c = t % 2
    half, _, max_order, width = x_ref.shape
    for p in range(half):
        here, there = factor_ref[table_ref[OWNER, p]], factor_other[table_ref[OWNER, p]]
        upper, lower = unfold_factor(jnp.where(c == 0, here, there), jnp.where(c == 0, there, here))
        upper, lower = split(upper), split(lower)
        upper_high[p], upper_low[p] = upper
        lower_high[p], lower_low[p] = lower
        tiles = [x_ref[p, m, :, e * CTW : (e + 1) * CTW] for m in range(2) for e in range(2)]
        tile_ids = [(t ^ m) * 2 + e for m in range(2) for e in range(2)]
        w = whiten(tiles, table_ref, p, upper, lower, tile_ids)
        rows = pl.ds(p * max_order, max_order)
        w0_high[rows, :], w0_low[rows, :] = split(w[:, :width])
        w0t_high[:, rows], w0t_low[:, rows] = split(w[:, :width].T)
        w1t_high[:, rows], w1t_low[:, rows] = split(w[:, width:].T)
    w0 = w0_high[...], w0_low[...]
    g_out[:width] = dot3((w0t_high[...], w0t_low[...]), w0)
    g_out[width:] = dot3((w1t_high[...], w1t_low[...]), w0)


def across(table_ref, rows_ref, group, p, upper_high, upper_low, lower_high, lower_low, max_order):
    t = lax.axis_index("tile")
    last = rows_ref.shape[0] - max_order
    tiles = []
    for e in range(2):
        at = pl.multiple_of(jnp.minimum(table_ref[ROW_AT + group - 2, p * 2 + e], last), 8)
        tiles.append(rows_ref[pl.ds(at, max_order), :])
    upper, lower = (upper_high[p], upper_low[p]), (lower_high[p], lower_low[p])
    return whiten(tiles, table_ref, p, upper, lower, [(t ^ group) * 2 + e for e in range(2)])


def gram_y(
    table_ref, y_ref, upper_high, upper_low, lower_high, lower_low, w0_high, w0_low, w1t_high, w1t_low,
    w2_high, w2_low, g_out, w2t_high, w2t_low,
):
    depth, width = w0_high.shape
    half = upper_high.shape[0]
    max_order = depth // half
    for p in range(half):
        w = across(table_ref, y_ref, 2, p, upper_high, upper_low, lower_high, lower_low, max_order)
        rows = pl.ds(p * max_order, max_order)
        w2_high[rows, :], w2_low[rows, :] = split(w)
        w2t_high[:, rows], w2t_low[:, rows] = split(w.T)
    w2, w2t = (w2_high[...], w2_low[...]), (w2t_high[...], w2t_low[...])
    g_out[:width] = dot3(w2t, (w0_high[...], w0_low[...]))
    g_out[width : 2 * width] = dot3((w1t_high[...], w1t_low[...]), w2)
    g_out[2 * width :] = dot3(w2t, w2)


def gram_rest(
    table_ref, yc_ref, upper_high, upper_low, lower_high, lower_low, w0_high, w0_low, w2_high, w2_low, g_own, g_y, *refs
):
    firsts, seconds = refs[:4], refs[4:8]
    w3t_high, w3t_low, gram = refs[8:]
    s = lax.axis_index("blk")
    t = lax.axis_index("tile")
    depth, width = w0_high.shape
    half = upper_high.shape[0]
    max_order = depth // half
    for p in range(half):
        w = across(table_ref, yc_ref, 3, p, upper_high, upper_low, lower_high, lower_low, max_order)
        rows = pl.ds(p * max_order, max_order)
        w3t_high[:, rows], w3t_low[:, rows] = split(w.T)
    w3t = w3t_high[...], w3t_low[...]
    for m in range(2):
        gram[0, m] = g_own[m * width : (m + 1) * width]
    gram[0, 2] = g_y[:width]
    gram[0, 3] = dot3(w3t, (w0_high[...], w0_low[...]))
    gram[1, 0] = g_y[:width].T
    for m in range(1, 3):
        gram[1, m] = g_y[m * width : (m + 1) * width]
    gram[1, 3] = dot3(w3t, (w2_high[...], w2_low[...]))

    z, x = s // 2, s % 2

    for n in range(4):
        for a in range(2):
            for b in range(2):
                m, at = (z ^ n) ^ t, (x ^ a) * 128
                firsts[2 * a + b][n] = gram[b, m, pl.ds(pl.multiple_of(at, 8), XY_FIRST), :]
                seconds[n][a, b] = gram[b, m, pl.ds(pl.multiple_of(at + XY_FIRST, 8), 128 - XY_FIRST), :]


def paired_body(blocks, orders, pattern, dest, inv_factor):
    slots, max_order, width = blocks.shape
    n_blk = lax.axis_size("blk")
    half = slots // 2
    tiles = width // CTW
    blocks = pltpu.with_memory_space_constraint(blocks, pltpu.HBM)
    inv_factor = pltpu.with_memory_space_constraint(inv_factor, pltpu.HBM)
    dest, orders, pattern = (pltpu.with_memory_space_constraint(v, pltpu.HBM) for v in (dest, orders, pattern.T))
    hbm = pl.BlockSpec(memory_space=pltpu.HBM)
    smem = pl.BlockSpec(memory_space=pltpu.SMEM)
    vmem = pl.BlockSpec(memory_space=pltpu.VMEM)
    shape = jax.ShapeDtypeStruct
    factor_send, table, level = pl.pallas_call(
        plan,
        out_shape=(
            shape((n_blk, FACTOR_ROWS, CTW), F32),
            shape((9, half * tiles), jnp.int32),
            shape((1,), jnp.int32),
        ),
        in_specs=[hbm] * 4,
        out_specs=(vmem, smem, smem),
        scratch_shapes=[
            pltpu.SMEM(dest.shape, jnp.int32),
            pltpu.SMEM(orders.shape, jnp.int32),
            pltpu.SMEM(pattern.shape, jnp.int32),
            pltpu.VMEM(orders.shape, jnp.int32),
            pltpu.VMEM(pattern.shape, jnp.int32),
            pltpu.VMEM((2, dest.shape[0]), jnp.int32),
            pltpu.SMEM((2, dest.shape[0]), jnp.int32),
            pltpu.SMEM((n_blk, 2, n_blk), jnp.int32),
            pltpu.SMEM((n_blk, n_blk), jnp.int32),
            pltpu.SMEM((n_blk, 3), jnp.int32),
            pltpu.SMEM((n_blk + 1,), jnp.int32),
            pltpu.VMEM((slots, 3, 128, 128), F32),
            pltpu.VMEM((slots, TOP_ROWS, 128), F32),
            pltpu.SemaphoreType.DMA,
            pltpu.SemaphoreType.DMA,
        ],
        compiler_params=pltpu.CompilerParams(vmem_limit_bytes=VMEM_LIMIT),
        name="plan",
    )(dest, orders, pattern, inv_factor)
    rest = [functools.partial(paired_rest, rows) for rows in row_counts(half * tiles * max_order)]
    return lax.switch(level[0], rest, table, blocks, factor_send)


def paired_rest(row_count, table, blocks, factor_send):
    slots, max_order, width = blocks.shape
    n_blk = lax.axis_size("blk")
    n_tile = lax.axis_size("tile")
    half = slots // 2
    tiles = width // CTW
    axes = ("blk", "tile")

    def exchange(value, blk_bits, tile_bits):
        perm = [
            (b * n_tile + t, (b ^ blk_bits) * n_tile + (t ^ tile_bits)) for b in range(n_blk) for t in range(n_tile)
        ]
        return lax.ppermute(value, axes, perm)

    hbm = pl.BlockSpec(memory_space=pltpu.HBM)
    smem = pl.BlockSpec(memory_space=pltpu.SMEM)
    vmem = pl.BlockSpec(memory_space=pltpu.VMEM)
    shape = jax.ShapeDtypeStruct
    params = pltpu.CompilerParams(vmem_limit_bytes=VMEM_LIMIT)
    dma = pltpu.SemaphoreType.DMA

    y_rows = pl.pallas_call(
        pack_rows,
        out_shape=shape((row_count, CTW), F32),
        in_specs=[smem, hbm],
        out_specs=vmem,
        scratch_shapes=[pltpu.VMEM((half, max_order, width), F32), dma((half,))],
        compiler_params=params,
        name="pack_rows",
    )(table, blocks)
    y_recv = exchange(y_rows, 0, 2)
    factors = lax.all_to_all(factor_send, "blk", split_axis=0, concat_axis=0, tiled=True)
    core_blocks = exchange(blocks, 0, 1)
    factors_other = exchange(factors, 0, 1)
    own_table, _ = lax.optimization_barrier((table, factors))
    columns = pl.pallas_call(
        load_columns,
        out_shape=shape((half, 2, max_order, width), F32),
        in_specs=[smem, hbm, hbm],
        out_specs=vmem,
        scratch_shapes=[dma],
        compiler_params=params,
        name="load_columns",
    )(own_table, blocks, core_blocks)

    depth = half * max_order
    *factor, w0_high, w0_low, w1t_high, w1t_low, g_own = pl.pallas_call(
        gram_own,
        out_shape=(
            shape((half, 256, 256), BF16),
            shape((half, 256, 256), BF16),
            shape((half, 128, 384), BF16),
            shape((half, 128, 384), BF16),
            shape((depth, width), BF16),
            shape((depth, width), BF16),
            shape((width, depth), BF16),
            shape((width, depth), BF16),
            shape((2 * width, width), F32),
        ),
        in_specs=[smem] + [vmem] * 3,
        out_specs=(vmem,) * 9,
        scratch_shapes=[pltpu.VMEM((width, depth), BF16), pltpu.VMEM((width, depth), BF16)],
        compiler_params=params,
        name="gram_own",
    )(table, columns, factors, factors_other)

    y_recv, g_own = lax.optimization_barrier((y_recv, g_own))
    yc_recv = exchange(y_recv, 0, 1)
    w2_high, w2_low, g_y = pl.pallas_call(
        gram_y,
        out_shape=(shape((depth, width), BF16), shape((depth, width), BF16), shape((3 * width, width), F32)),
        in_specs=[smem] + [vmem] * 9,
        out_specs=(vmem,) * 3,
        scratch_shapes=[pltpu.VMEM((width, depth), BF16), pltpu.VMEM((width, depth), BF16)],
        compiler_params=params,
        name="gram_y",
    )(table, y_recv, *factor, w0_high, w0_low, w1t_high, w1t_low)
    first_shape, second_shape = (4, XY_FIRST, width), (2, 2, 128 - XY_FIRST, width)
    pieces = pl.pallas_call(
        gram_rest,
        out_shape=(shape(first_shape, F32),) * 4 + (shape(second_shape, F32),) * 4,
        in_specs=[smem] + [vmem] * 11,
        out_specs=(vmem,) * 8,
        scratch_shapes=[
            pltpu.VMEM((width, depth), BF16),
            pltpu.VMEM((width, depth), BF16),
            pltpu.VMEM((2, 4, width, width), F32),
        ],
        compiler_params=params,
        name="gram_rest",
    )(table, yc_recv, *factor, w0_high, w0_low, w2_high, w2_low, g_own, g_y)
    firsts, seconds = pieces[:4], pieces[4:]

    plane = [(a, b) for a in range(2) for b in range(2) if a or b]
    plane_in = [exchange(firsts[2 * a + b], a, 2 * b) for a, b in plane]
    line_in = [exchange(seconds[n], 2 * n, 0) for n in range(1, 4)]
    first = firsts[0] + sum(plane_in)
    second = seconds[0] + sum(line_in)
    line_in = [exchange(first[n], 2 * n, 0) for n in range(1, 4)]
    plane_in = [exchange(second[a, b], a, 2 * b) for a, b in plane]
    gram_tile = jnp.concatenate([first[0] + sum(line_in), second[0, 0] + sum(plane_in)], axis=0)
    return gram_tile * (1.0 / (n_blk * slots * max_order**0.5))


def solution(mesh):
    in_specs = (P("blk", None, "tile"), P(), P(), P(), P("blk", None, None))
    out_specs = P("blk", "tile")
    paired = mesh.shape["blk"] == 8 and mesh.shape["tile"] == 4
    body = paired_body if paired else general_body
    return jax.shard_map(body, mesh=mesh, in_specs=in_specs, out_specs=out_specs, check_vma=False)
```

```python
import functools

import jax
import jax.numpy as jnp
from jax import lax
from jax.experimental import pallas as pl
from jax.experimental.pallas import tpu as pltpu
from jax.sharding import PartitionSpec as P

CTW = 128
F32 = jnp.float32
BF16 = jnp.bfloat16
XY_FIRST = 80
VMEM_LIMIT = 24 << 20


def general_body(blocks, orders, pattern, dest, inv_factor):
    source_index = lax.axis_index("blk")
    owner_count = lax.axis_size("blk")
    tile_index = lax.axis_index("tile")
    slot_count, max_order, column_width = blocks.shape
    block_count = dest.shape[0]
    tiles_here = column_width // CTW
    highest = lax.Precision.HIGHEST
    capacity = (slot_count + owner_count - 1) // owner_count
    dest_grid = dest.reshape(owner_count, slot_count)
    earlier = lax.broadcasted_iota(jnp.int32, (slot_count, slot_count), 1) < lax.broadcasted_iota(
        jnp.int32, (slot_count, slot_count), 0
    )
    matching = dest_grid[:, :, None] == dest_grid[:, None, :]
    ranks = jnp.sum((matching & earlier[None]).astype(jnp.int32), axis=2).reshape(block_count)
    my_dest = lax.dynamic_slice_in_dim(dest, source_index * slot_count, slot_count)
    my_rank = lax.dynamic_slice_in_dim(ranks, source_index * slot_count, slot_count)
    my_orders = lax.dynamic_slice_in_dim(orders, source_index * slot_count, slot_count)
    my_tiles = lax.dynamic_slice(
        pattern, (source_index * slot_count, tile_index * tiles_here), (slot_count, tiles_here)
    )
    row_ids = lax.broadcasted_iota(jnp.int32, (slot_count, max_order), 1)
    row_mask = (row_ids < my_orders[:, None]).astype(F32)
    col_mask = jnp.repeat(my_tiles.astype(F32), CTW, axis=1)
    masked = blocks * row_mask[:, :, None] * col_mask[:, None, :]
    owned = lax.dynamic_slice_in_dim(
        jnp.argsort(dest, stable=True), source_index * slot_count, slot_count
    )
    slot_ids = my_dest * capacity + my_rank
    placing = (
        lax.broadcasted_iota(jnp.int32, (owner_count * capacity, slot_count), 0)
        == slot_ids[None, :]
    ).astype(F32)
    outgoing = jnp.einsum("ak,krc->arc", placing, masked, precision=highest, preferred_element_type=F32)
    arrived = lax.all_to_all(outgoing, "blk", split_axis=0, concat_axis=0, tiled=True)
    positions = owned // slot_count * capacity + ranks[owned]
    own_blocks = jnp.take(arrived, positions, axis=0)
    own_mask = (row_ids < orders[owned][:, None]).astype(F32)
    whitened = jnp.einsum(
        "jrq,jqc->jrc", inv_factor, own_blocks, precision=highest, preferred_element_type=F32
    )
    whitened_rows = (whitened * own_mask[:, :, None]).reshape(slot_count * max_order, column_width)
    factor = 1.0 / (block_count * max_order**0.5)
    partial_sums = lax.dot_general(
        lax.all_gather(whitened_rows, "tile", axis=1, tiled=True),
        whitened_rows,
        (((0,), (0,)), ((), ())),
        precision=highest,
        preferred_element_type=F32,
    )
    gram_tile = lax.psum_scatter(partial_sums, "blk", scatter_dimension=0, tiled=True)
    return gram_tile * factor


MINE, OWNER, ORDER, BITS, OTHERS, ORDER_OTHERS, BITS_OTHERS, ROW_AT = 0, 1, 2, 3, 4, 5, 6, 7
SHARES = (0.625, 1.0)
CHUNK = 64


def round8(order):
    return (order + 7) // 8 * 8


def row_counts(all_rows):
    return [int(share * all_rows) // 8 * 8 for share in SHARES]


TOP_ROWS = 32
FACTOR_ROWS = 128 + 128 + 8 + TOP_ROWS


def iotas(rows):
    return tuple(lax.broadcasted_iota(jnp.int32, (rows, 128), axis) for axis in range(2))


def fold_factor(c, tiles, top, out):
    @pl.when(c == 0)
    def _():
        row, col = iotas(128)
        t11 = tiles[2]
        out[:128] = tiles[1]
        out[128:256] = jnp.where(row >= col, tiles[0], t11.T)
        out[256:264] = jnp.broadcast_to(jnp.sum(jnp.where(row == col, t11, 0.0), axis=0, keepdims=True), (8, 128))
        out[264:] = top[...]

    @pl.when(c == 1)
    def _():
        row, col = iotas(64)
        t22 = tiles[2]
        low = t22[64:]
        out[: 128 - TOP_ROWS] = tiles[0, TOP_ROWS:]
        out[128 - TOP_ROWS : 256 - TOP_ROWS] = tiles[1]
        out[256 - TOP_ROWS : 320 - TOP_ROWS] = jnp.where(
            col >= 64,
            pltpu.roll(low, 64, 1),
            jnp.where(row >= col, t22[:64], pltpu.roll(t22.T[64:], 64, 1)),
        )
        out[320 - TOP_ROWS :] = jnp.broadcast_to(
            jnp.sum(jnp.where(row + 64 == col, low, 0.0), axis=0, keepdims=True), (8, 128)
        )


def unfold_factor(first, second):
    row, col = iotas(128)
    both = first[128:256]
    f00 = jnp.where(row >= col, both, 0.0)
    f11 = jnp.where(row > col, both.T, jnp.where(row == col, first[256:257], 0.0))
    upper = jnp.concatenate(
        [jnp.concatenate([f00, jnp.zeros_like(f00)], axis=1), jnp.concatenate([first[:128], f11], axis=1)], axis=0
    )
    f20 = jnp.concatenate([first[264:], second[: 128 - TOP_ROWS]], axis=0)
    f21 = second[128 - TOP_ROWS : 256 - TOP_ROWS]
    fold, diagonal = second[256 - TOP_ROWS : 320 - TOP_ROWS], second[320 - TOP_ROWS : 321 - TOP_ROWS]
    turned = jnp.concatenate([fold, fold], axis=0).T[:64]
    row, col = iotas(64)
    f22 = jnp.concatenate(
        [
            jnp.where((row >= col) & (col < 64), fold, 0.0),
            jnp.where(
                col < 64,
                pltpu.roll(fold, 64, 1),
                jnp.where(row + 64 > col, pltpu.roll(turned, 64, 1), jnp.where(row + 64 == col, diagonal, 0.0)),
            ),
        ],
        axis=0,
    )
    return upper, jnp.concatenate([f20, f21, f22], axis=1)


def plan(
    dest_hbm, orders_hbm, pattern_hbm, inv_ref, factor_out, table_ref, level_ref,
    dest_ref, orders_ref, pattern_ref, orders_at, pattern_at, weight_at, weight_ref, block_at, count, found_at, factor_at, tiles_at, top_at, small_sem, factor_sem,
):
    s = lax.axis_index("blk")
    t = lax.axis_index("tile")
    y, c = t // 2, t % 2
    slots, max_order, _ = inv_ref.shape
    n_blk = count.shape[0]
    tiles = pattern_ref.shape[0] // 4

    def small_loads():
        for src, dst in (
            (orders_hbm, orders_at), (pattern_hbm, pattern_at), (dest_hbm, dest_ref), (orders_hbm, orders_ref), (pattern_hbm, pattern_ref),
        ):
            yield pltpu.make_async_copy(src, dst, small_sem)

    def factor_loads():
        for row in range(slots):
            for k, (ti, tj) in enumerate(((0, 0), (1, 0), (1, 1))):
                ri, rj = jnp.where(c == 0, ti, 2), jnp.where(c == 0, tj, k)
                yield pltpu.make_async_copy(
                    inv_ref.at[row, pl.ds(pl.multiple_of(ri * 128, 128), 128), pl.ds(pl.multiple_of(rj * 128, 128), 128)],
                    tiles_at.at[row, k],
                    factor_sem,
                )
            yield pltpu.make_async_copy(
                inv_ref.at[row, pl.ds(256, TOP_ROWS), pl.ds(0, 128)], top_at.at[row], factor_sem
            )

    for copy in small_loads():
        copy.start()
    for copy in factor_loads():
        copy.start()
    for copy in small_loads():
        copy.wait()
    ones = pattern_at[...]
    counts = [sum(ones[q * tiles + e : q * tiles + e + 1] for e in range(tiles)) for q in range(4)]
    rows = round8(orders_at[...])[None, :]
    weight_at[...] = jnp.concatenate([rows * (counts[q] + counts[q + 1] * 65536) for q in (0, 2)], axis=0)
    weights = pltpu.make_async_copy(weight_at, weight_ref, small_sem)
    weights.start()

    def scan_blocks(source, found):
        for o in range(n_blk):
            count[source, o] = 0
            block_at[source, 0, o] = 0
            block_at[source, 1, o] = 0
        found_at[source, 0] = 0
        found_at[source, 1] = 0
        for i in range(slots):
            o = dest_ref[source * slots + i]
            r = count[source, o]
            block_at[source, r, o] = i
            count[source, o] = r + 1
            mine = o == s
            found_at[source, jnp.where(mine, r, 2)] = found
            found = found + jnp.where(mine, 1, 0)
        return found

    lax.fori_loop(0, n_blk, scan_blocks, jnp.int32(0))
    weights.wait()

    def scan_source(source, most):
        base = source * slots

        def top(v):
            return jnp.maximum(jnp.maximum(v[0] & 65535, v[0] >> 16), jnp.maximum(v[1] & 65535, v[1] >> 16))

        here = source == s
        p, low, high = jnp.int32(0), jnp.int32(0), jnp.int32(0)
        for o in range(n_blk):
            on = count[source, o] > 0
            first, second = block_at[source, 0, o], block_at[source, 1, o]
            straight = low + weight_ref[0, base + second], high + weight_ref[1, base + first]
            crossed = low + weight_ref[0, base + first], high + weight_ref[1, base + second]
            flip = top(crossed) < top(straight)
            side = y ^ jnp.where(flip, 1, 0)
            factor_at[jnp.where(on & (s == o), source, n_blk)] = found_at[source, side]
            column = jnp.where(on & here, p, slots // 2)
            table_ref[MINE, column] = jnp.where(side == 0, first, second)
            table_ref[OTHERS, column] = jnp.where(side == 0, second, first)
            table_ref[OWNER, column] = jnp.int32(o)
            low = jnp.where(on, jnp.where(flip, crossed[0], straight[0]), low)
            high = jnp.where(on, jnp.where(flip, crossed[1], straight[1]), high)
            p = p + jnp.where(on, 1, 0)
        return jnp.maximum(most, top((low, high)))

    for source in range(n_blk):
        factor_at[source] = 0
    most = lax.fori_loop(0, n_blk, scan_source, jnp.int32(0))

    level = jnp.int32(0)
    for rows in row_counts(slots // 2 * tiles * max_order)[:-1]:
        level = level + jnp.where(most + (CHUNK - 8) > rows, 1, 0)
    level_ref[0] = level

    for which, order_row, bits_row in ((MINE, ORDER, BITS), (OTHERS, ORDER_OTHERS, BITS_OTHERS)):
        for p in range(slots // 2):
            number = s * slots + table_ref[which, p]
            table_ref[order_row, p] = orders_ref[number]
            bits = jnp.int32(0)
            for ct in range(4 * tiles):
                bits = bits + jnp.where(pattern_ref[ct, number] != 0, 1 << ct, 0)
            table_ref[bits_row, p] = bits
    for k in range(2):
        at = jnp.int32(0)
        for p in range(slots // 2):
            rows, bits = round8(table_ref[ORDER, p]), table_ref[BITS, p]
            for e in range(tiles):
                table_ref[ROW_AT + k, p * tiles + e] = at
                at = at + jnp.where(tile_on(bits, (t ^ (2 + k)) * tiles + e), rows, 0)

    for copy in factor_loads():
        copy.wait()

    def fold(source, carry):
        row = factor_at[source]
        fold_factor(c, tiles_at.at[row], top_at.at[row], factor_out.at[source])
        return carry

    lax.fori_loop(0, n_blk, fold, 0)


def tile_on(bits, tile):
    return ((bits >> tile) & 1) == 1


def pack_rows(table_ref, blocks_ref, packed, staged, sems):
    t = lax.axis_index("tile")
    slots, max_order, width = blocks_ref.shape
    tiles = width // CTW

    def loads():
        for p in range(slots // 2):
            yield pltpu.make_async_copy(blocks_ref.at[table_ref[OTHERS, p]], staged.at[p], sems.at[p])

    for copy in loads():
        copy.start()
    at = jnp.int32(0)
    for p, copy in enumerate(loads()):
        copy.wait()
        for e in range(tiles):
            on = tile_on(table_ref[BITS_OTHERS, p], t * tiles + e)

            def write(k, carry, at=at, p=p, e=e):
                packed[pl.ds(pl.multiple_of(at + k * CHUNK, 8), CHUNK), :] = staged[
                    p, pl.ds(pl.multiple_of(k * CHUNK, CHUNK), CHUNK), e * CTW : (e + 1) * CTW
                ]
                return carry

            chunks = (table_ref[ORDER_OTHERS, p] + CHUNK - 1) // CHUNK
            lax.fori_loop(0, jnp.where(on, chunks, 0), write, 0)
            at = at + jnp.where(on, round8(table_ref[ORDER_OTHERS, p]), 0)


def load_columns(table_ref, blocks_ref, core_ref, x_out, sem):
    def loads():
        for p in range(x_out.shape[0]):
            for m, ref in enumerate((blocks_ref, core_ref)):
                yield pltpu.make_async_copy(ref.at[table_ref[MINE, p]], x_out.at[p, m], sem)

    for copy in loads():
        copy.start()
    for copy in loads():
        copy.wait()


def split(x):
    high = x.astype(BF16)
    return high, (x - high.astype(F32)).astype(BF16)


def dot3(a, b):
    def dot(p, q):
        return jnp.dot(p, q, preferred_element_type=F32)

    return dot(a[0], b[0]) + (dot(a[0], b[1]) + dot(a[1], b[0]))


def whiten(tiles, table_ref, p, upper, lower, tile_ids):
    order = table_ref[ORDER, p]
    row_on = lax.broadcasted_iota(jnp.int32, tiles[0].shape, 0) < order
    parts = [
        jnp.where(row_on & tile_on(table_ref[BITS, p], ct), tile, 0.0) for tile, ct in zip(tiles, tile_ids)
    ]
    x = split(jnp.concatenate(parts, axis=1))
    w = jnp.concatenate([dot3(upper, (x[0][:256], x[1][:256])), dot3(lower, x)], axis=0)
    return jnp.where(lax.broadcasted_iota(jnp.int32, w.shape, 0) < order, w, 0.0)


def gram_own(
    table_ref, x_ref, factor_ref, factor_other,
    upper_high, upper_low, lower_high, lower_low, w0_high, w0_low, w1t_high, w1t_low, g_out, w0t_high, w0t_low,
):
    t = lax.axis_index("tile")
    c = t % 2
    half, _, max_order, width = x_ref.shape
    for p in range(half):
        here, there = factor_ref[table_ref[OWNER, p]], factor_other[table_ref[OWNER, p]]
        upper, lower = unfold_factor(jnp.where(c == 0, here, there), jnp.where(c == 0, there, here))
        upper, lower = split(upper), split(lower)
        upper_high[p], upper_low[p] = upper
        lower_high[p], lower_low[p] = lower
        tiles = [x_ref[p, m, :, e * CTW : (e + 1) * CTW] for m in range(2) for e in range(2)]
        tile_ids = [(t ^ m) * 2 + e for m in range(2) for e in range(2)]
        w = whiten(tiles, table_ref, p, upper, lower, tile_ids)
        rows = pl.ds(p * max_order, max_order)
        w0_high[rows, :], w0_low[rows, :] = split(w[:, :width])
        w0t_high[:, rows], w0t_low[:, rows] = split(w[:, :width].T)
        w1t_high[:, rows], w1t_low[:, rows] = split(w[:, width:].T)
    w0 = w0_high[...], w0_low[...]
    g_out[:width] = dot3((w0t_high[...], w0t_low[...]), w0)
    g_out[width:] = dot3((w1t_high[...], w1t_low[...]), w0)


def across(table_ref, rows_ref, group, p, upper_high, upper_low, lower_high, lower_low, max_order):
    t = lax.axis_index("tile")
    last = rows_ref.shape[0] - CHUNK
    tiles = []
    for e in range(2):
        at = table_ref[ROW_AT + group - 2, p * 2 + e]
        starts = [jnp.minimum(at + k, last) for k in range(0, max_order, CHUNK)]
        tiles.append(jnp.concatenate([rows_ref[pl.ds(pl.multiple_of(k, 8), CHUNK), :] for k in starts], axis=0))
    upper, lower = (upper_high[p], upper_low[p]), (lower_high[p], lower_low[p])
    return whiten(tiles, table_ref, p, upper, lower, [(t ^ group) * 2 + e for e in range(2)])


def gram_y(
    table_ref, y_ref, upper_high, upper_low, lower_high, lower_low, w0_high, w0_low, w1t_high, w1t_low,
    w2_high, w2_low, g_out, w2t_high, w2t_low,
):
    depth, width = w0_high.shape
    half = upper_high.shape[0]
    max_order = depth // half
    for p in range(half):
        w = across(table_ref, y_ref, 2, p, upper_high, upper_low, lower_high, lower_low, max_order)
        rows = pl.ds(p * max_order, max_order)
        w2_high[rows, :], w2_low[rows, :] = split(w)
        w2t_high[:, rows], w2t_low[:, rows] = split(w.T)
    w2, w2t = (w2_high[...], w2_low[...]), (w2t_high[...], w2t_low[...])
    g_out[:width] = dot3(w2t, (w0_high[...], w0_low[...]))
    g_out[width : 2 * width] = dot3((w1t_high[...], w1t_low[...]), w2)
    g_out[2 * width :] = dot3(w2t, w2)


def gram_rest(
    table_ref, yc_ref, upper_high, upper_low, lower_high, lower_low, w0_high, w0_low, w2_high, w2_low, g_own, g_y, *refs
):
    firsts, seconds = refs[:4], refs[4:8]
    w3t_high, w3t_low, gram = refs[8:]
    s = lax.axis_index("blk")
    t = lax.axis_index("tile")
    depth, width = w0_high.shape
    half = upper_high.shape[0]
    max_order = depth // half
    for p in range(half):
        w = across(table_ref, yc_ref, 3, p, upper_high, upper_low, lower_high, lower_low, max_order)
        rows = pl.ds(p * max_order, max_order)
        w3t_high[:, rows], w3t_low[:, rows] = split(w.T)
    w3t = w3t_high[...], w3t_low[...]
    for m in range(2):
        gram[0, m] = g_own[m * width : (m + 1) * width]
    gram[0, 2] = g_y[:width]
    gram[0, 3] = dot3(w3t, (w0_high[...], w0_low[...]))
    gram[1, 0] = g_y[:width].T
    for m in range(1, 3):
        gram[1, m] = g_y[m * width : (m + 1) * width]
    gram[1, 3] = dot3(w3t, (w2_high[...], w2_low[...]))

    z, x = s // 2, s % 2

    for n in range(4):
        for a in range(2):
            for b in range(2):
                m, at = (z ^ n) ^ t, (x ^ a) * 128
                firsts[2 * a + b][n] = gram[b, m, pl.ds(pl.multiple_of(at, 8), XY_FIRST), :]
                seconds[n][a, b] = gram[b, m, pl.ds(pl.multiple_of(at + XY_FIRST, 8), 128 - XY_FIRST), :]


def paired_body(blocks, orders, pattern, dest, inv_factor):
    slots, max_order, width = blocks.shape
    n_blk = lax.axis_size("blk")
    half = slots // 2
    tiles = width // CTW
    blocks = pltpu.with_memory_space_constraint(blocks, pltpu.HBM)
    inv_factor = pltpu.with_memory_space_constraint(inv_factor, pltpu.HBM)
    dest, orders, pattern = (pltpu.with_memory_space_constraint(v, pltpu.HBM) for v in (dest, orders, pattern.T))
    hbm = pl.BlockSpec(memory_space=pltpu.HBM)
    smem = pl.BlockSpec(memory_space=pltpu.SMEM)
    vmem = pl.BlockSpec(memory_space=pltpu.VMEM)
    shape = jax.ShapeDtypeStruct
    factor_send, table, level = pl.pallas_call(
        plan,
        out_shape=(
            shape((n_blk, FACTOR_ROWS, CTW), F32),
            shape((9, half * tiles), jnp.int32),
            shape((1,), jnp.int32),
        ),
        in_specs=[hbm] * 4,
        out_specs=(vmem, smem, smem),
        scratch_shapes=[
            pltpu.SMEM(dest.shape, jnp.int32),
            pltpu.SMEM(orders.shape, jnp.int32),
            pltpu.SMEM(pattern.shape, jnp.int32),
            pltpu.VMEM(orders.shape, jnp.int32),
            pltpu.VMEM(pattern.shape, jnp.int32),
            pltpu.VMEM((2, dest.shape[0]), jnp.int32),
            pltpu.SMEM((2, dest.shape[0]), jnp.int32),
            pltpu.SMEM((n_blk, 2, n_blk), jnp.int32),
            pltpu.SMEM((n_blk, n_blk), jnp.int32),
            pltpu.SMEM((n_blk, 3), jnp.int32),
            pltpu.SMEM((n_blk + 1,), jnp.int32),
            pltpu.VMEM((slots, 3, 128, 128), F32),
            pltpu.VMEM((slots, TOP_ROWS, 128), F32),
            pltpu.SemaphoreType.DMA,
            pltpu.SemaphoreType.DMA,
        ],
        compiler_params=pltpu.CompilerParams(vmem_limit_bytes=VMEM_LIMIT),
        name="plan",
    )(dest, orders, pattern, inv_factor)
    rest = [functools.partial(paired_rest, rows) for rows in row_counts(half * tiles * max_order)]
    return lax.switch(level[0], rest, table, blocks, factor_send)


def paired_rest(row_count, table, blocks, factor_send):
    slots, max_order, width = blocks.shape
    n_blk = lax.axis_size("blk")
    n_tile = lax.axis_size("tile")
    half = slots // 2
    tiles = width // CTW
    axes = ("blk", "tile")

    def exchange(value, blk_bits, tile_bits):
        perm = [
            (b * n_tile + t, (b ^ blk_bits) * n_tile + (t ^ tile_bits)) for b in range(n_blk) for t in range(n_tile)
        ]
        return lax.ppermute(value, axes, perm)

    hbm = pl.BlockSpec(memory_space=pltpu.HBM)
    smem = pl.BlockSpec(memory_space=pltpu.SMEM)
    vmem = pl.BlockSpec(memory_space=pltpu.VMEM)
    shape = jax.ShapeDtypeStruct
    params = pltpu.CompilerParams(vmem_limit_bytes=VMEM_LIMIT)
    dma = pltpu.SemaphoreType.DMA

    y_rows = pl.pallas_call(
        pack_rows,
        out_shape=shape((row_count, CTW), F32),
        in_specs=[smem, hbm],
        out_specs=vmem,
        scratch_shapes=[pltpu.VMEM((half, max_order, width), F32), dma((half,))],
        compiler_params=params,
        name="pack_rows",
    )(table, blocks)
    y_recv = exchange(y_rows, 0, 2)
    factors = lax.all_to_all(factor_send, "blk", split_axis=0, concat_axis=0, tiled=True)
    core_blocks = exchange(blocks, 0, 1)
    factors_other = exchange(factors, 0, 1)
    own_table, _ = lax.optimization_barrier((table, factors))
    columns = pl.pallas_call(
        load_columns,
        out_shape=shape((half, 2, max_order, width), F32),
        in_specs=[smem, hbm, hbm],
        out_specs=vmem,
        scratch_shapes=[dma],
        compiler_params=params,
        name="load_columns",
    )(own_table, blocks, core_blocks)

    depth = half * max_order
    *factor, w0_high, w0_low, w1t_high, w1t_low, g_own = pl.pallas_call(
        gram_own,
        out_shape=(
            shape((half, 256, 256), BF16),
            shape((half, 256, 256), BF16),
            shape((half, 128, 384), BF16),
            shape((half, 128, 384), BF16),
            shape((depth, width), BF16),
            shape((depth, width), BF16),
            shape((width, depth), BF16),
            shape((width, depth), BF16),
            shape((2 * width, width), F32),
        ),
        in_specs=[smem] + [vmem] * 3,
        out_specs=(vmem,) * 9,
        scratch_shapes=[pltpu.VMEM((width, depth), BF16), pltpu.VMEM((width, depth), BF16)],
        compiler_params=params,
        name="gram_own",
    )(table, columns, factors, factors_other)

    y_recv, g_own = lax.optimization_barrier((y_recv, g_own))
    yc_recv = exchange(y_recv, 0, 1)
    w2_high, w2_low, g_y = pl.pallas_call(
        gram_y,
        out_shape=(shape((depth, width), BF16), shape((depth, width), BF16), shape((3 * width, width), F32)),
        in_specs=[smem] + [vmem] * 9,
        out_specs=(vmem,) * 3,
        scratch_shapes=[pltpu.VMEM((width, depth), BF16), pltpu.VMEM((width, depth), BF16)],
        compiler_params=params,
        name="gram_y",
    )(table, y_recv, *factor, w0_high, w0_low, w1t_high, w1t_low)
    first_shape, second_shape = (4, XY_FIRST, width), (2, 2, 128 - XY_FIRST, width)
    pieces = pl.pallas_call(
        gram_rest,
        out_shape=(shape(first_shape, F32),) * 4 + (shape(second_shape, F32),) * 4,
        in_specs=[smem] + [vmem] * 11,
        out_specs=(vmem,) * 8,
        scratch_shapes=[
            pltpu.VMEM((width, depth), BF16),
            pltpu.VMEM((width, depth), BF16),
            pltpu.VMEM((2, 4, width, width), F32),
        ],
        compiler_params=params,
        name="gram_rest",
    )(table, yc_recv, *factor, w0_high, w0_low, w2_high, w2_low, g_own, g_y)
    firsts, seconds = pieces[:4], pieces[4:]

    plane = [(a, b) for a in range(2) for b in range(2) if a or b]
    plane_in = [exchange(firsts[2 * a + b], a, 2 * b) for a, b in plane]
    line_in = [exchange(seconds[n], 2 * n, 0) for n in range(1, 4)]
    first = firsts[0] + sum(plane_in)
    second = seconds[0] + sum(line_in)
    line_in = [exchange(first[n], 2 * n, 0) for n in range(1, 4)]
    plane_in = [exchange(second[a, b], a, 2 * b) for a, b in plane]
    gram_tile = jnp.concatenate([first[0] + sum(line_in), second[0, 0] + sum(plane_in)], axis=0)
    return gram_tile * (1.0 / (n_blk * slots * max_order**0.5))


def solution(mesh):
    in_specs = (P("blk", None, "tile"), P(), P(), P(), P("blk", None, None))
    out_specs = P("blk", "tile")
    paired = mesh.shape["blk"] == 8 and mesh.shape["tile"] == 4
    body = paired_body if paired else general_body
    return jax.shard_map(body, mesh=mesh, in_specs=in_specs, out_specs=out_specs, check_vma=False)
```

```python
import functools

import jax
import jax.numpy as jnp
from jax import lax
from jax.experimental import pallas as pl
from jax.experimental.pallas import tpu as pltpu
from jax.sharding import PartitionSpec as P

CTW = 128
F32 = jnp.float32
BF16 = jnp.bfloat16
XY_FIRST = 80
VMEM_LIMIT = 24 << 20


def general_body(blocks, orders, pattern, dest, inv_factor):
    source_index = lax.axis_index("blk")
    owner_count = lax.axis_size("blk")
    tile_index = lax.axis_index("tile")
    slot_count, max_order, column_width = blocks.shape
    block_count = dest.shape[0]
    tiles_here = column_width // CTW
    highest = lax.Precision.HIGHEST
    capacity = (slot_count + owner_count - 1) // owner_count
    dest_grid = dest.reshape(owner_count, slot_count)
    earlier = lax.broadcasted_iota(jnp.int32, (slot_count, slot_count), 1) < lax.broadcasted_iota(
        jnp.int32, (slot_count, slot_count), 0
    )
    matching = dest_grid[:, :, None] == dest_grid[:, None, :]
    ranks = jnp.sum((matching & earlier[None]).astype(jnp.int32), axis=2).reshape(block_count)
    my_dest = lax.dynamic_slice_in_dim(dest, source_index * slot_count, slot_count)
    my_rank = lax.dynamic_slice_in_dim(ranks, source_index * slot_count, slot_count)
    my_orders = lax.dynamic_slice_in_dim(orders, source_index * slot_count, slot_count)
    my_tiles = lax.dynamic_slice(
        pattern, (source_index * slot_count, tile_index * tiles_here), (slot_count, tiles_here)
    )
    row_ids = lax.broadcasted_iota(jnp.int32, (slot_count, max_order), 1)
    row_mask = (row_ids < my_orders[:, None]).astype(F32)
    col_mask = jnp.repeat(my_tiles.astype(F32), CTW, axis=1)
    masked = blocks * row_mask[:, :, None] * col_mask[:, None, :]
    owned = lax.dynamic_slice_in_dim(
        jnp.argsort(dest, stable=True), source_index * slot_count, slot_count
    )
    slot_ids = my_dest * capacity + my_rank
    placing = (
        lax.broadcasted_iota(jnp.int32, (owner_count * capacity, slot_count), 0)
        == slot_ids[None, :]
    ).astype(F32)
    outgoing = jnp.einsum("ak,krc->arc", placing, masked, precision=highest, preferred_element_type=F32)
    arrived = lax.all_to_all(outgoing, "blk", split_axis=0, concat_axis=0, tiled=True)
    positions = owned // slot_count * capacity + ranks[owned]
    own_blocks = jnp.take(arrived, positions, axis=0)
    own_mask = (row_ids < orders[owned][:, None]).astype(F32)
    whitened = jnp.einsum(
        "jrq,jqc->jrc", inv_factor, own_blocks, precision=highest, preferred_element_type=F32
    )
    whitened_rows = (whitened * own_mask[:, :, None]).reshape(slot_count * max_order, column_width)
    factor = 1.0 / (block_count * max_order**0.5)
    partial_sums = lax.dot_general(
        lax.all_gather(whitened_rows, "tile", axis=1, tiled=True),
        whitened_rows,
        (((0,), (0,)), ((), ())),
        precision=highest,
        preferred_element_type=F32,
    )
    gram_tile = lax.psum_scatter(partial_sums, "blk", scatter_dimension=0, tiled=True)
    return gram_tile * factor


MINE, OWNER, ORDER, BITS, OTHERS, ORDER_OTHERS, BITS_OTHERS, ROW_AT = 0, 1, 2, 3, 4, 5, 6, 7
SHARES = (0.625, 1.0)
CHUNK = 64


def round8(order):
    return (order + 7) // 8 * 8


def row_counts(all_rows):
    return [int(share * all_rows) // 8 * 8 for share in SHARES]


TOP_ROWS = 32
FACTOR_ROWS = 128 + 128 + 8 + TOP_ROWS


def iotas(rows):
    return tuple(lax.broadcasted_iota(jnp.int32, (rows, 128), axis) for axis in range(2))


def fold_factor(c, tiles, top, out):
    @pl.when(c == 0)
    def _():
        row, col = iotas(128)
        t11 = tiles[2]
        out[:128] = tiles[1]
        out[128:256] = jnp.where(row >= col, tiles[0], t11.T)
        out[256:264] = jnp.broadcast_to(jnp.sum(jnp.where(row == col, t11, 0.0), axis=0, keepdims=True), (8, 128))
        out[264:] = top[...]

    @pl.when(c == 1)
    def _():
        row, col = iotas(64)
        t22 = tiles[2]
        low = t22[64:]
        out[: 128 - TOP_ROWS] = tiles[0, TOP_ROWS:]
        out[128 - TOP_ROWS : 256 - TOP_ROWS] = tiles[1]
        out[256 - TOP_ROWS : 320 - TOP_ROWS] = jnp.where(
            col >= 64,
            pltpu.roll(low, 64, 1),
            jnp.where(row >= col, t22[:64], pltpu.roll(t22.T[64:], 64, 1)),
        )
        out[320 - TOP_ROWS :] = jnp.broadcast_to(
            jnp.sum(jnp.where(row + 64 == col, low, 0.0), axis=0, keepdims=True), (8, 128)
        )


def unfold_factor(first, second):
    row, col = iotas(128)
    both = first[128:256]
    f00 = jnp.where(row >= col, both, 0.0)
    f11 = jnp.where(row > col, both.T, jnp.where(row == col, first[256:257], 0.0))
    upper = jnp.concatenate(
        [jnp.concatenate([f00, jnp.zeros_like(f00)], axis=1), jnp.concatenate([first[:128], f11], axis=1)], axis=0
    )
    f20 = jnp.concatenate([first[264:], second[: 128 - TOP_ROWS]], axis=0)
    f21 = second[128 - TOP_ROWS : 256 - TOP_ROWS]
    fold, diagonal = second[256 - TOP_ROWS : 320 - TOP_ROWS], second[320 - TOP_ROWS : 321 - TOP_ROWS]
    turned = jnp.concatenate([fold, fold], axis=0).T[:64]
    row, col = iotas(64)
    f22 = jnp.concatenate(
        [
            jnp.where((row >= col) & (col < 64), fold, 0.0),
            jnp.where(
                col < 64,
                pltpu.roll(fold, 64, 1),
                jnp.where(row + 64 > col, pltpu.roll(turned, 64, 1), jnp.where(row + 64 == col, diagonal, 0.0)),
            ),
        ],
        axis=0,
    )
    return upper, jnp.concatenate([f20, f21, f22], axis=1)


def plan(
    dest_hbm, orders_hbm, pattern_hbm, inv_ref, factor_out, table_ref, level_ref,
    dest_ref, orders_ref, orders_at, pattern_at, weight_at, weight_ref, block_at, count, found_at, factor_at, tiles_at, top_at, small_sem, factor_sem,
):
    s = lax.axis_index("blk")
    t = lax.axis_index("tile")
    y, c = t // 2, t % 2
    slots, max_order, _ = inv_ref.shape
    n_blk = count.shape[0]
    tiles = pattern_at.shape[0] // 4

    def small_loads():
        for src, dst in (
            (orders_hbm, orders_at), (pattern_hbm, pattern_at), (dest_hbm, dest_ref), (orders_hbm, orders_ref),
        ):
            yield pltpu.make_async_copy(src, dst, small_sem)

    def factor_loads():
        for row in range(slots):
            for k, (ti, tj) in enumerate(((0, 0), (1, 0), (1, 1))):
                ri, rj = jnp.where(c == 0, ti, 2), jnp.where(c == 0, tj, k)
                yield pltpu.make_async_copy(
                    inv_ref.at[row, pl.ds(pl.multiple_of(ri * 128, 128), 128), pl.ds(pl.multiple_of(rj * 128, 128), 128)],
                    tiles_at.at[row, k],
                    factor_sem,
                )
            yield pltpu.make_async_copy(
                inv_ref.at[row, pl.ds(256, TOP_ROWS), pl.ds(0, 128)], top_at.at[row], factor_sem
            )

    for copy in small_loads():
        copy.start()
    for copy in factor_loads():
        copy.start()
    for copy in small_loads():
        copy.wait()
    ones = pattern_at[...]
    counts = [sum(ones[q * tiles + e : q * tiles + e + 1] for e in range(tiles)) for q in range(4)]
    rows = round8(orders_at[...])[None, :]
    bits_of = sum(jnp.where(ones[ct : ct + 1] != 0, 1 << ct, 0) for ct in range(4 * tiles))
    weight_at[...] = jnp.concatenate(
        [rows * (counts[q] + counts[q + 1] * 65536) for q in (0, 2)] + [bits_of], axis=0
    )
    weights = pltpu.make_async_copy(weight_at, weight_ref, small_sem)
    weights.start()

    def scan_blocks(source, found):
        for o in range(n_blk):
            count[source, o] = 0
            block_at[source, 0, o] = 0
            block_at[source, 1, o] = 0
        found_at[source, 0] = 0
        found_at[source, 1] = 0
        for i in range(slots):
            o = dest_ref[source * slots + i]
            r = count[source, o]
            block_at[source, r, o] = i
            count[source, o] = r + 1
            mine = o == s
            found_at[source, jnp.where(mine, r, 2)] = found
            found = found + jnp.where(mine, 1, 0)
        return found

    lax.fori_loop(0, n_blk, scan_blocks, jnp.int32(0), unroll=True)
    weights.wait()

    def scan_source(source, most):
        base = source * slots

        def top(v):
            return jnp.maximum(jnp.maximum(v[0] & 65535, v[0] >> 16), jnp.maximum(v[1] & 65535, v[1] >> 16))

        here = source == s
        p, low, high = jnp.int32(0), jnp.int32(0), jnp.int32(0)
        for o in range(n_blk):
            on = count[source, o] > 0
            first, second = block_at[source, 0, o], block_at[source, 1, o]
            straight = low + weight_ref[0, base + second], high + weight_ref[1, base + first]
            crossed = low + weight_ref[0, base + first], high + weight_ref[1, base + second]
            flip = top(crossed) < top(straight)
            side = y ^ jnp.where(flip, 1, 0)
            factor_at[jnp.where(on & (s == o), source, n_blk)] = found_at[source, side]
            column = jnp.where(on & here, p, slots // 2)
            table_ref[MINE, column] = jnp.where(side == 0, first, second)
            table_ref[OTHERS, column] = jnp.where(side == 0, second, first)
            table_ref[OWNER, column] = jnp.int32(o)
            low = jnp.where(on, jnp.where(flip, crossed[0], straight[0]), low)
            high = jnp.where(on, jnp.where(flip, crossed[1], straight[1]), high)
            p = p + jnp.where(on, 1, 0)
        return jnp.maximum(most, top((low, high)))

    for source in range(n_blk):
        factor_at[source] = 0
    most = lax.fori_loop(0, n_blk, scan_source, jnp.int32(0), unroll=True)

    level = jnp.int32(0)
    for rows in row_counts(slots // 2 * tiles * max_order)[:-1]:
        level = level + jnp.where(most + (CHUNK - 8) > rows, 1, 0)
    level_ref[0] = level

    for which, order_row, bits_row in ((MINE, ORDER, BITS), (OTHERS, ORDER_OTHERS, BITS_OTHERS)):
        for p in range(slots // 2):
            number = s * slots + table_ref[which, p]
            table_ref[order_row, p] = orders_ref[number]
            table_ref[bits_row, p] = weight_ref[2, number]
    for k in range(2):
        at = jnp.int32(0)
        for p in range(slots // 2):
            rows, bits = round8(table_ref[ORDER, p]), table_ref[BITS, p]
            for e in range(tiles):
                table_ref[ROW_AT + k, p * tiles + e] = at
                at = at + jnp.where(tile_on(bits, (t ^ (2 + k)) * tiles + e), rows, 0)

    for copy in factor_loads():
        copy.wait()

    def fold(source, carry):
        row = factor_at[source]
        fold_factor(c, tiles_at.at[row], top_at.at[row], factor_out.at[source])
        return carry

    lax.fori_loop(0, n_blk, fold, 0)


def tile_on(bits, tile):
    return ((bits >> tile) & 1) == 1


def pack_rows(table_ref, blocks_ref, packed, staged, sems):
    t = lax.axis_index("tile")
    slots, max_order, width = blocks_ref.shape
    tiles = width // CTW

    def loads():
        for p in range(slots // 2):
            yield pltpu.make_async_copy(blocks_ref.at[table_ref[OTHERS, p]], staged.at[p], sems.at[p])

    for copy in loads():
        copy.start()
    at = jnp.int32(0)
    for p, copy in enumerate(loads()):
        copy.wait()
        for e in range(tiles):
            on = tile_on(table_ref[BITS_OTHERS, p], t * tiles + e)

            def write(k, carry, at=at, p=p, e=e):
                packed[pl.ds(pl.multiple_of(at + k * CHUNK, 8), CHUNK), :] = staged[
                    p, pl.ds(pl.multiple_of(k * CHUNK, CHUNK), CHUNK), e * CTW : (e + 1) * CTW
                ]
                return carry

            chunks = (table_ref[ORDER_OTHERS, p] + CHUNK - 1) // CHUNK
            lax.fori_loop(0, jnp.where(on, chunks, 0), write, 0)
            at = at + jnp.where(on, round8(table_ref[ORDER_OTHERS, p]), 0)


def load_columns(table_ref, blocks_ref, core_ref, x_out, sem):
    def loads():
        for p in range(x_out.shape[0]):
            for m, ref in enumerate((blocks_ref, core_ref)):
                yield pltpu.make_async_copy(ref.at[table_ref[MINE, p]], x_out.at[p, m], sem)

    for copy in loads():
        copy.start()
    for copy in loads():
        copy.wait()


def split(x):
    high = x.astype(BF16)
    return high, (x - high.astype(F32)).astype(BF16)


def dot3(a, b):
    def dot(p, q):
        return jnp.dot(p, q, preferred_element_type=F32)

    return dot(a[0], b[0]) + (dot(a[0], b[1]) + dot(a[1], b[0]))


def whiten(tiles, table_ref, p, upper, lower, tile_ids):
    order = table_ref[ORDER, p]
    row_on = lax.broadcasted_iota(jnp.int32, tiles[0].shape, 0) < order
    parts = [
        jnp.where(row_on & tile_on(table_ref[BITS, p], ct), tile, 0.0) for tile, ct in zip(tiles, tile_ids)
    ]
    x = split(jnp.concatenate(parts, axis=1))
    w = jnp.concatenate([dot3(upper, (x[0][:256], x[1][:256])), dot3(lower, x)], axis=0)
    return jnp.where(lax.broadcasted_iota(jnp.int32, w.shape, 0) < order, w, 0.0)


def gram_own(
    table_ref, x_ref, factor_ref, factor_other,
    upper_high, upper_low, lower_high, lower_low, w0_high, w0_low, w1t_high, w1t_low, g_out, w0t_high, w0t_low,
):
    t = lax.axis_index("tile")
    c = t % 2
    half, _, max_order, width = x_ref.shape
    for p in range(half):
        here, there = factor_ref[table_ref[OWNER, p]], factor_other[table_ref[OWNER, p]]
        upper, lower = unfold_factor(jnp.where(c == 0, here, there), jnp.where(c == 0, there, here))
        upper, lower = split(upper), split(lower)
        upper_high[p], upper_low[p] = upper
        lower_high[p], lower_low[p] = lower
        tiles = [x_ref[p, m, :, e * CTW : (e + 1) * CTW] for m in range(2) for e in range(2)]
        tile_ids = [(t ^ m) * 2 + e for m in range(2) for e in range(2)]
        w = whiten(tiles, table_ref, p, upper, lower, tile_ids)
        rows = pl.ds(p * max_order, max_order)
        w0_high[rows, :], w0_low[rows, :] = split(w[:, :width])
        w0t_high[:, rows], w0t_low[:, rows] = split(w[:, :width].T)
        w1t_high[:, rows], w1t_low[:, rows] = split(w[:, width:].T)
    w0 = w0_high[...], w0_low[...]
    g_out[:width] = dot3((w0t_high[...], w0t_low[...]), w0)
    g_out[width:] = dot3((w1t_high[...], w1t_low[...]), w0)


def across(table_ref, rows_ref, group, p, upper_high, upper_low, lower_high, lower_low, max_order):
    t = lax.axis_index("tile")
    last = rows_ref.shape[0] - CHUNK
    tiles = []
    for e in range(2):
        at = table_ref[ROW_AT + group - 2, p * 2 + e]
        starts = [jnp.minimum(at + k, last) for k in range(0, max_order, CHUNK)]
        tiles.append(jnp.concatenate([rows_ref[pl.ds(pl.multiple_of(k, 8), CHUNK), :] for k in starts], axis=0))
    upper, lower = (upper_high[p], upper_low[p]), (lower_high[p], lower_low[p])
    return whiten(tiles, table_ref, p, upper, lower, [(t ^ group) * 2 + e for e in range(2)])


def gram_y(
    table_ref, y_ref, upper_high, upper_low, lower_high, lower_low, w0_high, w0_low, w1t_high, w1t_low,
    w2_high, w2_low, g_out, w2t_high, w2t_low,
):
    depth, width = w0_high.shape
    half = upper_high.shape[0]
    max_order = depth // half
    for p in range(half):
        w = across(table_ref, y_ref, 2, p, upper_high, upper_low, lower_high, lower_low, max_order)
        rows = pl.ds(p * max_order, max_order)
        w2_high[rows, :], w2_low[rows, :] = split(w)
        w2t_high[:, rows], w2t_low[:, rows] = split(w.T)
    w2, w2t = (w2_high[...], w2_low[...]), (w2t_high[...], w2t_low[...])
    g_out[:width] = dot3(w2t, (w0_high[...], w0_low[...]))
    g_out[width : 2 * width] = dot3((w1t_high[...], w1t_low[...]), w2)
    g_out[2 * width :] = dot3(w2t, w2)


def gram_rest(
    table_ref, yc_ref, upper_high, upper_low, lower_high, lower_low, w0_high, w0_low, w2_high, w2_low, g_own, g_y, *refs
):
    firsts, seconds = refs[:4], refs[4:8]
    w3t_high, w3t_low, gram = refs[8:]
    s = lax.axis_index("blk")
    t = lax.axis_index("tile")
    depth, width = w0_high.shape
    half = upper_high.shape[0]
    max_order = depth // half
    for p in range(half):
        w = across(table_ref, yc_ref, 3, p, upper_high, upper_low, lower_high, lower_low, max_order)
        rows = pl.ds(p * max_order, max_order)
        w3t_high[:, rows], w3t_low[:, rows] = split(w.T)
    w3t = w3t_high[...], w3t_low[...]
    for m in range(2):
        gram[0, m] = g_own[m * width : (m + 1) * width]
    gram[0, 2] = g_y[:width]
    gram[0, 3] = dot3(w3t, (w0_high[...], w0_low[...]))
    gram[1, 0] = g_y[:width].T
    for m in range(1, 3):
        gram[1, m] = g_y[m * width : (m + 1) * width]
    gram[1, 3] = dot3(w3t, (w2_high[...], w2_low[...]))

    z, x = s // 2, s % 2

    for n in range(4):
        for a in range(2):
            for b in range(2):
                m, at = (z ^ n) ^ t, (x ^ a) * 128
                firsts[2 * a + b][n] = gram[b, m, pl.ds(pl.multiple_of(at, 8), XY_FIRST), :]
                seconds[n][a, b] = gram[b, m, pl.ds(pl.multiple_of(at + XY_FIRST, 8), 128 - XY_FIRST), :]


def paired_body(blocks, orders, pattern, dest, inv_factor):
    slots, max_order, width = blocks.shape
    n_blk = lax.axis_size("blk")
    half = slots // 2
    tiles = width // CTW
    blocks = pltpu.with_memory_space_constraint(blocks, pltpu.HBM)
    inv_factor = pltpu.with_memory_space_constraint(inv_factor, pltpu.HBM)
    dest, orders, pattern = (pltpu.with_memory_space_constraint(v, pltpu.HBM) for v in (dest, orders, pattern.T))
    hbm = pl.BlockSpec(memory_space=pltpu.HBM)
    smem = pl.BlockSpec(memory_space=pltpu.SMEM)
    vmem = pl.BlockSpec(memory_space=pltpu.VMEM)
    shape = jax.ShapeDtypeStruct
    factor_send, table, level = pl.pallas_call(
        plan,
        out_shape=(
            shape((n_blk, FACTOR_ROWS, CTW), F32),
            shape((9, half * tiles), jnp.int32),
            shape((1,), jnp.int32),
        ),
        in_specs=[hbm] * 4,
        out_specs=(vmem, smem, smem),
        scratch_shapes=[
            pltpu.SMEM(dest.shape, jnp.int32),
            pltpu.SMEM(orders.shape, jnp.int32),
            pltpu.VMEM(orders.shape, jnp.int32),
            pltpu.VMEM(pattern.shape, jnp.int32),
            pltpu.VMEM((3, dest.shape[0]), jnp.int32),
            pltpu.SMEM((3, dest.shape[0]), jnp.int32),
            pltpu.SMEM((n_blk, 2, n_blk), jnp.int32),
            pltpu.SMEM((n_blk, n_blk), jnp.int32),
            pltpu.SMEM((n_blk, 3), jnp.int32),
            pltpu.SMEM((n_blk + 1,), jnp.int32),
            pltpu.VMEM((slots, 3, 128, 128), F32),
            pltpu.VMEM((slots, TOP_ROWS, 128), F32),
            pltpu.SemaphoreType.DMA,
            pltpu.SemaphoreType.DMA,
        ],
        compiler_params=pltpu.CompilerParams(vmem_limit_bytes=VMEM_LIMIT),
        name="plan",
    )(dest, orders, pattern, inv_factor)
    rest = [functools.partial(paired_rest, rows) for rows in row_counts(half * tiles * max_order)]
    return lax.switch(level[0], rest, table, blocks, factor_send)


def paired_rest(row_count, table, blocks, factor_send):
    slots, max_order, width = blocks.shape
    n_blk = lax.axis_size("blk")
    n_tile = lax.axis_size("tile")
    half = slots // 2
    tiles = width // CTW
    axes = ("blk", "tile")

    def exchange(value, blk_bits, tile_bits):
        perm = [
            (b * n_tile + t, (b ^ blk_bits) * n_tile + (t ^ tile_bits)) for b in range(n_blk) for t in range(n_tile)
        ]
        return lax.ppermute(value, axes, perm)

    hbm = pl.BlockSpec(memory_space=pltpu.HBM)
    smem = pl.BlockSpec(memory_space=pltpu.SMEM)
    vmem = pl.BlockSpec(memory_space=pltpu.VMEM)
    shape = jax.ShapeDtypeStruct
    params = pltpu.CompilerParams(vmem_limit_bytes=VMEM_LIMIT)
    dma = pltpu.SemaphoreType.DMA

    y_rows = pl.pallas_call(
        pack_rows,
        out_shape=shape((row_count, CTW), F32),
        in_specs=[smem, hbm],
        out_specs=vmem,
        scratch_shapes=[pltpu.VMEM((half, max_order, width), F32), dma((half,))],
        compiler_params=params,
        name="pack_rows",
    )(table, blocks)
    y_recv = exchange(y_rows, 0, 2)
    factors = lax.all_to_all(factor_send, "blk", split_axis=0, concat_axis=0, tiled=True)
    core_blocks = exchange(blocks, 0, 1)
    factors_other = exchange(factors, 0, 1)
    own_table, _ = lax.optimization_barrier((table, factors))
    columns = pl.pallas_call(
        load_columns,
        out_shape=shape((half, 2, max_order, width), F32),
        in_specs=[smem, hbm, hbm],
        out_specs=vmem,
        scratch_shapes=[dma],
        compiler_params=params,
        name="load_columns",
    )(own_table, blocks, core_blocks)

    depth = half * max_order
    *factor, w0_high, w0_low, w1t_high, w1t_low, g_own = pl.pallas_call(
        gram_own,
        out_shape=(
            shape((half, 256, 256), BF16),
            shape((half, 256, 256), BF16),
            shape((half, 128, 384), BF16),
            shape((half, 128, 384), BF16),
            shape((depth, width), BF16),
            shape((depth, width), BF16),
            shape((width, depth), BF16),
            shape((width, depth), BF16),
            shape((2 * width, width), F32),
        ),
        in_specs=[smem] + [vmem] * 3,
        out_specs=(vmem,) * 9,
        scratch_shapes=[pltpu.VMEM((width, depth), BF16), pltpu.VMEM((width, depth), BF16)],
        compiler_params=params,
        name="gram_own",
    )(table, columns, factors, factors_other)

    y_recv, g_own = lax.optimization_barrier((y_recv, g_own))
    yc_recv = exchange(y_recv, 0, 1)
    w2_high, w2_low, g_y = pl.pallas_call(
        gram_y,
        out_shape=(shape((depth, width), BF16), shape((depth, width), BF16), shape((3 * width, width), F32)),
        in_specs=[smem] + [vmem] * 9,
        out_specs=(vmem,) * 3,
        scratch_shapes=[pltpu.VMEM((width, depth), BF16), pltpu.VMEM((width, depth), BF16)],
        compiler_params=params,
        name="gram_y",
    )(table, y_recv, *factor, w0_high, w0_low, w1t_high, w1t_low)
    first_shape, second_shape = (4, XY_FIRST, width), (2, 2, 128 - XY_FIRST, width)
    pieces = pl.pallas_call(
        gram_rest,
        out_shape=(shape(first_shape, F32),) * 4 + (shape(second_shape, F32),) * 4,
        in_specs=[smem] + [vmem] * 11,
        out_specs=(vmem,) * 8,
        scratch_shapes=[
            pltpu.VMEM((width, depth), BF16),
            pltpu.VMEM((width, depth), BF16),
            pltpu.VMEM((2, 4, width, width), F32),
        ],
        compiler_params=params,
        name="gram_rest",
    )(table, yc_recv, *factor, w0_high, w0_low, w2_high, w2_low, g_own, g_y)
    firsts, seconds = pieces[:4], pieces[4:]

    plane = [(a, b) for a in range(2) for b in range(2) if a or b]
    plane_in = [exchange(firsts[2 * a + b], a, 2 * b) for a, b in plane]
    line_in = [exchange(seconds[n], 2 * n, 0) for n in range(1, 4)]
    first = firsts[0] + sum(plane_in)
    second = seconds[0] + sum(line_in)
    line_in = [exchange(first[n], 2 * n, 0) for n in range(1, 4)]
    plane_in = [exchange(second[a, b], a, 2 * b) for a, b in plane]
    gram_tile = jnp.concatenate([first[0] + sum(line_in), second[0, 0] + sum(plane_in)], axis=0)
    return gram_tile * (1.0 / (n_blk * slots * max_order**0.5))


def solution(mesh):
    in_specs = (P("blk", None, "tile"), P(), P(), P(), P("blk", None, None))
    out_specs = P("blk", "tile")
    paired = mesh.shape["blk"] == 8 and mesh.shape["tile"] == 4
    body = paired_body if paired else general_body
    return jax.shard_map(body, mesh=mesh, in_specs=in_specs, out_specs=out_specs, check_vma=False)
```

```python
import functools

import jax
import jax.numpy as jnp
from jax import lax
from jax.experimental import pallas as pl
from jax.experimental.pallas import tpu as pltpu
from jax.sharding import PartitionSpec as P

CTW = 128
F32 = jnp.float32
BF16 = jnp.bfloat16
XY_FIRST = 80
VMEM_LIMIT = 16 << 20


def general_body(blocks, orders, pattern, dest, inv_factor):
    source_index = lax.axis_index("blk")
    owner_count = lax.axis_size("blk")
    tile_index = lax.axis_index("tile")
    slot_count, max_order, column_width = blocks.shape
    block_count = dest.shape[0]
    tiles_here = column_width // CTW
    highest = lax.Precision.HIGHEST
    capacity = (slot_count + owner_count - 1) // owner_count
    dest_grid = dest.reshape(owner_count, slot_count)
    earlier = lax.broadcasted_iota(jnp.int32, (slot_count, slot_count), 1) < lax.broadcasted_iota(
        jnp.int32, (slot_count, slot_count), 0
    )
    matching = dest_grid[:, :, None] == dest_grid[:, None, :]
    ranks = jnp.sum((matching & earlier[None]).astype(jnp.int32), axis=2).reshape(block_count)
    my_dest = lax.dynamic_slice_in_dim(dest, source_index * slot_count, slot_count)
    my_rank = lax.dynamic_slice_in_dim(ranks, source_index * slot_count, slot_count)
    my_orders = lax.dynamic_slice_in_dim(orders, source_index * slot_count, slot_count)
    my_tiles = lax.dynamic_slice(
        pattern, (source_index * slot_count, tile_index * tiles_here), (slot_count, tiles_here)
    )
    row_ids = lax.broadcasted_iota(jnp.int32, (slot_count, max_order), 1)
    row_mask = (row_ids < my_orders[:, None]).astype(F32)
    col_mask = jnp.repeat(my_tiles.astype(F32), CTW, axis=1)
    masked = blocks * row_mask[:, :, None] * col_mask[:, None, :]
    owned = lax.dynamic_slice_in_dim(
        jnp.argsort(dest, stable=True), source_index * slot_count, slot_count
    )
    slot_ids = my_dest * capacity + my_rank
    placing = (
        lax.broadcasted_iota(jnp.int32, (owner_count * capacity, slot_count), 0)
        == slot_ids[None, :]
    ).astype(F32)
    outgoing = jnp.einsum("ak,krc->arc", placing, masked, precision=highest, preferred_element_type=F32)
    arrived = lax.all_to_all(outgoing, "blk", split_axis=0, concat_axis=0, tiled=True)
    positions = owned // slot_count * capacity + ranks[owned]
    own_blocks = jnp.take(arrived, positions, axis=0)
    own_mask = (row_ids < orders[owned][:, None]).astype(F32)
    whitened = jnp.einsum(
        "jrq,jqc->jrc", inv_factor, own_blocks, precision=highest, preferred_element_type=F32
    )
    whitened_rows = (whitened * own_mask[:, :, None]).reshape(slot_count * max_order, column_width)
    factor = 1.0 / (block_count * max_order**0.5)
    partial_sums = lax.dot_general(
        lax.all_gather(whitened_rows, "tile", axis=1, tiled=True),
        whitened_rows,
        (((0,), (0,)), ((), ())),
        precision=highest,
        preferred_element_type=F32,
    )
    gram_tile = lax.psum_scatter(partial_sums, "blk", scatter_dimension=0, tiled=True)
    return gram_tile * factor


MINE, OWNER, ORDER, BITS, OTHERS, ORDER_OTHERS, BITS_OTHERS, ROW_AT = 0, 1, 2, 3, 4, 5, 6, 7
SHARES = (0.625, 1.0)
CHUNK = 64


def round8(order):
    return (order + 7) // 8 * 8


def row_counts(all_rows):
    return [int(share * all_rows) // 8 * 8 for share in SHARES]


TOP_ROWS = 32
FACTOR_ROWS = 128 + 128 + 8 + TOP_ROWS


def iotas(rows):
    return tuple(lax.broadcasted_iota(jnp.int32, (rows, 128), axis) for axis in range(2))


def fold_factor(c, tiles, top, out):
    @pl.when(c == 0)
    def _():
        row, col = iotas(128)
        t11 = tiles[2]
        out[:128] = tiles[1]
        out[128:256] = jnp.where(row >= col, tiles[0], t11.T)
        out[256:264] = jnp.broadcast_to(jnp.sum(jnp.where(row == col, t11, 0.0), axis=0, keepdims=True), (8, 128))
        out[264:] = top[...]

    @pl.when(c == 1)
    def _():
        row, col = iotas(64)
        t22 = tiles[2]
        low = t22[64:]
        out[: 128 - TOP_ROWS] = tiles[0, TOP_ROWS:]
        out[128 - TOP_ROWS : 256 - TOP_ROWS] = tiles[1]
        out[256 - TOP_ROWS : 320 - TOP_ROWS] = jnp.where(
            col >= 64,
            pltpu.roll(low, 64, 1),
            jnp.where(row >= col, t22[:64], pltpu.roll(t22.T[64:], 64, 1)),
        )
        out[320 - TOP_ROWS :] = jnp.broadcast_to(
            jnp.sum(jnp.where(row + 64 == col, low, 0.0), axis=0, keepdims=True), (8, 128)
        )


def unfold_factor(first, second):
    row, col = iotas(128)
    both = first[128:256]
    f00 = jnp.where(row >= col, both, 0.0)
    f11 = jnp.where(row > col, both.T, jnp.where(row == col, first[256:257], 0.0))
    upper = jnp.concatenate(
        [jnp.concatenate([f00, jnp.zeros_like(f00)], axis=1), jnp.concatenate([first[:128], f11], axis=1)], axis=0
    )
    f20 = jnp.concatenate([first[264:], second[: 128 - TOP_ROWS]], axis=0)
    f21 = second[128 - TOP_ROWS : 256 - TOP_ROWS]
    fold, diagonal = second[256 - TOP_ROWS : 320 - TOP_ROWS], second[320 - TOP_ROWS : 321 - TOP_ROWS]
    turned = jnp.concatenate([fold, fold], axis=0).T[:64]
    row, col = iotas(64)
    f22 = jnp.concatenate(
        [
            jnp.where((row >= col) & (col < 64), fold, 0.0),
            jnp.where(
                col < 64,
                pltpu.roll(fold, 64, 1),
                jnp.where(row + 64 > col, pltpu.roll(turned, 64, 1), jnp.where(row + 64 == col, diagonal, 0.0)),
            ),
        ],
        axis=0,
    )
    return upper, jnp.concatenate([f20, f21, f22], axis=1)


def plan(
    dest_hbm, orders_hbm, pattern_hbm, inv_ref, factor_out, table_ref, level_ref,
    dest_ref, orders_ref, orders_at, pattern_at, weight_at, weight_ref, block_at, count, found_at, factor_at, tiles_at, top_at, small_sem, factor_sem,
):
    s = lax.axis_index("blk")
    t = lax.axis_index("tile")
    y, c = t // 2, t % 2
    slots, max_order, _ = inv_ref.shape
    n_blk = count.shape[0]
    tiles = pattern_at.shape[0] // 4

    def small_loads():
        for src, dst in (
            (orders_hbm, orders_at), (pattern_hbm, pattern_at), (dest_hbm, dest_ref), (orders_hbm, orders_ref),
        ):
            yield pltpu.make_async_copy(src, dst, small_sem)

    def factor_loads():
        for row in range(slots):
            for k, (ti, tj) in enumerate(((0, 0), (1, 0), (1, 1))):
                ri, rj = jnp.where(c == 0, ti, 2), jnp.where(c == 0, tj, k)
                yield pltpu.make_async_copy(
                    inv_ref.at[row, pl.ds(pl.multiple_of(ri * 128, 128), 128), pl.ds(pl.multiple_of(rj * 128, 128), 128)],
                    tiles_at.at[row, k],
                    factor_sem,
                )
            yield pltpu.make_async_copy(
                inv_ref.at[row, pl.ds(256, TOP_ROWS), pl.ds(0, 128)], top_at.at[row], factor_sem
            )

    for copy in small_loads():
        copy.start()
    for copy in factor_loads():
        copy.start()
    for copy in small_loads():
        copy.wait()
    ones = pattern_at[...]
    counts = [sum(ones[q * tiles + e : q * tiles + e + 1] for e in range(tiles)) for q in range(4)]
    rows = round8(orders_at[...])[None, :]
    bits_of = sum(jnp.where(ones[ct : ct + 1] != 0, 1 << ct, 0) for ct in range(4 * tiles))
    weight_at[...] = jnp.concatenate(
        [rows * (counts[q] + counts[q + 1] * 65536) for q in (0, 2)] + [bits_of], axis=0
    )
    weights = pltpu.make_async_copy(weight_at, weight_ref, small_sem)
    weights.start()

    def scan_blocks(source, found):
        for o in range(n_blk):
            count[source, o] = 0
            block_at[source, 0, o] = 0
            block_at[source, 1, o] = 0
        found_at[source, 0] = 0
        found_at[source, 1] = 0
        for i in range(slots):
            o = dest_ref[source * slots + i]
            r = count[source, o]
            block_at[source, r, o] = i
            count[source, o] = r + 1
            mine = o == s
            found_at[source, jnp.where(mine, r, 2)] = found
            found = found + jnp.where(mine, 1, 0)
        return found

    lax.fori_loop(0, n_blk, scan_blocks, jnp.int32(0), unroll=True)
    weights.wait()

    def scan_source(source, most):
        base = source * slots

        def top(v):
            return jnp.maximum(jnp.maximum(v[0] & 65535, v[0] >> 16), jnp.maximum(v[1] & 65535, v[1] >> 16))

        here = source == s
        p, low, high = jnp.int32(0), jnp.int32(0), jnp.int32(0)
        for o in range(n_blk):
            on = count[source, o] > 0
            first, second = block_at[source, 0, o], block_at[source, 1, o]
            straight = low + weight_ref[0, base + second], high + weight_ref[1, base + first]
            crossed = low + weight_ref[0, base + first], high + weight_ref[1, base + second]
            flip = top(crossed) < top(straight)
            side = y ^ jnp.where(flip, 1, 0)
            factor_at[jnp.where(on & (s == o), source, n_blk)] = found_at[source, side]
            column = jnp.where(on & here, p, slots // 2)
            table_ref[MINE, column] = jnp.where(side == 0, first, second)
            table_ref[OTHERS, column] = jnp.where(side == 0, second, first)
            table_ref[OWNER, column] = jnp.int32(o)
            low = jnp.where(on, jnp.where(flip, crossed[0], straight[0]), low)
            high = jnp.where(on, jnp.where(flip, crossed[1], straight[1]), high)
            p = p + jnp.where(on, 1, 0)
        return jnp.maximum(most, top((low, high)))

    for source in range(n_blk):
        factor_at[source] = 0
    most = lax.fori_loop(0, n_blk, scan_source, jnp.int32(0), unroll=True)

    level = jnp.int32(0)
    for rows in row_counts(slots // 2 * tiles * max_order)[:-1]:
        level = level + jnp.where(most + (CHUNK - 8) > rows, 1, 0)
    level_ref[0] = level

    for which, order_row, bits_row in ((MINE, ORDER, BITS), (OTHERS, ORDER_OTHERS, BITS_OTHERS)):
        for p in range(slots // 2):
            number = s * slots + table_ref[which, p]
            table_ref[order_row, p] = orders_ref[number]
            table_ref[bits_row, p] = weight_ref[2, number]
    for k in range(2):
        at = jnp.int32(0)
        for p in range(slots // 2):
            rows, bits = round8(table_ref[ORDER, p]), table_ref[BITS, p]
            for e in range(tiles):
                table_ref[ROW_AT + k, p * tiles + e] = at
                at = at + jnp.where(tile_on(bits, (t ^ (2 + k)) * tiles + e), rows, 0)

    for copy in factor_loads():
        copy.wait()

    def fold(source, carry):
        row = factor_at[source]
        fold_factor(c, tiles_at.at[row], top_at.at[row], factor_out.at[source])
        return carry

    lax.fori_loop(0, n_blk, fold, 0)


def tile_on(bits, tile):
    return ((bits >> tile) & 1) == 1


def pack_rows(table_ref, blocks_ref, packed, staged, sems):
    t = lax.axis_index("tile")
    slots, max_order, width = blocks_ref.shape
    tiles = width // CTW

    def loads():
        for p in range(slots // 2):
            yield pltpu.make_async_copy(blocks_ref.at[table_ref[OTHERS, p]], staged.at[p], sems.at[p])

    for copy in loads():
        copy.start()
    at = jnp.int32(0)
    for p, copy in enumerate(loads()):
        copy.wait()
        for e in range(tiles):
            on = tile_on(table_ref[BITS_OTHERS, p], t * tiles + e)

            def write(k, carry, at=at, p=p, e=e):
                packed[pl.ds(pl.multiple_of(at + k * CHUNK, 8), CHUNK), :] = staged[
                    p, pl.ds(pl.multiple_of(k * CHUNK, CHUNK), CHUNK), e * CTW : (e + 1) * CTW
                ]
                return carry

            chunks = (table_ref[ORDER_OTHERS, p] + CHUNK - 1) // CHUNK
            lax.fori_loop(0, jnp.where(on, chunks, 0), write, 0)
            at = at + jnp.where(on, round8(table_ref[ORDER_OTHERS, p]), 0)


def load_columns(table_ref, blocks_ref, core_ref, x_out, sem):
    def loads():
        for p in range(x_out.shape[0]):
            for m, ref in enumerate((blocks_ref, core_ref)):
                yield pltpu.make_async_copy(ref.at[table_ref[MINE, p]], x_out.at[p, m], sem)

    for copy in loads():
        copy.start()
    for copy in loads():
        copy.wait()


def split(x):
    high = x.astype(BF16)
    return high, (x - high.astype(F32)).astype(BF16)


def dot3(a, b):
    def dot(p, q):
        return jnp.dot(p, q, preferred_element_type=F32)

    return dot(a[0], b[0]) + (dot(a[0], b[1]) + dot(a[1], b[0]))


def whiten(tiles, table_ref, p, upper, lower, tile_ids):
    order = table_ref[ORDER, p]
    row_on = lax.broadcasted_iota(jnp.int32, tiles[0].shape, 0) < order
    parts = [
        jnp.where(row_on & tile_on(table_ref[BITS, p], ct), tile, 0.0) for tile, ct in zip(tiles, tile_ids)
    ]
    x = split(jnp.concatenate(parts, axis=1))
    w = jnp.concatenate([dot3(upper, (x[0][:256], x[1][:256])), dot3(lower, x)], axis=0)
    return jnp.where(lax.broadcasted_iota(jnp.int32, w.shape, 0) < order, w, 0.0)


def gram_own(
    table_ref, x_ref, factor_ref, factor_other,
    upper_high, upper_low, lower_high, lower_low, w0_high, w0_low, w1t_high, w1t_low, g_out, w0t_high, w0t_low,
):
    t = lax.axis_index("tile")
    c = t % 2
    half, _, max_order, width = x_ref.shape
    for p in range(half):
        here, there = factor_ref[table_ref[OWNER, p]], factor_other[table_ref[OWNER, p]]
        upper, lower = unfold_factor(jnp.where(c == 0, here, there), jnp.where(c == 0, there, here))
        upper, lower = split(upper), split(lower)
        upper_high[p], upper_low[p] = upper
        lower_high[p], lower_low[p] = lower
        tiles = [x_ref[p, m, :, e * CTW : (e + 1) * CTW] for m in range(2) for e in range(2)]
        tile_ids = [(t ^ m) * 2 + e for m in range(2) for e in range(2)]
        w = whiten(tiles, table_ref, p, upper, lower, tile_ids)
        rows = pl.ds(p * max_order, max_order)
        w0_high[rows, :], w0_low[rows, :] = split(w[:, :width])
        w0t_high[:, rows], w0t_low[:, rows] = split(w[:, :width].T)
        w1t_high[:, rows], w1t_low[:, rows] = split(w[:, width:].T)
    w0 = w0_high[...], w0_low[...]
    g_out[:width] = dot3((w0t_high[...], w0t_low[...]), w0)
    g_out[width:] = dot3((w1t_high[...], w1t_low[...]), w0)


def across(table_ref, rows_ref, group, p, upper_high, upper_low, lower_high, lower_low, max_order):
    t = lax.axis_index("tile")
    last = rows_ref.shape[0] - CHUNK
    tiles = []
    for e in range(2):
        at = table_ref[ROW_AT + group - 2, p * 2 + e]
        starts = [jnp.minimum(at + k, last) for k in range(0, max_order, CHUNK)]
        tiles.append(jnp.concatenate([rows_ref[pl.ds(pl.multiple_of(k, 8), CHUNK), :] for k in starts], axis=0))
    upper, lower = (upper_high[p], upper_low[p]), (lower_high[p], lower_low[p])
    return whiten(tiles, table_ref, p, upper, lower, [(t ^ group) * 2 + e for e in range(2)])


def gram_y(
    table_ref, y_ref, upper_high, upper_low, lower_high, lower_low, w0_high, w0_low, w1t_high, w1t_low,
    w2_high, w2_low, g_out, w2t_high, w2t_low,
):
    depth, width = w0_high.shape
    half = upper_high.shape[0]
    max_order = depth // half
    for p in range(half):
        w = across(table_ref, y_ref, 2, p, upper_high, upper_low, lower_high, lower_low, max_order)
        rows = pl.ds(p * max_order, max_order)
        w2_high[rows, :], w2_low[rows, :] = split(w)
        w2t_high[:, rows], w2t_low[:, rows] = split(w.T)
    w2, w2t = (w2_high[...], w2_low[...]), (w2t_high[...], w2t_low[...])
    g_out[:width] = dot3(w2t, (w0_high[...], w0_low[...]))
    g_out[width : 2 * width] = dot3((w1t_high[...], w1t_low[...]), w2)
    g_out[2 * width :] = dot3(w2t, w2)


def gram_rest(
    table_ref, yc_ref, upper_high, upper_low, lower_high, lower_low, w0_high, w0_low, w2_high, w2_low, g_own, g_y, *refs
):
    firsts, seconds = refs[:4], refs[4:8]
    w3t_high, w3t_low, gram = refs[8:]
    s = lax.axis_index("blk")
    t = lax.axis_index("tile")
    depth, width = w0_high.shape
    half = upper_high.shape[0]
    max_order = depth // half
    for p in range(half):
        w = across(table_ref, yc_ref, 3, p, upper_high, upper_low, lower_high, lower_low, max_order)
        rows = pl.ds(p * max_order, max_order)
        w3t_high[:, rows], w3t_low[:, rows] = split(w.T)
    w3t = w3t_high[...], w3t_low[...]
    for m in range(2):
        gram[0, m] = g_own[m * width : (m + 1) * width]
    gram[0, 2] = g_y[:width]
    gram[0, 3] = dot3(w3t, (w0_high[...], w0_low[...]))
    gram[1, 0] = g_y[:width].T
    for m in range(1, 3):
        gram[1, m] = g_y[m * width : (m + 1) * width]
    gram[1, 3] = dot3(w3t, (w2_high[...], w2_low[...]))

    z, x = s // 2, s % 2

    for n in range(4):
        for a in range(2):
            for b in range(2):
                m, at = (z ^ n) ^ t, (x ^ a) * 128
                firsts[2 * a + b][n] = gram[b, m, pl.ds(pl.multiple_of(at, 8), XY_FIRST), :]
                seconds[n][a, b] = gram[b, m, pl.ds(pl.multiple_of(at + XY_FIRST, 8), 128 - XY_FIRST), :]


def paired_body(blocks, orders, pattern, dest, inv_factor):
    slots, max_order, width = blocks.shape
    n_blk = lax.axis_size("blk")
    half = slots // 2
    tiles = width // CTW
    blocks = pltpu.with_memory_space_constraint(blocks, pltpu.HBM)
    inv_factor = pltpu.with_memory_space_constraint(inv_factor, pltpu.HBM)
    dest, orders, pattern = (pltpu.with_memory_space_constraint(v, pltpu.HBM) for v in (dest, orders, pattern.T))
    hbm = pl.BlockSpec(memory_space=pltpu.HBM)
    smem = pl.BlockSpec(memory_space=pltpu.SMEM)
    vmem = pl.BlockSpec(memory_space=pltpu.VMEM)
    shape = jax.ShapeDtypeStruct
    factor_send, table, level = pl.pallas_call(
        plan,
        out_shape=(
            shape((n_blk, FACTOR_ROWS, CTW), F32),
            shape((9, half * tiles), jnp.int32),
            shape((1,), jnp.int32),
        ),
        in_specs=[hbm] * 4,
        out_specs=(vmem, smem, smem),
        scratch_shapes=[
            pltpu.SMEM(dest.shape, jnp.int32),
            pltpu.SMEM(orders.shape, jnp.int32),
            pltpu.VMEM(orders.shape, jnp.int32),
            pltpu.VMEM(pattern.shape, jnp.int32),
            pltpu.VMEM((3, dest.shape[0]), jnp.int32),
            pltpu.SMEM((3, dest.shape[0]), jnp.int32),
            pltpu.SMEM((n_blk, 2, n_blk), jnp.int32),
            pltpu.SMEM((n_blk, n_blk), jnp.int32),
            pltpu.SMEM((n_blk, 3), jnp.int32),
            pltpu.SMEM((n_blk + 1,), jnp.int32),
            pltpu.VMEM((slots, 3, 128, 128), F32),
            pltpu.VMEM((slots, TOP_ROWS, 128), F32),
            pltpu.SemaphoreType.DMA,
            pltpu.SemaphoreType.DMA,
        ],
        compiler_params=pltpu.CompilerParams(vmem_limit_bytes=VMEM_LIMIT),
        name="plan",
    )(dest, orders, pattern, inv_factor)
    rest = [functools.partial(paired_rest, rows) for rows in row_counts(half * tiles * max_order)]
    return lax.switch(level[0], rest, table, blocks, factor_send)


def paired_rest(row_count, table, blocks, factor_send):
    slots, max_order, width = blocks.shape
    n_blk = lax.axis_size("blk")
    n_tile = lax.axis_size("tile")
    half = slots // 2
    tiles = width // CTW
    axes = ("blk", "tile")

    def exchange(value, blk_bits, tile_bits):
        perm = [
            (b * n_tile + t, (b ^ blk_bits) * n_tile + (t ^ tile_bits)) for b in range(n_blk) for t in range(n_tile)
        ]
        return lax.ppermute(value, axes, perm)

    hbm = pl.BlockSpec(memory_space=pltpu.HBM)
    smem = pl.BlockSpec(memory_space=pltpu.SMEM)
    vmem = pl.BlockSpec(memory_space=pltpu.VMEM)
    shape = jax.ShapeDtypeStruct
    params = pltpu.CompilerParams(vmem_limit_bytes=VMEM_LIMIT)
    dma = pltpu.SemaphoreType.DMA

    y_rows = pl.pallas_call(
        pack_rows,
        out_shape=shape((row_count, CTW), F32),
        in_specs=[smem, hbm],
        out_specs=vmem,
        scratch_shapes=[pltpu.VMEM((half, max_order, width), F32), dma((half,))],
        compiler_params=params,
        name="pack_rows",
    )(table, blocks)
    y_recv = exchange(y_rows, 0, 2)
    factors = lax.all_to_all(factor_send, "blk", split_axis=0, concat_axis=0, tiled=True)
    core_blocks = exchange(blocks, 0, 1)
    factors_other = exchange(factors, 0, 1)
    own_table, _ = lax.optimization_barrier((table, factors))
    columns = pl.pallas_call(
        load_columns,
        out_shape=shape((half, 2, max_order, width), F32),
        in_specs=[smem, hbm, hbm],
        out_specs=vmem,
        scratch_shapes=[dma],
        compiler_params=params,
        name="load_columns",
    )(own_table, blocks, core_blocks)

    depth = half * max_order
    *factor, w0_high, w0_low, w1t_high, w1t_low, g_own = pl.pallas_call(
        gram_own,
        out_shape=(
            shape((half, 256, 256), BF16),
            shape((half, 256, 256), BF16),
            shape((half, 128, 384), BF16),
            shape((half, 128, 384), BF16),
            shape((depth, width), BF16),
            shape((depth, width), BF16),
            shape((width, depth), BF16),
            shape((width, depth), BF16),
            shape((2 * width, width), F32),
        ),
        in_specs=[smem] + [vmem] * 3,
        out_specs=(vmem,) * 9,
        scratch_shapes=[pltpu.VMEM((width, depth), BF16), pltpu.VMEM((width, depth), BF16)],
        compiler_params=params,
        name="gram_own",
    )(table, columns, factors, factors_other)

    y_recv, g_own = lax.optimization_barrier((y_recv, g_own))
    yc_recv = exchange(y_recv, 0, 1)
    w2_high, w2_low, g_y = pl.pallas_call(
        gram_y,
        out_shape=(shape((depth, width), BF16), shape((depth, width), BF16), shape((3 * width, width), F32)),
        in_specs=[smem] + [vmem] * 9,
        out_specs=(vmem,) * 3,
        scratch_shapes=[pltpu.VMEM((width, depth), BF16), pltpu.VMEM((width, depth), BF16)],
        compiler_params=params,
        name="gram_y",
    )(table, y_recv, *factor, w0_high, w0_low, w1t_high, w1t_low)
    first_shape, second_shape = (4, XY_FIRST, width), (2, 2, 128 - XY_FIRST, width)
    pieces = pl.pallas_call(
        gram_rest,
        out_shape=(shape(first_shape, F32),) * 4 + (shape(second_shape, F32),) * 4,
        in_specs=[smem] + [vmem] * 11,
        out_specs=(vmem,) * 8,
        scratch_shapes=[
            pltpu.VMEM((width, depth), BF16),
            pltpu.VMEM((width, depth), BF16),
            pltpu.VMEM((2, 4, width, width), F32),
        ],
        compiler_params=params,
        name="gram_rest",
    )(table, yc_recv, *factor, w0_high, w0_low, w2_high, w2_low, g_own, g_y)
    firsts, seconds = pieces[:4], pieces[4:]

    plane = [(a, b) for a in range(2) for b in range(2) if a or b]
    plane_in = [exchange(firsts[2 * a + b], a, 2 * b) for a, b in plane]
    line_in = [exchange(seconds[n], 2 * n, 0) for n in range(1, 4)]
    first = firsts[0] + sum(plane_in)
    second = seconds[0] + sum(line_in)
    line_in = [exchange(first[n], 2 * n, 0) for n in range(1, 4)]
    plane_in = [exchange(second[a, b], a, 2 * b) for a, b in plane]
    gram_tile = jnp.concatenate([first[0] + sum(line_in), second[0, 0] + sum(plane_in)], axis=0)
    return gram_tile * (1.0 / (n_blk * slots * max_order**0.5))


def solution(mesh):
    in_specs = (P("blk", None, "tile"), P(), P(), P(), P("blk", None, None))
    out_specs = P("blk", "tile")
    paired = mesh.shape["blk"] == 8 and mesh.shape["tile"] == 4
    body = paired_body if paired else general_body
    return jax.shard_map(body, mesh=mesh, in_specs=in_specs, out_specs=out_specs, check_vma=False)
```
